32 devices in a mesh: dp: 8 (over y, x, core), tensor: 4 (over z).
Axes of the slice: x: 2, y: 2, z: 4, core: 2. Of those that a mesh axis runs over, the one named last changes fastest.
Arguments:
- tokens: bfloat16 [8192, 768], P(('dp', 'tensor')), may hold values from -6 to 6
- long_count: int32 [8], P('dp'), may hold values from 0 to 1
- timesteps: int32 [32], P('dp'), may hold values from 0 to 999
- norm_gain: float32 [768], replicated, may hold values from 0.1 to 1.9
- norm_bias: float32 [768], replicated, may hold values from -3 to 3
- w_qkv: bfloat16 [3, 768, 768], P(None, None, 'tensor'), may hold values from -0.21875 to 0.21875
- b_qkv: float32 [3, 768], P(None, 'tensor'), may hold values from -3 to 3
- w_out: bfloat16 [768, 768], P('tensor'), may hold values from -3 to 3
- b_out: float32 [768], replicated, may hold values from -3 to 3
- w_time: float32 [128, 2304], replicated, may hold values from -0.5 to 0.5
- b_time: float32 [2304], replicated, may hold values from -3 to 3
- w_up: bfloat16 [768, 3072], P(None, 'tensor'), may hold values from -0.21875 to 0.21875
- b_up: float32 [3072], P('tensor'), may hold values from -3 to 3
- w_down: bfloat16 [3072, 768], P('tensor'), may hold values from -0.109375 to 0.109375
- b_down: float32 [768], replicated, may hold values from -3 to 3
- cotangent: bfloat16 [8192, 768], P(('dp', 'tensor')), may hold values from -6 to 6
Outputs:
- result: bfloat16 [8192, 768], P(('dp', 'tensor'))
- grad_tokens: float32 [8192, 768], P(('dp', 'tensor'))
- grad_norm_gain: float32 [768], replicated
- grad_norm_bias: float32 [768], replicated
- grad_w_qkv: float32 [3, 768, 768], P(None, None, 'tensor')
- grad_b_qkv: float32 [3, 768], P(None, 'tensor')
- grad_w_out: float32 [768, 768], P('tensor')
- grad_b_out: float32 [768], replicated
- grad_w_time: float32 [128, 2304], replicated
- grad_b_time: float32 [2304], replicated
- grad_w_up: float32 [768, 3072], P(None, 'tensor')
- grad_b_up: float32 [3072], P('tensor')
- grad_w_down: float32 [3072, 768], P('tensor')
- grad_b_down: float32 [768], replicated
The draws below stay inside these ranges and needn't reach their ends.
Inputs may be any that keep to these rules, and one draw needn't show every extreme that they name: `long_count`: sequences of 1024 tokens on one index of dp; the rest of its 1024 rows hold sequences of 256 tokens. `timesteps`: entry i * 4 + s belongs to slot s of index i of dp; slots past that index's sequences are unused.
All inputs are finite; a program needn't handle non-finite values.
Results may differ from the reference program's by a relative error of at most 0.017.
Values may be sent and summed in bfloat16 or wider, within the bound.
A program may use at most 128 MiB of HBM per device.

```python
import math
import jax
import jax.numpy as jnp
from jax import lax

D = 768
HEADS = 12
HEAD = 64
FF = 3072
TE = 128
STEPS = 1000
LONG = 1024
SHORT = 256
WINDOWS = 1
SLOTS = 4
TOKENS = 8192
N_DP = 8
N_TENSOR = 4


def plant(values, own_key, low, largest):
    shape = values.shape
    spot = [jax.random.randint(jax.random.fold_in(own_key, axis), (), 0, shape[axis]) for axis in range(len(shape))]
    values = values.at[tuple(spot)].set(low)
    longest = shape.index(max(shape))
    spot[longest] = (spot[longest] + 1) % shape[longest]
    return values.at[tuple(spot)].set(largest)


def levels(key, extent, split, smallest, high):
    loudness = 1.0
    for position, parts in split:
        draws = jax.random.uniform(jax.random.fold_in(jax.random.fold_in(key, 6), position), (parts,), jnp.float32, smallest / len(split), high / len(split))
        loudness = loudness * jnp.repeat(jnp.exp(draws), extent[position] // parts).reshape((-1,) + (1,) * (len(extent) - 1 - position))
    return loudness


def centred(key, dims, deviation, limit, shards=(), kind=jnp.bfloat16):
    level = levels(key, dims, shards, -0.22, 0.18) if shards else 1.0
    entries = jax.random.normal(key, dims, jnp.float32) * deviation * level
    return jnp.minimum(jnp.maximum(entries, -limit), limit).astype(kind)


def setup_inputs(seed: int = 0) -> dict:
    splits = jax.random.split(jax.random.key(seed), 17)
    return {
        "tokens": centred(splits[0], (TOKENS, D), 1.0, 6.0, ((0, 32),)),
        "long_count": plant(jax.random.randint(splits[1], (N_DP,), 0, WINDOWS + 1), jax.random.fold_in(splits[1], 1), 0, WINDOWS).astype(jnp.int32),
        "timesteps": plant(jax.random.randint(splits[2], (N_DP * SLOTS,), 0, STEPS), jax.random.fold_in(splits[2], 1), 0, STEPS - 1).astype(jnp.int32),
        "norm_gain": jnp.clip(1.0 + 0.18 * jax.random.normal(splits[3], (D,), jnp.float32), 0.1, 1.9),
        "norm_bias": centred(splits[4], (D,), 0.5, 3.0, (), jnp.float32),
        "w_qkv": centred(splits[5], (3, D, HEADS * HEAD), D ** -0.5, 0.21875, ((2, 4),)),
        "b_qkv": centred(splits[6], (3, HEADS * HEAD), 0.5, 3.0, ((1, 4),), jnp.float32),
        "w_out": centred(splits[7], (HEADS * HEAD, D), 4 ** -0.5, 3.0, ((0, 4),)),
        "b_out": centred(splits[8], (D,), 0.5, 3.0, (), jnp.float32),
        "w_time": centred(splits[9], (TE, 3 * D), TE ** -0.5, 0.5, (), jnp.float32),
        "b_time": centred(splits[10], (3 * D,), 0.5, 3.0, (), jnp.float32),
        "w_up": centred(splits[11], (D, FF), D ** -0.5, 0.21875, ((1, 4),)),
        "b_up": centred(splits[12], (FF,), 0.5, 3.0, ((0, 4),), jnp.float32),
        "w_down": centred(splits[13], (FF, D), FF ** -0.5, 0.109375, ((0, 4),)),
        "b_down": centred(splits[14], (D,), 0.5, 3.0, (), jnp.float32),
        "cotangent": centred(splits[15], (TOKENS, D), 1.0, 6.0, ((0, 32),)),
    }


@jax.custom_vjp
def low(v):
    return lax.optimization_barrier(v.astype(jnp.bfloat16)).astype(jnp.float32)

@jax.custom_vjp
def low_back(v):
    return v

def low_keep(v):
    return (low(v), None)

def low_pass(kept, grad):
    return (grad,)

def back_keep(v):
    return (v, None)

def back_low(kept, grad):
    return (low(grad),)
low.defvjp(low_keep, low_pass)
low_back.defvjp(back_keep, back_low)
epsilon = 1e-05
time_scale = 64.0

def normalize(values):
    center = values - lax.optimization_barrier(jnp.mean(values, axis=-1, keepdims=True))
    spread = lax.optimization_barrier(jnp.mean(center * center, axis=-1, keepdims=True))
    return center * lax.rsqrt(spread + epsilon)

def layout(row_ids, long_seqs):
    ratio = LONG // SHORT
    tiles = row_ids // SHORT
    in_long = tiles < ratio * long_seqs
    slot_ids = jnp.where(in_long, tiles // ratio, long_seqs + tiles - ratio * long_seqs)
    places = jnp.where(in_long, row_ids % LONG, row_ids % SHORT)
    return (slot_ids, places)

def rotate(values, places):
    half_dim = HEAD // 2
    freqs = jnp.exp(-math.log(10000.0) * jnp.arange(half_dim, dtype=jnp.float32) / half_dim)
    angles = places.astype(jnp.float32)[:, None, None] * freqs
    cosine = jnp.cos(angles)
    sine = jnp.sin(angles)
    shaped = values.reshape(values.shape[0], -1, HEAD)
    first = shaped[..., :half_dim]
    second = shaped[..., half_dim:]
    turned = jnp.concatenate([first * cosine - second * sine, second * cosine + first * sine], axis=-1)
    return turned.reshape(values.shape)

def time_features(step_ids):
    half_dim = TE // 2
    freqs = jnp.exp(-math.log(10000.0) * jnp.arange(half_dim, dtype=jnp.float32) / half_dim)
    angles = (step_ids.astype(jnp.float32) / STEPS * time_scale)[:, None] * freqs[None, :]
    return jnp.concatenate([jnp.cos(angles), jnp.sin(angles)], axis=-1)

def heads_view(values):
    return values.reshape(values.shape[0], -1, HEAD)

def window_attend(window_item):
    queries, key_rows, values, slot_ids = window_item
    highest = lax.Precision.HIGHEST
    scale = 1.0 / math.sqrt(HEAD)
    scores = low_back(jnp.einsum('qhd,khd->hqk', heads_view(queries), heads_view(key_rows), precision=highest) * scale)
    same = (slot_ids[:, None] == slot_ids[None, :])[None]
    probs = low(jax.nn.softmax(jnp.where(same, scores, -1e+30), axis=-1))
    output = jnp.einsum('hqk,khd->qhd', probs, heads_view(values), precision=highest)
    return output.reshape(queries.shape)

def grouped_sum(left, right):
    highest = lax.Precision.HIGHEST
    span = left.shape[1] // N_TENSOR
    total = jnp.zeros((left.shape[0], right.shape[1]), jnp.float32)
    for group in range(N_TENSOR):
        part_sum = jnp.dot(left[:, group * span:(group + 1) * span], right[group * span:(group + 1) * span], precision=highest)
        total = total + low(part_sum)
    return total

def one_group(params, inputs, long_seqs, step_ids):
    norm_gain, norm_bias, w_qkv, b_qkv, w_out, b_out, w_time, b_time, w_up, b_up, w_down, b_down = params
    highest = lax.Precision.HIGHEST
    row_total = inputs.shape[0]
    windows = row_total // LONG
    width = inputs.shape[1]
    slot_ids, places = layout(jnp.arange(row_total, dtype=jnp.int32), long_seqs)
    normed = low(normalize(inputs) * norm_gain + norm_bias)
    head_span = w_qkv.shape[2] // N_TENSOR
    project_parts = [jnp.einsum('rd,cdh->crh', low_back(normed), w_qkv[:, :, group * head_span:(group + 1) * head_span], precision=highest) for group in range(N_TENSOR)]
    project = low_back(jnp.concatenate(project_parts, axis=2) + b_qkv[:, None, :])
    queries = low(rotate(project[0], places))
    key_rows = low(rotate(project[1], places))
    values = low(project[2])

    def split_windows(array):
        return array.reshape((windows, LONG) + array.shape[1:])
    outputs = lax.map(jax.checkpoint(window_attend), (split_windows(queries), split_windows(key_rows), split_windows(values), split_windows(slot_ids)))
    mixed = low_back(low(outputs.reshape(row_total, -1)))
    attended = low_back(grouped_sum(mixed, w_out) + b_out)
    resid = inputs + attended
    features = time_features(step_ids)
    modulation = jnp.dot(features, w_time, precision=highest) + b_time
    onehot = (slot_ids[:, None] == jnp.arange(step_ids.shape[0], dtype=jnp.int32)[None, :]).astype(jnp.float32)
    row_mod = jnp.dot(onehot, modulation, precision=highest)
    scale_rows = row_mod[:, :width]
    shift_rows = row_mod[:, width:2 * width]
    gate_rows = row_mod[:, 2 * width:]
    modulated = low(normalize(resid) * (1.0 + scale_rows) + shift_rows)
    unit_span = w_up.shape[1] // N_TENSOR
    hidden_parts = [jnp.dot(low_back(modulated), w_up[:, group * unit_span:(group + 1) * unit_span], precision=highest) for group in range(N_TENSOR)]
    hidden = low_back(jnp.concatenate(hidden_parts, axis=1) + b_up)
    active = low(jax.nn.gelu(hidden))
    branch = low_back(grouped_sum(active, w_down) + b_down)
    return resid + gate_rows * branch

def reference(tokens, long_count, timesteps, norm_gain, norm_bias, w_qkv, b_qkv, w_out, b_out, w_time, b_time, w_up, b_up, w_down, b_down, cotangent):
    params = tuple((item.astype(jnp.float32) for item in (norm_gain, norm_bias, w_qkv, b_qkv, w_out, b_out, w_time, b_time, w_up, b_up, w_down, b_down)))

    def forward(params, flat):

        def advance(carry, item):
            return (carry, jax.checkpoint(one_group)(params, item[0], item[1], item[2]))
        rows_each = flat.shape[0] // N_DP
        _, outputs = lax.scan(advance, jnp.zeros((), jnp.float32), (flat.reshape(N_DP, rows_each, -1), long_count, timesteps.reshape(N_DP, -1)))
        return outputs.reshape(flat.shape)
    result, pull = jax.vjp(forward, params, tokens.astype(jnp.float32))
    grads, grad_inputs = pull(cotangent.astype(jnp.float32))
    return (result.astype(jnp.bfloat16), grad_inputs, grads[0], grads[1], grads[2], grads[3], grads[4], grads[5], grads[6], grads[7], grads[8], grads[9], grads[10], grads[11])
```

```python
import functools
import math

import jax
import jax.numpy as jnp
from jax import lax
from jax.experimental import pallas as pl
from jax.experimental.pallas import tpu as pltpu
from jax.sharding import PartitionSpec as P

HEAD = 64
TE = 128
STEPS = 1000
LONG = 1024
SHORT = 256
D = 768
HALF = 384
EPS = 1e-05
TIME_SCALE = 64.0
SCALE = 1.0 / math.sqrt(HEAD)
BF = jnp.bfloat16
F32 = jnp.float32
MESH = pl.DeviceIdType.MESH

SEMS = {
    "load": 3,
    "ag_s": 8,
    "ag_r": 4,
    "bup_s": 4,
    "bup_r": 4,
    "wz_s": 24,
    "wz_r": 12,
    "wx_s": 36,
    "wx_r": 36,
    "wc_s": 4,
    "wc_r": 4,
    "mix_s": 4,
    "mix_r": 4,
    "pair_s": 4,
    "pair_r": 4,
    "gm_s": 4,
    "gm_r": 4,
    "r1_s": 2,
    "r1_r": 2,
    "r2_s": 12,
    "r2_r": 12,
    "r3_s": 12,
    "r3_r": 12,
    "r4_s": 12,
    "r4_r": 12,
    "r5_s": 4,
    "r5_r": 4,
    "rs_s": 6,
    "rs_r": 6,
    "sz_s": 4,
    "sz_r": 4,
    "sd_s": 8,
    "sd_r": 8,
}
BASE = {}
COUNT = 0
for _name, _number in SEMS.items():
    BASE[_name] = COUNT
    COUNT += _number

SCRATCH = {
    "normed": ((4, 256, D), BF),
    "q": ((3, 1024, 128), BF),
    "k": ((3, 1024, 128), BF),
    "v": ((3, 1024, 128), BF),
    "kt": ((3, 4, 128, 256), BF),
    "vt": ((3, 4, 128, 256), BF),
    "probs": ((3, 4, 1024, 256), BF),
    "blocks": ((4, 256, 192), BF),
    "mixed": ((4, 256, 192), BF),
    "wo": ((4, 192, D), BF),
    "wu": ((D, 4 * HALF), BF),
    "wd": ((4, 4, 96, D), BF),
    "bup": ((4, 1, D), F32),
    "bupc": ((1, 4 * HALF), F32),
    "mod2": ((2, 256, D), BF),
    "gb2": ((2, 256, D), BF),
    "act": ((2, 256, 4 * HALF), BF),
    "wide": ((12, 512, 128), F32),
    "gh": ((2, 256, 4 * HALF), BF),
    "part_out": ((2, 256, D), BF),
    "part_in": ((2, 256, D), BF),
    "gwo": ((2, 4, 4, 48, HALF), BF),
    "gwu": ((D, 4 * HALF), BF),
    "gwd": ((4, 4, 96, D), BF),
    "gres": ((256, D), F32),
    "gm": ((4, 256, 192), BF),
    "gp": ((4, 256, 576), BF),
    "gqkv": ((2, 4, 96, 576), BF),
    "r1o": ((4, 4, 48, HALF), BF),
    "r1q": ((4, 96, 576), BF),
    "r2d": ((3, 4, 96, D), BF),
    "r2u": ((3, 192, 4 * HALF), BF),
    "r2o": ((3, 4, 48, HALF), BF),
    "r2q": ((3, 96, 576), BF),
    "r3d": ((4, 96, D), BF),
    "r3u": ((4, 192, HALF), BF),
    "r3o": ((4, 48, HALF), BF),
    "rs_out": ((3, 256, D), BF),
    "rs_in": ((2, 3, 256, D), BF),
    "small": ((16, D), F32),
    "zs": ((4, 16, D), F32),
}
INPUTS = [
    "neg",
    "tok",
    "cot",
    "gain",
    "bias",
    "b_out",
    "b_down",
    "mod",
    "feat",
    "b_flat",
    "w_flat",
    "cos",
    "sin",
    "wo_own",
    "wu_own",
    "wd_own",
    "bup_own",
]
OUTPUTS = ["result", "gtok", "oqkv", "oo", "ou", "od", "ds"]


def dot(a, b):
    return jnp.dot(a, b, preferred_element_type=F32)


def dot_nt(a, b):
    return lax.dot_general(a, b, (((1,), (1,)), ((), ())), preferred_element_type=F32)


def dot_tn(a, b):
    return lax.dot_general(a, b, (((0,), (0,)), ((), ())), preferred_element_type=F32)


def norm_parts(values):
    center = values - jnp.mean(values, axis=-1, keepdims=True)
    rstd = lax.rsqrt(jnp.mean(center * center, axis=-1, keepdims=True) + EPS)
    return center * rstd, rstd


def norm_back(unit, rstd, grad):
    mean_g = jnp.mean(grad, axis=-1, keepdims=True)
    mean_gn = jnp.mean(grad * unit, axis=-1, keepdims=True)
    return (grad - mean_g - unit * mean_gn) * rstd


def body(*refs):
    names = INPUTS + OUTPUTS + list(SCRATCH) + ["sem"]
    r = dict(zip(names, refs, strict=True))
    sem = r["sem"]
    dp = lax.axis_index("dp")
    t = lax.axis_index("tensor")
    block = dp - lax.rem(dp, 8)
    c = lax.rem(dp, 2)
    q = lax.div(lax.rem(dp, 8), 2)
    other = 1 - c
    sibling = (dp + 1 - 2 * c, t)
    qx = q + 1 - 2 * lax.rem(q, 2)
    qy = q + 2 - 4 * lax.div(q, 2)
    columns = [q, qx, qy, 3 - q]

    def column(j):
        return (block + 2 * columns[j] + c, t)

    def sid(name, index=0):
        return BASE[name] + index

    def remote(src, dst, send, recv, device):
        return pltpu.make_async_remote_copy(
            src_ref=src,
            dst_ref=dst,
            send_sem=sem.at[send],
            recv_sem=sem.at[recv],
            device_id=device,
            device_id_type=MESH,
        )

    def got(ref, recv):
        remote(ref, ref, recv, recv, sibling).wait_recv()

    def sent(ref, send):
        remote(ref, ref, send, send, sibling).wait_send()

    def rows(index, size):
        return pl.ds(pl.multiple_of(index * size, size), size)

    barrier = pltpu.get_barrier_semaphore()

    def zpeer(j):
        return lax.rem(t + j, 4)

    for j in range(1, 4):
        pl.semaphore_signal(barrier, inc=1, device_id=(dp, zpeer(j)), device_id_type=MESH)
    for j in range(1, 8):
        peer = block + lax.rem(dp - block + j, 8)
        pl.semaphore_signal(barrier, inc=1, device_id=(peer, t), device_id_type=MESH)

    loads = [
        pltpu.make_async_copy(r["wo_own"], r["wo"].at[t], sem.at[sid("load", 0)]),
        pltpu.make_async_copy(
            r["wu_own"].at[:, rows(c, HALF)], r["wu"].at[:, rows(t, HALF)], sem.at[sid("load", 1)]
        ),
        pltpu.make_async_copy(r["wd_own"].at[c], r["wd"].at[t], sem.at[sid("load", 2)]),
    ]
    for load in loads:
        load.start()

    def wpiece(a, shard, col):
        if a == 0:
            return r["wo"].at[shard, rows(col, 48), rows(c, HALF)]
        if a == 1:
            return r["wu"].at[rows(col, 192), rows(shard, HALF)]
        return r["wd"].at[shard, col]

    inputs = r["tok"][...].astype(F32)
    unit, _ = norm_parts(inputs)
    r["normed"][t] = (unit * r["gain"][...] + r["bias"][...]).astype(BF)
    r["bup"][t] = r["bup_own"][...]
    gate = r["mod"][:, 2 * D :]
    r["gb2"][c] = (gate * r["cot"][...].astype(F32)).astype(BF)
    for load in loads:
        load.wait()
    pl.semaphore_wait(barrier, 10)

    def ag_copy(b, side, k, device):
        return remote(
            r["normed"].at[b], r["normed"].at[b], sid("ag_s", side * 4 + k), sid("ag_r", b), (dp, device)
        )

    @pl.when(t < 3)
    def _():
        ag_copy(t, 0, 0, t + 1).start()

    @pl.when(t > 0)
    def _():
        ag_copy(t, 1, 0, t - 1).start()

    for j in range(1, 4):
        remote(
            r["bup"].at[t], r["bup"].at[t], sid("bup_s", j), sid("bup_r", t), (dp, zpeer(j))
        ).start()
    remote(r["gb2"].at[c], r["gb2"].at[c], sid("pair_s", 0), sid("pair_r", 0), sibling).start()

    def hop(i):
        k = lax.div(i + 1, 2)
        side = 1 - lax.rem(i, 2)
        step = 2 * side - 1
        b = t + step * k
        return k, side, b, t - step

    lower = lax.broadcasted_iota(jnp.int32, (256, 128), 1) < HEAD

    def project(b):
        y = dot(r["normed"][b], r["w_flat"][...]) + r["b_flat"][...]
        at = rows(b, 256)
        cosine = r["cos"][at, :]
        sine = r["sin"][at, :]
        doubled = []
        for n in range(3):
            tile = y[:, 128 * n : 128 * (n + 1)]
            swapped = pltpu.roll(tile, HEAD, 1)
            doubled += [jnp.where(lower, tile, swapped), jnp.where(lower, swapped, tile)]
        for h in range(3):
            for part, name in ((doubled[h], "q"), (doubled[3 + h], "k")):
                turned = part * cosine + pltpu.roll(part, 32, 1) * sine
                r[name][h, at, :] = turned.astype(BF)
                if name == "k":
                    r["kt"][h, b] = turned.T.astype(BF)
        tile = y[:, 384:512]
        for h, value in enumerate((jnp.where(lower, tile, 0.0), jnp.where(lower, 0.0, tile))):
            r["v"][h, at, :] = value.astype(BF)
            r["vt"][h, b] = value.T.astype(BF)
        value = y[:, 512:576]
        r["v"][2, at, :HEAD] = value.astype(BF)
        r["vt"][2, b, :HEAD, :] = value.T.astype(BF)

    def ag_step(i, carry):
        k, side, b, nxt = hop(i)

        @pl.when((b >= 0) & (b <= 3))
        def _():
            @pl.when(i > 0)
            def _():
                got(r["normed"].at[b], sid("ag_r", b))

                @pl.when((nxt >= 0) & (nxt <= 3))
                def _():
                    ag_copy(b, side, k, nxt).start()

            project(b)

        return carry

    lax.fori_loop(0, 7, ag_step, 0)

    def wz_copy(a, b, side, k, device):
        return remote(
            wpiece(a, b, q),
            wpiece(a, b, q),
            sid("wz_s", a * 8 + side * 4 + k),
            sid("wz_r", a * 4 + b),
            (dp, device),
        )

    def wx_copy(a, b, j):
        return remote(
            wpiece(a, b, q),
            wpiece(a, b, q),
            sid("wx_s", (a * 4 + b) * 3 + j - 1),
            sid("wx_r", (a * 4 + b) * 3 + j - 1),
            column(j),
        )

    def wz_begin():
        @pl.when(t < 3)
        def _():
            for a in range(3):
                wz_copy(a, t, 0, 0, t + 1).start()

        @pl.when(t > 0)
        def _():
            for a in range(3):
                wz_copy(a, t, 1, 0, t - 1).start()

    def wz_step(i, carry):
        k, side, b, nxt = hop(i)

        @pl.when((b >= 0) & (b <= 3))
        def _():
            for a in range(3):
                got(wpiece(a, b, q), sid("wz_r", a * 4 + b))

                @pl.when((nxt >= 0) & (nxt <= 3))
                def _():
                    wz_copy(a, b, side, k, nxt).start()

                for j in range(1, 4):
                    wx_copy(a, b, j).start()

        return carry

    def ag_sent(i, carry):
        k, side, b, nxt = hop(i)

        @pl.when((i > 0) & (b >= 0) & (b <= 3) & (nxt >= 0) & (nxt <= 3))
        def _():
            sent(r["normed"].at[b], sid("ag_s", side * 4 + k))

        return carry

    @pl.when(t < 3)
    def _():
        sent(r["normed"].at[t], sid("ag_s", 0))

    @pl.when(t > 0)
    def _():
        sent(r["normed"].at[t], sid("ag_s", 4))

    lax.fori_loop(0, 7, ag_sent, 0)
    wz_begin()

    neg = r["neg"][0]

    def attend(qb):
        outs = []
        for h in range(3):
            queries = r["q"][h, rows(qb, 256), :]
            parts = []
            for kb in range(4):
                s = dot_nt(r["k"][h, kb * 256 : (kb + 1) * 256, :], queries) * (0.5 * SCALE)
                parts.append(s + jnp.where(qb == kb, 0.0, neg))
            top = parts[0].max(axis=0, keepdims=True)
            for kb in range(1, 4):
                top = jnp.maximum(top, parts[kb].max(axis=0, keepdims=True))
            parts = [jnp.exp(s - top) for s in parts]
            total = sum(s.sum(axis=0, keepdims=True) for s in parts)
            inverse = 1.0 / total
            out = None
            for kb in range(4):
                p = (parts[kb] * inverse).astype(BF)
                r["probs"][h, qb, kb * 256 : (kb + 1) * 256, :] = p
                term = dot(r["vt"][h, kb] if h < 2 else r["vt"][h, kb, :HEAD, :], p)
                out = term if out is None else out + term
            outs.append(out)
        return (outs[0] + outs[1]).T.astype(BF), outs[2].T.astype(BF)

    for i in range(4):
        qb = lax.rem(t + 1 + i, 4)
        low, high = attend(qb)
        dest = r["blocks"].at[qb] if i < 3 else r["mixed"].at[t]
        dest[:, :128] = low
        dest[:, 128:192] = high
        if i < 3:
            remote(
                r["blocks"].at[qb], r["mixed"].at[t], sid("mix_s", i), sid("mix_r", t), (dp, qb)
            ).start()
        if i == 1:
            lax.fori_loop(1, 3, wz_step, 0)
        if i == 3:
            lax.fori_loop(3, 5, wz_step, 0)

    lax.fori_loop(5, 7, wz_step, 0)

    def wx_wait(arrays):
        def step(i, carry):
            k, side, b, nxt = hop(i)

            @pl.when((b >= 0) & (b <= 3))
            def _():
                for a in arrays:
                    for j in range(1, 4):
                        got(wpiece(a, b, columns[j]), sid("wx_r", (a * 4 + b) * 3 + j - 1))
                if 0 in arrays:
                    half = r["wo"].at[b, :, rows(c, HALF)]
                    remote(half, half, sid("wc_s", b), sid("wc_r", b), sibling).start()

            return carry

        lax.fori_loop(1, 7, step, 0)

    wx_wait((0,))
    for j in range(1, 4):
        got(r["bup"].at[zpeer(j)], sid("bup_r", zpeer(j)))
    for s in range(4):
        r["bupc"][:, HALF * s : HALF * (s + 1)] = r["bup"][s, :, rows(c, HALF)]
    for j in range(1, 4):
        got(r["mixed"].at[zpeer(j)], sid("mix_r", zpeer(j)))
        got(r["wo"].at[zpeer(j), :, rows(other, HALF)], sid("wc_r", zpeer(j)))

    attended = jnp.broadcast_to(r["b_out"][...], (256, D))
    for g in range(4):
        attended = attended + dot(r["mixed"][g], r["wo"][g])
    resid = r["tok"][...].astype(F32) + attended
    unit2, rstd2 = norm_parts(resid)
    scale1 = 1.0 + r["mod"][:, :D]
    r["mod2"][c] = (unit2 * scale1 + r["mod"][:, D : 2 * D]).astype(BF)
    pair_mod = remote(r["mod2"].at[c], r["mod2"].at[c], sid("pair_s", 1), sid("pair_r", 1), sibling)
    pair_mod.start()
    wx_wait((1,))
    got(r["mod2"].at[other], sid("pair_r", 1))

    for ch in range(3):
        lanes = slice(512 * ch, 512 * (ch + 1))
        hidden = dot(r["mod2"][...].reshape(512, D), r["wu"][:, lanes]) + r["bupc"][:, lanes]
        inner = math.sqrt(2.0 / math.pi)
        square = hidden * hidden
        th = jnp.tanh(inner * hidden * (1.0 + 0.044715 * square))
        halfsum = 0.5 * (1.0 + th)
        r["act"][:, :, lanes] = (hidden * halfsum).astype(BF).reshape(2, 256, 512)
        slope = halfsum + 0.5 * hidden * (1.0 - th * th) * (inner * (1.0 + 3 * 0.044715 * square))
        for n in range(4):
            r["wide"][4 * ch + n] = slope[:, 128 * n : 128 * (n + 1)]
    got(r["gb2"].at[other], sid("pair_r", 0))
    wx_wait((2,))
    for ch in range(3):
        lanes = slice(512 * ch, 512 * (ch + 1))
        w_down = r["wd"][...].reshape(4 * HALF, D)[lanes]
        grad_active = dot_nt(r["gb2"][...].reshape(512, D), w_down)
        for n in range(4):
            grad = grad_active[:, 128 * n : 128 * (n + 1)] * r["wide"][4 * ch + n]
            lane = 512 * ch + 128 * n
            r["gh"][:, :, lane : lane + 128] = grad.astype(BF).reshape(2, 256, 128)

    r["part_out"][0] = dot_nt(r["gh"][other], r["wu"][...]).astype(BF)
    remote(
        r["part_out"].at[0], r["part_in"].at[0], sid("pair_s", 2), sid("pair_r", 2), sibling
    ).start()
    w_down = r["wd"][...].reshape(4 * HALF, D)
    r["part_out"][1] = dot(r["act"][other], w_down).astype(BF)
    remote(
        r["part_out"].at[1], r["part_in"].at[1], sid("pair_s", 3), sid("pair_r", 3), sibling
    ).start()
    grad_mod = dot_nt(r["gh"][c], r["wu"][...])
    branch = dot(r["act"][c], w_down) + r["b_down"][...]

    def r2_copy(a, j):
        col = columns[j]
        if a == 0:
            src, dst = r["gwo"].at[c, :, col], r["r2o"].at[j - 1]
        elif a == 1:
            src, dst = r["gwu"].at[rows(col, 192), :], r["r2u"].at[j - 1]
        elif a == 2:
            src, dst = r["gwd"].at[:, col], r["r2d"].at[j - 1]
        else:
            src, dst = r["gqkv"].at[c, col], r["r2q"].at[j - 1]
        return remote(src, dst, sid("r2_s", a * 3 + j - 1), sid("r2_r", a * 3 + j - 1), column(j))

    for s in range(4):
        units = slice(HALF * s, HALF * (s + 1))
        grad = dot_tn(r["act"][:, :, units].reshape(512, HALF), r["gb2"][...].reshape(512, D))
        r["gwd"][s] = grad.astype(BF).reshape(4, 96, D)
    for j in range(1, 4):
        r2_copy(2, j).start()

    got(r["part_in"].at[0], sid("pair_r", 2))
    got(r["part_in"].at[1], sid("pair_r", 3))
    upstream = r["cot"][...].astype(F32)
    branch = branch + r["part_in"][1].astype(F32)
    r["result"][...] = (resid + gate * branch).astype(BF)
    grad_mod = grad_mod + r["part_in"][0].astype(F32)
    grad_resid = upstream + norm_back(unit2, rstd2, grad_mod * scale1)
    r["gres"][...] = grad_resid
    grad_att = grad_resid.astype(BF)

    def total(values):
        return jnp.sum(values, axis=0, keepdims=True)

    r["small"][...] = jnp.zeros((16, D), F32)
    r["small"][0:1, :] = total(grad_mod * unit2)
    r["small"][1:2, :] = total(grad_mod)
    r["small"][2:3, :] = total(upstream * branch)
    r["small"][3:4, :TE] = r["feat"][...]
    r["small"][4:5, :] = total(grad_att.astype(F32))
    r["small"][5:6, :] = total(r["gb2"][c].astype(F32))
    for i in range(3):
        sent(r["blocks"].at[0], sid("mix_s", i))
    for i in range(4):
        g = lax.rem(t + i, 4)
        grad_mixed = dot_nt(grad_att, r["wo"][g]).astype(BF)
        if i == 0:
            r["gm"][t] = grad_mixed
        else:
            r["blocks"][g] = grad_mixed
            remote(
                r["blocks"].at[g], r["gm"].at[t], sid("gm_s", i), sid("gm_r", t), (dp, g)
            ).start()

    for ch in range(3):
        lanes = slice(512 * ch, 512 * (ch + 1))
        grad_hidden = r["gh"][:, :, lanes].reshape(512, 512)
        r["gwu"][:, lanes] = dot_tn(r["mod2"][...].reshape(512, D), grad_hidden).astype(BF)
        units = total(grad_hidden.astype(F32))
        for half in range(2):
            place = 512 * ch + 256 * half
            row, lane = 8 + place // D, place % D
            r["small"][row : row + 1, lane : lane + 256] = units[:, 256 * half : 256 * (half + 1)]
    for j in range(1, 4):
        r2_copy(1, j).start()
    for g in range(4):
        grad = dot_tn(r["mixed"][g], grad_att).astype(BF)
        for half in range(2):
            r["gwo"][half, g] = grad[:, HALF * half : HALF * (half + 1)].reshape(4, 48, HALF)
    remote(r["gwo"].at[other], r["r1o"], sid("r1_s", 1), sid("r1_r", 1), sibling).start()

    def attend_back(qb, first):
        at = rows(qb, 256)
        cosine = r["cos"][at, :]
        sine = r["sin"][at, :]
        for h in range(3):
            if h < 2:
                grad_out = r["gm"][qb, :, :128]
            else:
                grad_out = r["gm"][qb, :, 128:192]
            queries = r["q"][h, at, :]
            probs = []
            grads = []
            inner = None
            for kb in range(4):
                keys = slice(kb * 256, (kb + 1) * 256)
                values = r["v"][h, keys, :] if h < 2 else r["v"][h, keys, :HEAD]
                p = r["probs"][h, qb, keys, :]
                g = dot_nt(values, grad_out)
                term = total(g * p.astype(F32))
                inner = term if inner is None else inner + term
                probs.append(p)
                grads.append(g)
                width = 128 if h < 2 else HEAD
                gv = dot(p, grad_out)
                dv = r["wide"].at[6 + 2 * h + kb // 2, 256 * (kb % 2) : 256 * (kb % 2 + 1), :width]
                dv[...] = gv if first else dv[...] + gv
            grad_q = None
            for kb in range(4):
                keys = slice(kb * 256, (kb + 1) * 256)
                ds = (probs[kb].astype(F32) * (grads[kb] - inner)).astype(BF)
                gk = dot(ds, queries)
                dk = r["wide"].at[2 * h + kb // 2, 256 * (kb % 2) : 256 * (kb % 2 + 1)]
                dk[...] = gk if first else dk[...] + gk
                term = dot(r["kt"][h, kb], ds)
                grad_q = term if grad_q is None else grad_q + term
            grad_q = grad_q.T * SCALE
            turned = grad_q * cosine - pltpu.roll(grad_q, 32, 1) * sine
            if h == 0:
                first_q = turned
            elif h == 1:
                r["gp"][qb, :, :128] = jnp.where(lower, first_q, turned).astype(BF)
            else:
                r["gp"][qb, :, 128:256] = turned.astype(BF)

    for i in range(4):
        qb = lax.rem(t + i, 4)
        if i > 0:
            got(r["gm"].at[qb], sid("gm_r", qb))
        attend_back(qb, i == 0)

    def finish(b, carry):
        at = rows(b, 256)
        cosine = r["cos"][at, :]
        sine = r["sin"][at, :]
        keys = []
        half = rows(lax.rem(b, 2), 256)
        place = lax.div(b, 2)
        for h in range(3):
            grad = r["wide"][2 * h + place, half, :] * SCALE
            keys.append(grad * cosine - pltpu.roll(grad, 32, 1) * sine)
        values = [r["wide"][6 + 2 * h + place, half, :] for h in range(3)]
        last_q = r["gp"][b, :, 128:256].astype(F32)
        r["gp"][b, :, 128:256] = jnp.where(lower, last_q, keys[0]).astype(BF)
        r["gp"][b, :, 256:384] = jnp.where(lower, keys[1], keys[2]).astype(BF)
        r["gp"][b, :, 384:512] = jnp.where(lower, values[0], values[1]).astype(BF)
        r["gp"][b, :, 512:576] = values[2][:, :HEAD].astype(BF)
        return carry

    lax.fori_loop(0, 4, finish, 0)

    def rs_part(b):
        return dot_nt(r["gp"][b], r["w_flat"][...])

    for k in range(1, 4):
        for side in range(2):
            step = 1 - 2 * side
            goal = t + step * (4 - k)
            nxt = t + step
            slot = 3 - k if side else k - 1

            @pl.when((goal >= 0) & (goal <= 3))
            def _():
                part = rs_part(goal)
                prev = t - step
                r["rs_out"][slot] = part.astype(BF)
                if k > 1:

                    @pl.when((prev >= 0) & (prev <= 3))
                    def _():
                        got(r["rs_in"].at[side, k - 2], sid("rs_r", side * 3 + k - 2))
                        summed = part + r["rs_in"][side, k - 2].astype(F32)
                        r["rs_out"][slot] = summed.astype(BF)

                remote(
                    r["rs_out"].at[slot],
                    r["rs_in"].at[side, k - 1],
                    sid("rs_s", side * 3 + k - 1),
                    sid("rs_r", side * 3 + k - 1),
                    (dp, nxt),
                ).start()

    own = rs_part(t)

    normed_all = r["normed"][...].reshape(1024, D)
    grad_w = dot_tn(normed_all, r["gp"][...].reshape(1024, 576)).astype(BF)
    r["gqkv"][...] = grad_w.reshape(2, 4, 96, 576)
    r["small"][10:11, :576] = total(r["gp"][...].reshape(1024, 576).astype(F32))
    remote(r["gqkv"].at[other], r["r1q"], sid("r1_s", 0), sid("r1_r", 0), sibling).start()

    got(r["r1q"], sid("r1_r", 0))
    sent(r["r1q"], sid("r1_s", 0))
    r["gqkv"][c] = (r["gqkv"][c].astype(F32) + r["r1q"][...].astype(F32)).astype(BF)
    for j in range(1, 4):
        r2_copy(3, j).start()
    got(r["r1o"], sid("r1_r", 1))
    sent(r["r1o"], sid("r1_s", 1))
    r["gwo"][c] = (r["gwo"][c].astype(F32) + r["r1o"][...].astype(F32)).astype(BF)
    for j in range(1, 4):
        r2_copy(0, j).start()

    for side in range(2):
        prev = t - (1 - 2 * side)

        @pl.when((prev >= 0) & (prev <= 3))
        def _():
            got(r["rs_in"].at[side, 2], sid("rs_r", side * 3 + 2))

        @pl.when((prev < 0) | (prev > 3))
        def _():
            r["rs_in"][side, 2] = jnp.zeros((256, D), BF)

    grad_normed = own + r["rs_in"][0, 2].astype(F32) + r["rs_in"][1, 2].astype(F32)
    unit1, rstd1 = norm_parts(r["tok"][...].astype(F32))
    r["small"][6:7, :] = total(grad_normed * unit1)
    r["small"][7:8, :] = total(grad_normed)
    r["zs"][t] = r["small"][...]
    for j in range(1, 4):
        remote(
            r["small"], r["zs"].at[t], sid("sz_s", j), sid("sz_r", t), (dp, zpeer(j))
        ).start()
    r["gtok"][...] = r["gres"][...] + norm_back(unit1, rstd1, grad_normed * r["gain"][...])

    def r2_sum(a):
        for j in range(1, 4):
            copy = r2_copy(a, j)
            copy.wait_recv()
            copy.wait_send()
        if a == 0:
            mine, theirs = r["gwo"].at[c, :, q], r["r2o"]
        elif a == 1:
            mine, theirs = r["gwu"].at[rows(q, 192), :], r["r2u"]
        elif a == 2:
            mine, theirs = r["gwd"].at[:, q], r["r2d"]
        else:
            mine, theirs = r["gqkv"].at[c, q], r["r2q"]
        acc = mine[...].astype(F32)
        for j in range(3):
            acc = acc + theirs[j].astype(F32)
        if a == 3:
            r["oqkv"][c, q] = acc.astype(BF)
        else:
            mine[...] = acc.astype(BF)

    def r3_piece(a, shard):
        if a == 0:
            return r["gwo"].at[c, shard, q]
        if a == 1:
            return r["gwu"].at[rows(q, 192), rows(shard, HALF)]
        return r["gwd"].at[shard, q]

    def r3_copy(a, j):
        goal = zpeer(j)
        dst = (r["r3o"], r["r3u"], r["r3d"])[a].at[t]
        return remote(
            r3_piece(a, goal), dst, sid("r3_s", a * 4 + j), sid("r3_r", a * 4 + t), (dp, goal)
        )

    def out_piece(a, col):
        if a == 0:
            return r["oo"].at[rows(col, 48), rows(c, HALF)]
        if a == 1:
            return r["ou"].at[rows(col, 192), rows(c, HALF)]
        if a == 2:
            return r["od"].at[c, col]
        return r["oqkv"].at[c, col]

    def r3_sum(a):
        buf = (r["r3o"], r["r3u"], r["r3d"])[a]
        acc = r3_piece(a, t)[...].astype(F32)
        for j in range(1, 4):
            got(buf.at[zpeer(j)], sid("r3_r", a * 4 + zpeer(j)))
            acc = acc + buf[zpeer(j)].astype(F32)
        out_piece(a, q)[...] = acc.astype(BF)

    def r4_copy(a, j):
        piece = out_piece(a, q)
        index = a * 3 + j - 1
        return remote(piece, piece, sid("r4_s", index), sid("r4_r", index), column(j))

    def r4_start(a):
        for j in range(1, 4):
            r4_copy(a, j).start()

    def half_out(a, who):
        if a == 0:
            return r["oo"].at[:, rows(who, HALF)]
        if a == 1:
            return r["ou"].at[:, rows(who, HALF)]
        if a == 2:
            return r["od"].at[who]
        return r["oqkv"].at[who]

    def r5_copy(a):
        piece = half_out(a, c)
        return remote(piece, piece, sid("r5_s", a), sid("r5_r", a), sibling)

    for a in (2, 1):
        r2_sum(a)
        for j in range(1, 4):
            r3_copy(a, j).start()
    r2_sum(3)
    r4_start(3)
    r2_sum(0)
    for j in range(1, 4):
        r3_copy(0, j).start()

    for j in range(1, 4):
        got(r["zs"].at[zpeer(j)], sid("sz_r", zpeer(j)))
    mine = lax.rem(dp, 8)
    for z in range(4):
        r["ds"][mine, 4 * z : 4 * z + 4, :] = r["zs"][z, 0:4, :]
    r["ds"][mine, 16:22, :] = (
        r["zs"][0, 4:10, :] + r["zs"][1, 4:10, :] + r["zs"][2, 4:10, :] + r["zs"][3, 4:10, :]
    )
    r["ds"][mine, 22:24, :] = r["small"][10:12, :]
    for j in range(1, 8):
        peer = lax.rem(mine + j, 8)
        remote(
            r["ds"].at[mine], r["ds"].at[mine], sid("sd_s", j), sid("sd_r", mine), (block + peer, t)
        ).start()

    for a in (2, 1, 0):
        r3_sum(a)
        r4_start(a)
    for a in (3, 2, 1, 0):
        for j in range(1, 4):
            got(out_piece(a, columns[j]), sid("r4_r", a * 3 + j - 1))
        r5_copy(a).start()
    for a in (3, 2, 1, 0):
        got(half_out(a, other), sid("r5_r", a))
    for j in range(1, 8):
        peer = lax.rem(mine + j, 8)
        got(r["ds"].at[peer], sid("sd_r", peer))

    for j in range(1, 4):
        sent(r["bup"].at[t], sid("bup_s", j))
        sent(r["small"], sid("sz_s", j))
        sent(r["blocks"].at[0], sid("gm_s", j))
        for a in range(3):
            sent(r3_piece(a, t), sid("r3_s", a * 4 + j))
    for i in range(4):
        sent(r["mod2"].at[c], sid("pair_s", i))
    for j in range(1, 8):
        sent(r["ds"].at[mine], sid("sd_s", j))
    for a in range(4):
        sent(half_out(a, c), sid("r5_s", a))
        for j in range(1, 4):
            sent(out_piece(a, q), sid("r4_s", a * 3 + j - 1))

    @pl.when(t < 3)
    def _():
        for a in range(3):
            sent(wpiece(a, t, q), sid("wz_s", a * 8))

    @pl.when(t > 0)
    def _():
        for a in range(3):
            sent(wpiece(a, t, q), sid("wz_s", a * 8 + 4))

    def w_sent(i, carry):
        k, side, b, nxt = hop(i)

        @pl.when((b >= 0) & (b <= 3))
        def _():
            sent(r["wo"].at[b, :, rows(c, HALF)], sid("wc_s", b))
            for a in range(3):
                for j in range(1, 4):
                    sent(wpiece(a, b, q), sid("wx_s", (a * 4 + b) * 3 + j - 1))

                @pl.when((nxt >= 0) & (nxt <= 3))
                def _():
                    sent(wpiece(a, b, q), sid("wz_s", a * 8 + side * 4 + k))

        return carry

    lax.fori_loop(1, 7, w_sent, 0)
    for k in range(1, 4):
        for side in range(2):
            goal = t + (1 - 2 * side) * (4 - k)

            @pl.when((goal >= 0) & (goal <= 3))
            def _():
                sent(r["rs_out"].at[k - 1], sid("rs_s", side * 3 + k - 1))


def fused(operands):
    vmem = pl.BlockSpec(memory_space=pltpu.VMEM)
    anywhere = pl.BlockSpec(memory_space=pl.ANY)
    specs = []
    for name in INPUTS:
        if name == "neg":
            specs.append(pl.BlockSpec(memory_space=pltpu.SMEM))
        elif name in ("wo_own", "wu_own", "wd_own"):
            specs.append(anywhere)
        else:
            specs.append(vmem)
    return pl.pallas_call(
        body,
        out_shape=(
            jax.ShapeDtypeStruct((256, D), BF),
            jax.ShapeDtypeStruct((256, D), F32),
            jax.ShapeDtypeStruct((2, 4, 96, 576), BF),
            jax.ShapeDtypeStruct((192, D), BF),
            jax.ShapeDtypeStruct((D, D), BF),
            jax.ShapeDtypeStruct((2, 4, 96, D), BF),
            jax.ShapeDtypeStruct((8, 24, D), F32),
        ),
        in_specs=specs,
        out_specs=(vmem,) * 7,
        scratch_shapes=[pltpu.VMEM(shape, kind) for shape, kind in SCRATCH.values()]
        + [pltpu.SemaphoreType.DMA((COUNT,))],
        compiler_params=pltpu.CompilerParams(
            collective_id=0, has_side_effects=True, vmem_limit_bytes=63 << 20
        ),
        name="layer",
    )(*[operands[name] for name in INPUTS])


def time_features(step_ids):
    half_dim = TE // 2
    freqs = jnp.exp(-math.log(10000.0) * jnp.arange(half_dim, dtype=F32) / half_dim)
    angles = (step_ids.astype(F32) / STEPS * TIME_SCALE)[:, None] * freqs[None, :]
    return jnp.concatenate([jnp.cos(angles), jnp.sin(angles)], axis=-1)


def on_device(
    tokens,
    long_count,
    timesteps,
    norm_gain,
    norm_bias,
    w_qkv,
    b_qkv,
    w_out,
    b_out,
    w_time,
    b_time,
    w_up,
    b_up,
    w_down,
    b_down,
    cotangent,
):
    highest = lax.Precision.HIGHEST
    n_dp = lax.axis_size("dp")
    n_tensor = lax.axis_size("tensor")
    assert tokens.shape == (SHORT, D) and n_tensor * SHORT == LONG and n_dp % 8 == 0
    rank = lax.axis_index("tensor")
    is_long = long_count[0] > 0
    row_ids = jnp.arange(LONG, dtype=jnp.int32)
    places = jnp.where(is_long, row_ids, row_ids % SHORT)
    half_dim = HEAD // 2
    freqs = jnp.exp(-math.log(10000.0) * jnp.arange(half_dim, dtype=F32) / half_dim)
    angles = places.astype(F32)[:, None] * jnp.tile(freqs, 4)[None, :]
    sign = jnp.tile(jnp.repeat(jnp.array([-1.0, 1.0], F32), half_dim), 2)
    slot = jnp.where(is_long, 0, rank)
    step = jnp.sum(jnp.where(jnp.arange(timesteps.shape[0]) == slot, timesteps, 0))
    features = time_features(step[None])
    modulation = jnp.dot(features, w_time, precision=highest) + b_time

    flat = jnp.transpose(w_qkv, (1, 0, 2)).reshape(D, 576)

    operands = {
        "neg": jnp.where(is_long, 0.0, -1e30).astype(F32)[None],
        "tok": tokens,
        "cot": cotangent,
        "gain": norm_gain[None],
        "bias": norm_bias[None],
        "b_out": b_out[None],
        "b_down": b_down[None],
        "mod": modulation,
        "feat": features,
        "b_flat": b_qkv.reshape(1, 576),
        "w_flat": flat,
        "cos": jnp.cos(angles),
        "sin": jnp.sin(angles) * sign[None, :],
        "wo_own": w_out,
        "wu_own": w_up,
        "wd_own": w_down.reshape(2, 4, 96, D),
        "bup_own": b_up[None],
    }
    result, grad_tokens, gqkv, gwo, gwu, gwd, small = fused(operands)

    gather = small[:, :16].reshape(8 * 4, 4, D)
    feats = gather[:, 3, :TE]
    grad_modulation = gather[:, :3].reshape(32, 3 * D)
    grad_w_time = lax.dot_general(
        feats, grad_modulation, (((0,), (0,)), ((), ())), precision=highest
    )
    grad_b_time = jnp.sum(grad_modulation, axis=0)
    units = small[:, 20:22].reshape(4, 2, 4, HALF).sum(axis=0)
    grad_b_up = lax.dynamic_index_in_dim(units, rank, 1, keepdims=False).reshape(2 * HALF)
    summed = small.sum(axis=0)
    grad_b_out, grad_b_down, grad_gain, grad_bias = (summed[n] for n in range(16, 20))
    grad_b_qkv = summed[22, :576].reshape(3, 192)
    grad_w_qkv = jnp.transpose(gqkv.astype(F32).reshape(D, 3, 192), (1, 0, 2))
    grads = (
        grad_gain,
        grad_bias,
        grad_w_qkv,
        grad_b_qkv,
        gwo.astype(F32),
        grad_b_out,
        grad_w_time,
        grad_b_time,
        gwu.astype(F32),
        grad_b_up,
        gwd.reshape(D, D).astype(F32),
        grad_b_down,
    )
    if n_dp > 8:
        groups = [[inner + 8 * outer for outer in range(n_dp // 8)] for inner in range(8)]
        grads = lax.psum(grads, "dp", axis_index_groups=groups)
    return (result, grad_tokens) + tuple(grads)


def solution(mesh):
    placed = (
        P(("dp", "tensor"), None),
        P("dp"),
        P("dp"),
        P(),
        P(),
        P(None, None, "tensor"),
        P(None, "tensor"),
        P("tensor", None),
        P(),
        P(),
        P(),
        P(None, "tensor"),
        P("tensor"),
        P("tensor", None),
        P(),
        P(("dp", "tensor"), None),
    )
    return jax.shard_map(
        on_device,
        mesh=mesh,
        in_specs=placed,
        out_specs=(
            P(("dp", "tensor"), None),
            P(("dp", "tensor"), None),
            P(),
            P(),
            P(None, None, "tensor"),
            P(None, "tensor"),
            P("tensor", None),
            P(),
            P(),
            P(),
            P(None, "tensor"),
            P("tensor"),
            P("tensor", None),
            P(),
        ),
        check_vma=False,
    )
```

```python
import math
from functools import partial
from itertools import accumulate
from types import SimpleNamespace

import jax
import jax.numpy as jnp
from jax import lax
from jax.experimental import pallas as pl
from jax.experimental.pallas import tpu as pltpu
from jax.sharding import PartitionSpec as P

HEAD = 64
TE = 128
STEPS = 1000
LONG = 1024
SHORT = 256
D = 768
HALF = 384
EPS = 1e-05
TIME_SCALE = 64.0
SCALE = 1.0 / math.sqrt(HEAD)
LOG_BASE = math.log(10000.0)
BF = jnp.bfloat16
F32 = jnp.float32
MESH = pl.DeviceIdType.MESH
HIGHEST = lax.Precision.HIGHEST

SEMS = dict(
    load=3,
    ag_s=16,
    ag_r=8,
    bup_s=4,
    bup_r=4,
    gb_s=4,
    gb_r=4,
    md_s=4,
    md_r=4,
    wz_s=8,
    wz_r=8,
    wx_s=12,
    wx_r=12,
    wc_s=8,
    wc_r=8,
    mix_s=4,
    mix_r=4,
    gmp_s=4,
    gmp_r=4,
    br_s=4,
    br_r=4,
    gm_s=4,
    gm_r=4,
    r1_s=4,
    r1_r=4,
    r2_s=6,
    r2_r=6,
    r3_s=12,
    r3_r=12,
    r4_s=12,
    r4_r=12,
    r5_s=4,
    r5_r=4,
    rs_s=12,
    rs_r=12,
    ez_s=4,
    ez_r=4,
    ed_s=8,
    ed_r=8,
    lz_s=4,
    lz_r=4,
    ld_s=8,
    ld_r=8,
)
COUNT = sum(SEMS.values())
S = SimpleNamespace(**dict(zip(SEMS, accumulate(SEMS.values(), initial=0))))

SCRATCH = dict(
    turn=((2, 256, 128), F32),
    feat=((1, TE), F32),
    modrow=((1, 3 * D), F32),
    normed=((4, 256, D), BF),
    q=((3, 1024, 128), BF),
    k=((3, 1024, 128), BF),
    v=((3, 1024, 128), BF),
    kt=((3, 4, 128, 256), BF),
    vt=((3, 4, 128, 256), BF),
    probs=((3, 4, 1024, 256), BF),
    blocks=((4, 256, 192), BF),
    mixed=((4, 256, 192), BF),
    wo=((4, 192, D), BF),
    w=((2, 4, 2, 96, D), BF),
    bup=((4, 1, D), F32),
    bqkv=((1, 576), F32),
    bupq=((1, D), F32),
    mod=((4, 256, D), BF),
    gb=((4, 256, D), BF),
    act=((4, 256, D), BF),
    gh=((4, 256, D), BF),
    wide=((12, 512, 128), F32),
    gmp_out=((3, 256, D), BF),
    gmp_in=((3, 256, D), BF),
    br_in=((3, 256, D), BF),
    gwo=((2, 4, 4, 48, HALF), BF),
    gw=((2, 4, 2, 96, D), BF),
    resid=((256, D), F32),
    gres=((256, D), F32),
    gm=((4, 256, 192), BF),
    gp=((4, 256, 576), BF),
    gqkv=((2, 4, 144, HALF), BF),
    r1o=((4, 4, 48, HALF), BF),
    r1w=((2, 4, 96, D), BF),
    r1q=((4, 144, HALF), BF),
    r2o=((3, 4, 48, HALF), BF),
    r2q=((3, 144, HALF), BF),
    r3w=((2, 4, 96, D), BF),
    r3o=((4, 48, HALF), BF),
    ow=((2, 4, 2, 96, D), BF),
    rs_out=((3, 256, D), BF),
    rs_in=((2, 3, 256, D), BF),
    small=((8, D), F32),
    zs=((4, 8, D), F32),
    ds=((8, 24, D), F32),
    late=((8, D), F32),
    zl=((4, 8, D), F32),
    dl=((8, 8, D), F32),
    gmat=((4, 32, D), F32),
)


def dot(a, b):
    return jnp.dot(a, b, preferred_element_type=F32)


def dot_nt(a, b):
    return lax.dot_general(a, b, (((1,), (1,)), ((), ())), preferred_element_type=F32)


def dot_tn(a, b, precision=None):
    dims = (((0,), (0,)), ((), ()))
    return lax.dot_general(a, b, dims, precision=precision, preferred_element_type=F32)


def norm_parts(values):
    center = values - jnp.mean(values, axis=-1, keepdims=True)
    rstd = lax.rsqrt(jnp.mean(center * center, axis=-1, keepdims=True) + EPS)
    return center * rstd, rstd


def norm_back(unit, rstd, grad):
    mean_g = jnp.mean(grad, axis=-1, keepdims=True)
    mean_gn = jnp.mean(grad * unit, axis=-1, keepdims=True)
    return (grad - mean_g - unit * mean_gn) * rstd


def total(values):
    return jnp.sum(values, axis=0, keepdims=True)


def row(ref):
    return ref[...].reshape(1, -1)


def pick(index, options):
    chosen = options[-1]
    for n in range(len(options) - 2, -1, -1):
        chosen = jnp.where(index == n, options[n], chosen)
    return chosen


def body(names, *refs):
    sem = refs[-1]
    r = SimpleNamespace(**dict(zip(names, refs[:-1], strict=True)))
    dp = lax.axis_index("dp")
    t = lax.axis_index("tensor")
    mine = lax.rem(dp, 8)
    block = dp - mine
    c = lax.rem(dp, 2)
    q = lax.div(mine, 2)
    other = 1 - c
    sibling = (dp + 1 - 2 * c, t)
    columns = [q, q + 1 - 2 * lax.rem(q, 2), q + 2 - 4 * lax.div(q, 2), 3 - q]

    def column(j):
        return (block + 2 * columns[j] + c, t)

    def zpeer(j):
        return lax.rem(t + j, 4)

    def remote(src, dst, send, recv, device):
        return pltpu.make_async_remote_copy(
            src_ref=src,
            dst_ref=dst,
            send_sem=sem.at[send],
            recv_sem=sem.at[recv],
            device_id=device,
            device_id_type=MESH,
        )

    def got(ref, recv):
        remote(ref, ref, recv, recv, sibling).wait_recv()

    def sent(ref, send):
        remote(ref, ref, send, send, sibling).wait_send()

    def rows(index, size):
        return pl.ds(pl.multiple_of(index * size, size), size)

    def hop(i):
        k = lax.div(i + 1, 2)
        side = 1 - lax.rem(i, 2)
        step = 2 * side - 1
        return k, side, t + step * k, t - step

    def inside(b):
        return (b >= 0) & (b <= 3)

    barrier = pltpu.get_barrier_semaphore()
    for j in range(1, 4):
        pl.semaphore_signal(barrier, inc=1, device_id=(dp, zpeer(j)), device_id_type=MESH)
    for j in range(1, 8):
        peer = block + lax.rem(mine + j, 8)
        pl.semaphore_signal(barrier, inc=1, device_id=(peer, t), device_id_type=MESH)

    loads = [
        pltpu.make_async_copy(r.wo_own, r.wo.at[t], sem.at[S.load]),
        pltpu.make_async_copy(r.wu_own, r.act.at[0:3], sem.at[S.load + 1]),
        pltpu.make_async_copy(r.wd_own.at[q], r.w.at[1, t], sem.at[S.load + 2]),
    ]
    for load in loads:
        load.start()

    unit, _ = norm_parts(r.tok[...].astype(F32))
    r.normed[t] = (unit * row(r.gain) + row(r.bias)).astype(BF)
    r.bup[t] = row(r.bup_own)
    for n in range(3):
        r.bqkv[:, 192 * n : 192 * (n + 1)] = r.b_qkv[n : n + 1, :]
    pl.semaphore_wait(barrier, 10)

    def ag_chunk(b, chunk):
        return r.normed.at[b, 128 * chunk : 128 * (chunk + 1)]

    def ag_copy(b, chunk, side, k, device):
        piece = ag_chunk(b, chunk)
        send = S.ag_s + (side * 4 + k) * 2 + chunk
        return remote(piece, piece, send, S.ag_r + 2 * b + chunk, (dp, device))

    for chunk in range(2):

        @pl.when(t < 3)
        def _():
            ag_copy(t, chunk, 0, 0, t + 1).start()

        @pl.when(t > 0)
        def _():
            ag_copy(t, chunk, 1, 0, t - 1).start()

    def wo_piece(shard, col):
        return r.wo.at[shard, rows(col, 48), rows(c, HALF)]

    def wz_piece(a, shard):
        return wo_piece(shard, q) if a == 0 else r.w.at[:, shard, c]

    def wz_copy(a, j):
        piece = wz_piece(a, t)
        return remote(piece, piece, S.wz_s + a * 4 + j, S.wz_r + a * 4 + t, (dp, zpeer(j)))

    loads[0].wait()
    for j in range(1, 4):
        wz_copy(0, j).start()
    for j in range(1, 4):
        remote(r.bup.at[t], r.bup.at[t], S.bup_s + j, S.bup_r + t, (dp, zpeer(j))).start()

    is_long = r.lc[0]
    slot = (1 - is_long) * t
    step = jnp.int32(0)
    for n in range(4):
        step = step + jnp.where(slot == n, r.ts[n], 0)
    lane = lax.broadcasted_iota(jnp.int32, (1, TE), 1)
    half_lane = lax.rem(lane, TE // 2).astype(F32)
    angle = (step.astype(F32) / STEPS * TIME_SCALE) * jnp.exp(half_lane * (-LOG_BASE / (TE // 2)))
    feat = jnp.where(lane < TE // 2, jnp.cos(angle), jnp.sin(angle))
    r.feat[...] = feat
    wide_feat = jnp.broadcast_to(feat, (8, TE))
    modulation = jnp.dot(wide_feat, r.w_time[...], precision=HIGHEST, preferred_element_type=F32)
    r.modrow[...] = modulation[0:1] + row(r.b_time)
    gate = r.modrow[:, 2 * D :]
    r.gb[q] = (gate * r.cot[...].astype(F32)).astype(BF)
    for j in range(1, 4):
        remote(r.gb.at[q], r.gb.at[q], S.gb_s + j, S.gb_r + q, column(j)).start()

    lane = lax.broadcasted_iota(jnp.int32, (1, 128), 1)
    freqs = jnp.exp(lax.rem(lane, 32).astype(F32) * (-LOG_BASE / 32))
    sign = jnp.where(lax.rem(lane, 64) < 32, -1.0, 1.0)
    angles = lax.broadcasted_iota(jnp.int32, (256, 128), 0).astype(F32) * freqs
    r.turn[0] = jnp.cos(angles)
    r.turn[1] = jnp.sin(angles) * sign

    def rope_tables(b):
        offset = (b * 256 * is_long).astype(F32) * freqs
        cosine = jnp.cos(offset)
        sine = jnp.sin(offset) * sign
        return (
            r.turn[0] * cosine - r.turn[1] * sine,
            r.turn[1] * cosine + r.turn[0] * sine,
        )

    loads[1].wait()
    loads[2].wait()
    for n in range(4):

        @pl.when(q == n)
        def _():
            part = r.act[0:3].reshape(D, D)[:, 192 * n : 192 * (n + 1)]
            r.w[0, t] = part.T.reshape(2, 96, D)

    lower = lax.broadcasted_iota(jnp.int32, (256, 128), 1) < HEAD

    def project(b):
        y = dot_nt(r.normed[b], r.w_qkv[...]) + r.bqkv[...]
        at = rows(b, 256)
        cosine, sine = rope_tables(b)
        doubled = []
        for n in range(3):
            tile = y[:, 128 * n : 128 * (n + 1)]
            swapped = pltpu.roll(tile, HEAD, 1)
            doubled += [jnp.where(lower, tile, swapped), jnp.where(lower, swapped, tile)]
        for h in range(3):
            for part, dest in ((doubled[h], r.q), (doubled[3 + h], r.k)):
                turned = part * cosine + pltpu.roll(part, 32, 1) * sine
                dest[h, at, :] = turned.astype(BF)
            r.kt[h, b] = turned.T.astype(BF)
        tile = y[:, 384:512]
        for h, value in enumerate((jnp.where(lower, tile, 0.0), jnp.where(lower, 0.0, tile))):
            r.v[h, at, :] = value.astype(BF)
            r.vt[h, b] = value.T.astype(BF)
        value = y[:, 512:576]
        r.v[2, at, :HEAD] = value.astype(BF)
        r.vt[2, b, :HEAD, :] = value.T.astype(BF)

    def ag_step(i, carry):
        k, side, b, nxt = hop(i)

        @pl.when(inside(b))
        def _():
            @pl.when(i > 0)
            def _():
                for chunk in range(2):
                    got(ag_chunk(b, chunk), S.ag_r + 2 * b + chunk)

                    @pl.when(inside(nxt))
                    def _():
                        ag_copy(b, chunk, side, k, nxt).start()

            project(b)

        return carry

    lax.fori_loop(0, 7, ag_step, 0)

    for chunk in range(2):

        @pl.when(t < 3)
        def _():
            sent(ag_chunk(t, 0), S.ag_s + chunk)

        @pl.when(t > 0)
        def _():
            sent(ag_chunk(t, 0), S.ag_s + 8 + chunk)

    def ag_sent(i, carry):
        k, side, b, nxt = hop(i)

        @pl.when(inside(b) & inside(nxt))
        def _():
            for chunk in range(2):
                sent(ag_chunk(b, 0), S.ag_s + (side * 4 + k) * 2 + chunk)

        return carry

    lax.fori_loop(1, 7, ag_sent, 0)

    def wx_copy(b, j):
        index = b * 3 + j - 1
        piece = wo_piece(b, q)
        return remote(piece, piece, S.wx_s + index, S.wx_r + index, column(j))

    def wc_copy(a, b):
        piece = r.wo.at[b, :, rows(c, HALF)] if a == 0 else r.w.at[:, b, c]
        return remote(piece, piece, S.wc_s + a * 4 + b, S.wc_r + a * 4 + b, sibling)

    for j in range(1, 4):
        b = zpeer(j)
        got(wz_piece(0, b), S.wz_r + b)
        for col in range(1, 4):
            wx_copy(b, col).start()

    neg = jnp.where(is_long > 0, 0.0, -1e30)

    def attend(i, carry):
        qb = lax.rem(t + 1 + i, 4)
        outs = []
        for h in range(3):
            queries = r.q[h, rows(qb, 256), :]
            parts = []
            for kb in range(4):
                s = dot_nt(r.k[h, kb * 256 : (kb + 1) * 256, :], queries) * (0.5 * SCALE)
                parts.append(s + jnp.where(qb == kb, 0.0, neg))
            top = parts[0].max(axis=0, keepdims=True)
            for kb in range(1, 4):
                top = jnp.maximum(top, parts[kb].max(axis=0, keepdims=True))
            parts = [jnp.exp(s - top) for s in parts]
            inverse = 1.0 / sum(total(s) for s in parts)
            out = None
            for kb in range(4):
                p = (parts[kb] * inverse).astype(BF)
                r.probs[h, qb, kb * 256 : (kb + 1) * 256, :] = p
                term = dot(r.vt[h, kb] if h < 2 else r.vt[h, kb, :HEAD, :], p)
                out = term if out is None else out + term
            outs.append(out)
        low, high = (outs[0] + outs[1]).T.astype(BF), outs[2].T.astype(BF)

        @pl.when(i < 3)
        def _():
            r.blocks[qb, :, :128] = low
            r.blocks[qb, :, 128:192] = high
            remote(r.blocks.at[qb], r.mixed.at[t], S.mix_s + i, S.mix_r + t, (dp, qb)).start()

        @pl.when(i == 3)
        def _():
            r.mixed[t, :, :128] = low
            r.mixed[t, :, 128:192] = high

        return carry

    lax.fori_loop(0, 4, attend, 0)
    for j in range(1, 4):
        wz_copy(1, j).start()

    for j in range(1, 4):
        got(r.bup.at[zpeer(j)], S.bup_r + zpeer(j))
    for s in range(4):
        options = [r.bup[s, :, 192 * n : 192 * (n + 1)] for n in range(4)]
        r.bupq[:, 192 * s : 192 * (s + 1)] = pick(q, options)

    for j in range(1, 4):
        b = zpeer(j)
        for col in range(1, 4):
            got(wo_piece(b, columns[col]), S.wx_r + b * 3 + col - 1)
        wc_copy(0, b).start()
    for j in range(1, 4):
        got(r.wo.at[zpeer(j), :, rows(other, HALF)], S.wc_r + zpeer(j))
    for j in range(1, 4):
        got(r.mixed.at[zpeer(j)], S.mix_r + zpeer(j))

    attended = jnp.broadcast_to(row(r.b_out), (256, D))
    for g in range(4):
        attended = attended + dot(r.mixed[g], r.wo[g])
    resid = r.tok[...].astype(F32) + attended
    r.resid[...] = resid
    unit2, rstd2 = norm_parts(resid)
    scale1 = 1.0 + r.modrow[:, :D]
    r.mod[q] = (unit2 * scale1 + r.modrow[:, D : 2 * D]).astype(BF)
    for j in range(1, 4):
        remote(r.mod.at[q], r.mod.at[q], S.md_s + j, S.md_r + q, column(j)).start()
    for j in range(1, 4):
        b = zpeer(j)
        got(wz_piece(1, b), S.wz_r + 4 + b)
        wc_copy(1, b).start()
    for j in range(1, 4):
        got(r.w.at[:, zpeer(j), other], S.wc_r + 4 + zpeer(j))

    def forward(j, carry):
        col = pick(j, columns)

        @pl.when(j > 0)
        def _():
            got(r.gb.at[col], S.gb_r + col)
            got(r.mod.at[col], S.md_r + col)

        w_up = r.w[0].reshape(D, D)
        hidden = dot_nt(r.mod[col], w_up) + r.bupq[...]
        inner = math.sqrt(2.0 / math.pi)
        square = hidden * hidden
        th = jnp.tanh(inner * hidden * (1.0 + 0.044715 * square))
        halfsum = 0.5 * (1.0 + th)
        r.act[col] = (hidden * halfsum).astype(BF)
        slope = halfsum + 0.5 * hidden * (1.0 - th * th) * (inner * (1.0 + 3 * 0.044715 * square))
        grad_active = dot_nt(r.gb[col], r.w[1].reshape(D, D))
        gh = (slope * grad_active).astype(BF)
        r.gh[col] = gh
        grad_mod = dot(gh, w_up)

        @pl.when(j == 0)
        def _():
            r.gres[...] = grad_mod

        @pl.when(j > 0)
        def _():
            r.gmp_out[j - 1] = grad_mod.astype(BF)
            device = (block + 2 * col + c, t)
            remote(r.gmp_out.at[j - 1], r.gmp_in.at[j - 1], S.gmp_s + j, S.gmp_r + j, device).start()

        return carry

    lax.fori_loop(0, 4, forward, 0)

    def r2_copy(a, j):
        col = columns[j]
        src = r.gwo.at[c, :, col] if a == 0 else r.gqkv.at[c, col]
        dst = (r.r2o, r.r2q)[a].at[j - 1]
        return remote(src, dst, S.r2_s + a * 3 + j - 1, S.r2_r + a * 3 + j - 1, column(j))

    def r3_piece(a, shard):
        return r.gwo.at[c, shard, q] if a == 0 else r.gw.at[a - 1, shard, c]

    def r3_copy(a, j):
        goal = zpeer(j)
        dst = r.r3o.at[t] if a == 0 else r.r3w.at[a - 1, t]
        return remote(
            r3_piece(a, goal), dst, S.r3_s + a * 4 + j, S.r3_r + a * 4 + t, (dp, goal)
        )

    def out_piece(a, col):
        if a == 0:
            return r.oo.at[rows(col, 48), rows(c, HALF)]
        if a < 3:
            return r.ow.at[a - 1, col, c]
        return r.oqkv.at[rows(col, 144), rows(c, HALF)]

    def r4_copy(a, j):
        piece = out_piece(a, q)
        index = a * 3 + j - 1
        return remote(piece, piece, S.r4_s + index, S.r4_r + index, column(j))

    def half_out(a, who):
        if a == 0:
            return r.oo.at[:, rows(who, HALF)]
        if a < 3:
            return r.ow.at[a - 1, :, who]
        return r.oqkv.at[:, rows(who, HALF)]

    def r5_copy(a):
        piece = half_out(a, c)
        return remote(piece, piece, S.r5_s + a, S.r5_r + a, sibling)

    def r1_copy_w(a):
        return remote(r.gw.at[a, :, other], r.r1w.at[a], S.r1_s + a, S.r1_r + a, sibling)

    def r1_sum_w(a):
        got(r.r1w.at[a], S.r1_r + a)
        r.gw[a, :, c] = (r.gw[a, :, c].astype(F32) + r.r1w[a].astype(F32)).astype(BF)

    def r3_start(a):
        for j in range(1, 4):
            r3_copy(a, j).start()

    def r1_sum_o():
        got(r.r1o, S.r1_r + 2)
        r.gwo[c] = (r.gwo[c].astype(F32) + r.r1o[...].astype(F32)).astype(BF)
        for j in range(1, 4):
            r2_copy(0, j).start()

    def r2_sum(a):
        for j in range(1, 4):
            copy = r2_copy(a, j)
            copy.wait_recv()
            copy.wait_send()
        mine_ref = r.gwo.at[c, :, q] if a == 0 else r.gqkv.at[c, q]
        theirs = (r.r2o, r.r2q)[a]
        acc = mine_ref[...].astype(F32)
        for j in range(3):
            acc = acc + theirs[j].astype(F32)
        if a == 0:
            mine_ref[...] = acc.astype(BF)
            r3_start(0)
        else:
            out_piece(3, q)[...] = acc.astype(BF)
            for j in range(1, 4):
                r4_copy(3, j).start()

    def r3_sum(a):
        buf = r.r3o if a == 0 else r.r3w.at[a - 1]
        acc = r3_piece(a, t)[...].astype(F32)
        for j in range(1, 4):
            got(buf.at[zpeer(j)], S.r3_r + a * 4 + zpeer(j))
            acc = acc + buf[zpeer(j)].astype(F32)
        out_piece(a, q)[...] = acc.astype(BF)
        for j in range(1, 4):
            r4_copy(a, j).start()

    def r4_wait(a):
        for j in range(1, 4):
            got(out_piece(a, columns[j]), S.r4_r + a * 3 + j - 1)
        r5_copy(a).start()

    def weight_grad(a):
        left = (r.gh, r.act)[a][...].reshape(1024, D)
        right = (r.mod, r.gb)[a][...].reshape(1024, D)
        for s in range(4):
            grad = dot_tn(left[:, 192 * s : 192 * (s + 1)], right)
            r.gw[a, s] = grad.astype(BF).reshape(2, 96, D)

    for a in (1, 0):
        weight_grad(a)
        r1_copy_w(a).start()
    r1_sum_w(1)
    r3_start(2)
    r1_sum_w(0)

    grad_mod = r.gres[...]
    for j in range(1, 4):
        got(r.gmp_in.at[j - 1], S.gmp_r + j)
        grad_mod = grad_mod + r.gmp_in[j - 1].astype(F32)
    unit2, rstd2 = norm_parts(r.resid[...])
    scale1 = 1.0 + r.modrow[:, :D]
    grad_resid = r.cot[...].astype(F32) + norm_back(unit2, rstd2, grad_mod * scale1)
    r.gres[...] = grad_resid
    grad_att = grad_resid.astype(BF)
    for i in range(3):
        sent(r.blocks.at[0], S.mix_s + i)
    for i in range(1, 4):
        g = lax.rem(t + i, 4)
        r.blocks[g] = dot_nt(grad_att, r.wo[g]).astype(BF)
        remote(r.blocks.at[g], r.gm.at[t], S.gm_s + i, S.gm_r + t, (dp, g)).start()
    r.gm[t] = dot_nt(grad_att, r.wo[t]).astype(BF)
    r.small[0:1, :] = total(grad_mod * unit2)
    r.small[1:2, :] = total(grad_mod)
    r.small[3:4, :] = jnp.zeros((1, D), F32)
    r.small[3:4, :TE] = r.feat[...]
    r.small[4:5, :] = total(grad_att.astype(F32))
    r.small[5:6, :] = total(r.gb[q].astype(F32))
    r.small[6:7, :] = total(r.gh[...].reshape(1024, D).astype(F32))
    r.small[7:8, :] = jnp.zeros((1, D), F32)
    for g in range(4):
        grad = dot_tn(r.mixed[g], grad_att).astype(BF)
        for half in range(2):
            r.gwo[half, g] = grad[:, HALF * half : HALF * (half + 1)].reshape(4, 48, HALF)
    remote(r.gwo.at[other], r.r1o, S.r1_s + 2, S.r1_r + 2, sibling).start()
    for j in range(1, 4):
        sent(r.gmp_out.at[j - 1], S.gmp_s + j)

    def down(n, carry):
        j = lax.rem(n + 1, 4)
        col = pick(j, columns)
        branch = dot(r.act[col], r.w[1].reshape(D, D))

        @pl.when(j == 0)
        def _():
            r.gtok[...] = branch

        @pl.when(j > 0)
        def _():
            r.gmp_out[j - 1] = branch.astype(BF)
            device = (block + 2 * col + c, t)
            remote(r.gmp_out.at[j - 1], r.br_in.at[j - 1], S.br_s + j, S.br_r + j, device).start()

        return carry

    lax.fori_loop(0, 4, down, 0)


    r1_sum_o()

    r.wide[...] = jnp.zeros((12, 512, 128), F32)

    def attend_back(i, carry):
        qb = lax.rem(t + i, 4)

        @pl.when(i > 0)
        def _():
            got(r.gm.at[qb], S.gm_r + qb)

        @pl.when(i == 3)
        def _():
            r3_start(1)

        at = rows(qb, 256)
        cosine, sine = rope_tables(qb)
        for h in range(3):
            width = 128 if h < 2 else HEAD
            grad_out = r.gm[qb, :, :128] if h < 2 else r.gm[qb, :, 128:192]
            queries = r.q[h, at, :]
            probs = []
            grads = []
            inner = None
            for kb in range(4):
                keys = slice(kb * 256, (kb + 1) * 256)
                p = r.probs[h, qb, keys, :]
                g = dot_nt(r.v[h, keys, :width], grad_out)
                term = total(g * p.astype(F32))
                inner = term if inner is None else inner + term
                probs.append(p)
                grads.append(g)
                place = slice(256 * (kb % 2), 256 * (kb % 2 + 1))
                r.wide[6 + 2 * h + kb // 2, place, :width] += dot(p, grad_out)
            grad_q = None
            for kb in range(4):
                ds = (probs[kb].astype(F32) * (grads[kb] - inner)).astype(BF)
                place = slice(256 * (kb % 2), 256 * (kb % 2 + 1))
                r.wide[2 * h + kb // 2, place, :] += dot(ds, queries)
                term = dot(r.kt[h, kb], ds)
                grad_q = term if grad_q is None else grad_q + term
            grad_q = grad_q.T * SCALE
            turned = grad_q * cosine - pltpu.roll(grad_q, 32, 1) * sine
            if h == 0:
                first_q = turned
            elif h == 1:
                r.gp[qb, :, :128] = jnp.where(lower, first_q, turned).astype(BF)
            else:
                r.gp[qb, :, 128:256] = turned.astype(BF)
        return carry

    lax.fori_loop(0, 4, attend_back, 0)

    def finish(b, carry):
        cosine, sine = rope_tables(b)
        keys = []
        half = rows(lax.rem(b, 2), 256)
        place = lax.div(b, 2)
        for h in range(3):
            grad = r.wide[2 * h + place, half, :] * SCALE
            keys.append(grad * cosine - pltpu.roll(grad, 32, 1) * sine)
        values = [r.wide[6 + 2 * h + place, half, :] for h in range(3)]
        last_q = r.gp[b, :, 128:256].astype(F32)
        r.gp[b, :, 128:256] = jnp.where(lower, last_q, keys[0]).astype(BF)
        r.gp[b, :, 256:384] = jnp.where(lower, keys[1], keys[2]).astype(BF)
        r.gp[b, :, 384:512] = jnp.where(lower, values[0], values[1]).astype(BF)
        r.gp[b, :, 512:576] = values[2][:, :HEAD].astype(BF)
        return carry

    lax.fori_loop(0, 4, finish, 0)

    def rs_step(k):
        for side in range(2):
            step = 1 - 2 * side
            goal = t + step * (4 - k)
            nxt = t + step
            prev = t - step
            slot = 3 - k if side else k - 1

            @pl.when(inside(goal))
            def _():
                for chunk in range(2):
                    at = slice(128 * chunk, 128 * (chunk + 1))
                    part = dot(r.gp[goal, at, :], r.w_qkv[...])
                    r.rs_out[slot, at, :] = part.astype(BF)
                    if k > 1:

                        @pl.when(inside(prev))
                        def _():
                            index = (side * 3 + k - 2) * 2 + chunk
                            got(r.rs_in.at[side, k - 2, at], S.rs_r + index)
                            summed = part + r.rs_in[side, k - 2, at, :].astype(F32)
                            r.rs_out[slot, at, :] = summed.astype(BF)

                    index = (side * 3 + k - 1) * 2 + chunk
                    remote(
                        r.rs_out.at[slot, at],
                        r.rs_in.at[side, k - 1, at],
                        S.rs_s + index,
                        S.rs_r + index,
                        (dp, nxt),
                    ).start()

    rs_step(1)
    r2_sum(0)

    branch = r.gtok[...] + row(r.b_down)
    for j in range(1, 4):
        got(r.br_in.at[j - 1], S.br_r + j)
        branch = branch + r.br_in[j - 1].astype(F32)
    r.result[...] = (r.resid[...] + r.modrow[:, 2 * D :] * branch).astype(BF)
    r.small[2:3, :] = total(r.cot[...].astype(F32) * branch)
    r.zs[t] = r.small[...]
    for j in range(1, 4):
        remote(r.small, r.zs.at[t], S.ez_s + j, S.ez_r + t, (dp, zpeer(j))).start()

    grad_w = dot_tn(r.gp[...].reshape(1024, 576), r.normed[...].reshape(1024, D)).astype(BF)
    for half in range(2):
        lanes = slice(HALF * half, HALF * (half + 1))
        r.gqkv[half] = grad_w[:, lanes].reshape(4, 144, HALF)
    r3_sum(2)
    remote(r.gqkv.at[other], r.r1q, S.r1_s + 3, S.r1_r + 3, sibling).start()
    r.late[...] = jnp.zeros((8, D), F32)
    r.late[2:3, :576] = total(r.gp[...].reshape(1024, 576).astype(F32))
    got(r.r1q, S.r1_r + 3)
    r.gqkv[c] = (r.gqkv[c].astype(F32) + r.r1q[...].astype(F32)).astype(BF)
    for j in range(1, 4):
        r2_copy(1, j).start()
    rs_step(2)

    for j in range(1, 4):
        got(r.zs.at[zpeer(j)], S.ez_r + zpeer(j))
    for z in range(4):
        for n in range(4):
            r.ds[mine, 4 * n + z : 4 * n + z + 1, :] = r.zs[z, n : n + 1, :]
    r.ds[mine, 16:20, :] = r.zs[0, 4:8, :] + r.zs[1, 4:8, :] + r.zs[2, 4:8, :] + r.zs[3, 4:8, :]
    r.ds[mine, 20:24, :] = jnp.zeros((4, D), F32)
    for j in range(1, 8):
        peer = lax.rem(mine + j, 8)
        remote(
            r.ds.at[mine], r.ds.at[mine], S.ed_s + j, S.ed_r + mine, (block + peer, t)
        ).start()
    rs_step(3)
    own = dot(r.gp[t], r.w_qkv[...])
    r2_sum(1)
    r3_sum(1)
    r3_sum(0)

    for side in range(2):
        prev = t - (1 - 2 * side)

        @pl.when(inside(prev))
        def _():
            for chunk in range(2):
                at = slice(128 * chunk, 128 * (chunk + 1))
                got(r.rs_in.at[side, 2, at], S.rs_r + (side * 3 + 2) * 2 + chunk)

        @pl.when((prev < 0) | (prev > 3))
        def _():
            r.rs_in[side, 2] = jnp.zeros((256, D), BF)

    grad_normed = own + r.rs_in[0, 2].astype(F32) + r.rs_in[1, 2].astype(F32)
    unit1, rstd1 = norm_parts(r.tok[...].astype(F32))
    r.late[0:1, :] = total(grad_normed * unit1)
    r.late[1:2, :] = total(grad_normed)
    r.zl[t] = r.late[...]
    for j in range(1, 4):
        remote(r.late, r.zl.at[t], S.lz_s + j, S.lz_r + t, (dp, zpeer(j))).start()
    r.gtok[...] = r.gres[...] + norm_back(unit1, rstd1, grad_normed * row(r.gain))

    for a in (2, 3, 1, 0):
        r4_wait(a)
    for j in range(1, 4):
        got(r.zl.at[zpeer(j)], S.lz_r + zpeer(j))
    r.dl[mine] = r.zl[0] + r.zl[1] + r.zl[2] + r.zl[3]
    r.dl[mine, 2:3, :] = r.late[2:3, :]
    for j in range(1, 8):
        peer = lax.rem(mine + j, 8)
        remote(
            r.dl.at[mine], r.dl.at[mine], S.ld_s + j, S.ld_r + mine, (block + peer, t)
        ).start()
    for j in range(1, 8):
        peer = lax.rem(mine + j, 8)
        got(r.ds.at[peer], S.ed_r + peer)
    for peer in range(8):
        for n in range(4):
            r.gmat[n, 4 * peer : 4 * peer + 4, :] = r.ds[peer, 4 * n : 4 * n + 4, :]
    for n in range(3):
        r.gwt[:, D * n : D * (n + 1)] = dot_tn(r.gmat[3][:, :TE], r.gmat[n], HIGHEST)
        r.gbt[D * n : D * (n + 1)] = total(r.gmat[n]).reshape(D)
    r.gbo[...] = sum(r.ds[peer, 16:17, :] for peer in range(8)).reshape(D)
    r.gbd[...] = sum(r.ds[peer, 17:18, :] for peer in range(8)).reshape(D)
    for n in range(4):
        units = r.ds[2 * n, 18:19, :] + r.ds[2 * n + 1, 18:19, :]
        options = [units[:, 192 * s : 192 * (s + 1)] for s in range(4)]
        r.bupq[:, 192 * n : 192 * (n + 1)] = pick(t, options)
    r.gbu[...] = r.bupq[...].reshape(D)
    for a in (2, 3, 1, 0):
        got(half_out(a, other), S.r5_r + a)
    r.od[...] = r.ow[1].reshape(D, D)
    r.ou[...] = r.ow[0].reshape(D, D).T
    for j in range(1, 8):
        peer = lax.rem(mine + j, 8)
        got(r.dl.at[peer], S.ld_r + peer)
    last = sum(r.dl[peer, 0:3, :] for peer in range(8))
    r.ggain[...] = last[0:1].reshape(D)
    r.gbias[...] = last[1:2].reshape(D)
    for n in range(3):
        r.gbqkv[n : n + 1, :] = last[2:3, 192 * n : 192 * (n + 1)]

    for j in range(1, 4):
        sent(r.bup.at[t], S.bup_s + j)
        sent(r.small, S.ez_s + j)
        sent(r.late, S.lz_s + j)
        sent(r.blocks.at[0], S.gm_s + j)
        for base in (S.gb_s, S.md_s, S.br_s):
            sent(r.gb.at[0], base + j)
        for a in range(3):
            sent(r3_piece(a, t), S.r3_s + a * 4 + j)
        for a in range(2):
            sent(wz_piece(a, t), S.wz_s + a * 4 + j)
        b = zpeer(j)
        sent(r.wo.at[b, :, rows(c, HALF)], S.wc_s + b)
        sent(wz_piece(1, b), S.wc_s + 4 + b)
        for col in range(1, 4):
            sent(wo_piece(b, q), S.wx_s + b * 3 + col - 1)
    for a in range(2):
        sent(r.r1w.at[a], S.r1_s + a)
    sent(r.r1o, S.r1_s + 2)
    sent(r.r1q, S.r1_s + 3)
    for j in range(1, 8):
        sent(r.ds.at[mine], S.ed_s + j)
        sent(r.dl.at[mine], S.ld_s + j)
    for a in range(4):
        sent(half_out(a, c), S.r5_s + a)
        for j in range(1, 4):
            sent(out_piece(a, q), S.r4_s + a * 3 + j - 1)

    for k in range(1, 4):
        for side in range(2):
            goal = t + (1 - 2 * side) * (4 - k)

            @pl.when(inside(goal))
            def _():
                for chunk in range(2):
                    sent(r.rs_out.at[0, 0:128], S.rs_s + (side * 3 + k - 1) * 2 + chunk)


def fused(scalars, blocks, far, outs):
    vmem = pl.BlockSpec(memory_space=pltpu.VMEM)
    smem = pl.BlockSpec(memory_space=pltpu.SMEM)
    anywhere = pl.BlockSpec(memory_space=pl.ANY)
    operands = scalars | blocks | far
    return pl.pallas_call(
        partial(body, [*operands, *outs, *SCRATCH]),
        out_shape=[jax.ShapeDtypeStruct(shape, kind) for shape, kind in outs.values()],
        in_specs=[smem] * len(scalars) + [vmem] * len(blocks) + [anywhere] * len(far),
        out_specs=[vmem] * len(outs),
        scratch_shapes=[pltpu.VMEM(shape, kind) for shape, kind in SCRATCH.values()]
        + [pltpu.SemaphoreType.DMA((COUNT,))],
        compiler_params=pltpu.CompilerParams(
            collective_id=0, has_side_effects=True, vmem_limit_bytes=63 << 20
        ),
        name="layer",
    )(*operands.values())


def on_device(
    tokens,
    long_count,
    timesteps,
    norm_gain,
    norm_bias,
    w_qkv,
    b_qkv,
    w_out,
    b_out,
    w_time,
    b_time,
    w_up,
    b_up,
    w_down,
    b_down,
    cotangent,
):
    n_dp = lax.axis_size("dp")
    assert tokens.shape == (SHORT, D) and lax.axis_size("tensor") * SHORT == LONG and n_dp % 8 == 0
    scalars = dict(lc=long_count, ts=timesteps)
    blocks = dict(
        tok=tokens,
        cot=cotangent,
        gain=norm_gain,
        bias=norm_bias,
        b_out=b_out,
        b_down=b_down,
        b_time=b_time,
        bup_own=b_up,
        b_qkv=b_qkv,
        w_qkv=jnp.transpose(w_qkv, (0, 2, 1)).reshape(576, D),
        w_time=w_time,
    )
    far = dict(
        wo_own=w_out,
        wu_own=w_up.reshape(3, 256, D),
        wd_own=w_down.reshape(4, 2, 96, D),
    )
    outs = dict(
        result=((256, D), BF),
        gtok=((256, D), F32),
        oqkv=((576, D), BF),
        oo=((192, D), BF),
        ou=((D, D), BF),
        od=((D, D), BF),
        gwt=((TE, 3 * D), F32),
        ggain=((D,), F32),
        gbias=((D,), F32),
        gbqkv=((3, 192), F32),
        gbo=((D,), F32),
        gbt=((3 * D,), F32),
        gbu=((D,), F32),
        gbd=((D,), F32),
    )
    result, grad_tokens, gqkv, gwo, gwu, gwd, gwt, ggain, gbias, gbqkv, gbo, gbt, gbu, gbd = fused(
        scalars, blocks, far, outs
    )
    grads = (
        ggain,
        gbias,
        jnp.transpose(gqkv.reshape(3, 192, D), (0, 2, 1)).astype(F32),
        gbqkv,
        gwo.astype(F32),
        gbo,
        gwt,
        gbt,
        gwu.astype(F32),
        gbu,
        gwd.astype(F32),
        gbd,
    )
    if n_dp > 8:
        groups = [[inner + 8 * outer for outer in range(n_dp // 8)] for inner in range(8)]
        grads = lax.psum(grads, "dp", axis_index_groups=groups)
    return (result, grad_tokens) + tuple(grads)


def solution(mesh):
    rows = P(("dp", "tensor"), None)
    placed = (
        rows,
        P("dp"),
        P("dp"),
        P(),
        P(),
        P(None, None, "tensor"),
        P(None, "tensor"),
        P("tensor", None),
        P(),
        P(),
        P(),
        P(None, "tensor"),
        P("tensor"),
        P("tensor", None),
        P(),
        rows,
    )
    return jax.shard_map(
        on_device,
        mesh=mesh,
        in_specs=placed,
        out_specs=(rows, rows) + placed[3:15],
        check_vma=False,
    )
```

```python
import math
from functools import partial
from itertools import accumulate
from types import SimpleNamespace

import jax
import jax.numpy as jnp
from jax import lax
from jax.experimental import pallas as pl
from jax.experimental.pallas import tpu as pltpu
from jax.sharding import PartitionSpec as P

HEAD = 64
TE = 128
STEPS = 1000
LONG = 1024
SHORT = 256
D = 768
HALF = 384
EPS = 1e-05
TIME_SCALE = 64.0
SCALE = 1.0 / math.sqrt(HEAD)
LOG_BASE = math.log(10000.0)
BF = jnp.bfloat16
F32 = jnp.float32
MESH = pl.DeviceIdType.MESH
HIGHEST = lax.Precision.HIGHEST

SEMS = dict(
    load=6,
    store=9,
    ag_s=16,
    ag_r=8,
    bup_s=4,
    bup_r=4,
    gb_s=4,
    gb_r=4,
    md_s=4,
    md_r=4,
    wz_s=8,
    wz_r=8,
    wx_s=12,
    wx_r=12,
    wc_s=8,
    wc_r=8,
    mix_s=4,
    mix_r=4,
    gmp_s=4,
    gmp_r=4,
    br_s=4,
    br_r=4,
    gm_s=4,
    gm_r=4,
    r1_s=4,
    r1_r=4,
    r2_s=6,
    r2_r=6,
    r3_s=12,
    r3_r=12,
    r4_s=12,
    r4_r=12,
    r5_s=4,
    r5_r=4,
    rs_s=12,
    rs_r=12,
    ez_s=4,
    ez_r=4,
    ed_s=8,
    ed_r=8,
    lz_s=4,
    lz_r=4,
    ld_s=8,
    ld_r=8,
)
COUNT = sum(SEMS.values())
S = SimpleNamespace(**dict(zip(SEMS, accumulate(SEMS.values(), initial=0))))

SCRATCH = dict(
    cot=((256, D), BF),
    w_qkv=((576, D), BF),
    w_time=((TE, 3 * D), F32),
    result=((256, D), BF),
    gtok=((256, D), F32),
    oqkv=((576, D), BF),
    oo=((192, D), BF),
    ou=((D, D), BF),
    od=((D, D), BF),
    gwt=((TE, 3 * D), F32),
    vec=((16, D), F32),
    turn=((2, 256, 128), F32),
    feat=((1, TE), F32),
    modrow=((1, 3 * D), F32),
    normed=((4, 256, D), BF),
    q=((3, 1024, 128), BF),
    k=((3, 1024, 128), BF),
    v=((3, 1024, 128), BF),
    kt=((3, 4, 128, 256), BF),
    vt=((3, 4, 128, 256), BF),
    probs=((3, 4, 1024, 256), BF),
    blocks=((4, 256, 192), BF),
    mixed=((4, 256, 192), BF),
    wo=((4, 192, D), BF),
    w=((2, 4, 2, 96, D), BF),
    bup=((4, 1, D), F32),
    bqkv=((1, 576), F32),
    bupq=((1, D), F32),
    mod=((4, 256, D), BF),
    gb=((4, 256, D), BF),
    act=((4, 256, D), BF),
    gh=((4, 256, D), BF),
    wide=((12, 512, 128), F32),
    gmp_out=((3, 256, D), BF),
    gmp_in=((3, 256, D), BF),
    br_in=((3, 256, D), BF),
    gwo=((2, 4, 4, 48, HALF), BF),
    gw=((2, 4, 2, 96, D), BF),
    resid=((256, D), F32),
    gres=((256, D), F32),
    gm=((4, 256, 192), BF),
    gp=((4, 256, 576), BF),
    gqkv=((2, 4, 144, HALF), BF),
    r1o=((4, 4, 48, HALF), BF),
    r1w=((2, 4, 96, D), BF),
    r1q=((4, 144, HALF), BF),
    r2o=((3, 4, 48, HALF), BF),
    r2q=((3, 144, HALF), BF),
    r3w=((2, 4, 96, D), BF),
    r3o=((4, 48, HALF), BF),
    ow=((2, 4, 2, 96, D), BF),
    rs_out=((3, 256, D), BF),
    rs_in=((2, 3, 256, D), BF),
    small=((8, D), F32),
    zs=((4, 8, D), F32),
    ds=((8, 24, D), F32),
    late=((8, D), F32),
    zl=((4, 8, D), F32),
    dl=((8, 8, D), F32),
    gmat=((4, 32, D), F32),
)


def dot(a, b):
    return jnp.dot(a, b, preferred_element_type=F32)


def dot_nt(a, b):
    return lax.dot_general(a, b, (((1,), (1,)), ((), ())), preferred_element_type=F32)


def dot_tn(a, b, precision=None):
    dims = (((0,), (0,)), ((), ()))
    return lax.dot_general(a, b, dims, precision=precision, preferred_element_type=F32)


def norm_parts(values):
    center = values - jnp.mean(values, axis=-1, keepdims=True)
    rstd = lax.rsqrt(jnp.mean(center * center, axis=-1, keepdims=True) + EPS)
    return center * rstd, rstd


def norm_back(unit, rstd, grad):
    mean_g = jnp.mean(grad, axis=-1, keepdims=True)
    mean_gn = jnp.mean(grad * unit, axis=-1, keepdims=True)
    return (grad - mean_g - unit * mean_gn) * rstd


def total(values):
    return jnp.sum(values, axis=0, keepdims=True)


def row(ref):
    return ref[...].reshape(1, -1)


def pick(index, options):
    chosen = options[-1]
    for n in range(len(options) - 2, -1, -1):
        chosen = jnp.where(index == n, options[n], chosen)
    return chosen


def body(names, *refs):
    sem = refs[-1]
    r = SimpleNamespace(**dict(zip(names, refs[:-1], strict=True)))
    dp = lax.axis_index("dp")
    t = lax.axis_index("tensor")
    mine = lax.rem(dp, 8)
    block = dp - mine
    c = lax.rem(dp, 2)
    q = lax.div(mine, 2)
    other = 1 - c
    sibling = (dp + 1 - 2 * c, t)
    columns = [q, q + 1 - 2 * lax.rem(q, 2), q + 2 - 4 * lax.div(q, 2), 3 - q]

    def column(j):
        return (block + 2 * columns[j] + c, t)

    def zpeer(j):
        return lax.rem(t + j, 4)

    def remote(src, dst, send, recv, device):
        return pltpu.make_async_remote_copy(
            src_ref=src,
            dst_ref=dst,
            send_sem=sem.at[send],
            recv_sem=sem.at[recv],
            device_id=device,
            device_id_type=MESH,
        )

    def got(ref, recv):
        remote(ref, ref, recv, recv, sibling).wait_recv()

    def sent(ref, send):
        remote(ref, ref, send, send, sibling).wait_send()

    def rows(index, size):
        return pl.ds(pl.multiple_of(index * size, size), size)

    def hop(i):
        k = lax.div(i + 1, 2)
        side = 1 - lax.rem(i, 2)
        step = 2 * side - 1
        return k, side, t + step * k, t - step

    def inside(b):
        return (b >= 0) & (b <= 3)

    barrier = pltpu.get_barrier_semaphore()
    for j in range(1, 4):
        pl.semaphore_signal(barrier, inc=1, device_id=(dp, zpeer(j)), device_id_type=MESH)
    for j in range(1, 8):
        peer = block + lax.rem(mine + j, 8)
        pl.semaphore_signal(barrier, inc=1, device_id=(peer, t), device_id_type=MESH)

    loads = [
        pltpu.make_async_copy(r.wo_own, r.wo.at[t], sem.at[S.load]),
        pltpu.make_async_copy(r.wu_own, r.act.at[0:3], sem.at[S.load + 1]),
        pltpu.make_async_copy(r.wd_own.at[q], r.w.at[1, t], sem.at[S.load + 2]),
        pltpu.make_async_copy(r.w_time_far, r.w_time, sem.at[S.load + 3]),
        pltpu.make_async_copy(r.cot_far, r.cot, sem.at[S.load + 4]),
        pltpu.make_async_copy(r.w_qkv_far, r.w_qkv, sem.at[S.load + 5]),
    ]
    for load in loads:
        load.start()
    names_out = [name for name in names if name.startswith("out_")]

    def store(name):
        n = names_out.index("out_" + name)
        copy = pltpu.make_async_copy(getattr(r, name), getattr(r, "out_" + name), sem.at[S.store + n])
        copy.start()
        stores.append(copy)

    stores = []

    unit, _ = norm_parts(r.tok[...].astype(F32))
    r.normed[t] = (unit * row(r.gain) + row(r.bias)).astype(BF)
    r.bup[t] = row(r.bup_own)
    for n in range(3):
        r.bqkv[:, 192 * n : 192 * (n + 1)] = r.b_qkv[n : n + 1, :]
    pl.semaphore_wait(barrier, 10)

    def ag_chunk(b, chunk):
        return r.normed.at[b, 128 * chunk : 128 * (chunk + 1)]

    def ag_copy(b, chunk, side, k, device):
        piece = ag_chunk(b, chunk)
        send = S.ag_s + (side * 4 + k) * 2 + chunk
        return remote(piece, piece, send, S.ag_r + 2 * b + chunk, (dp, device))

    for chunk in range(2):

        @pl.when(t < 3)
        def _():
            ag_copy(t, chunk, 0, 0, t + 1).start()

        @pl.when(t > 0)
        def _():
            ag_copy(t, chunk, 1, 0, t - 1).start()

    def wo_piece(shard, col):
        return r.wo.at[shard, rows(col, 48), rows(c, HALF)]

    def wz_piece(a, shard):
        return wo_piece(shard, q) if a == 0 else r.w.at[:, shard, c]

    def wz_copy(a, j):
        piece = wz_piece(a, t)
        return remote(piece, piece, S.wz_s + a * 4 + j, S.wz_r + a * 4 + t, (dp, zpeer(j)))

    loads[0].wait()
    for j in range(1, 4):
        wz_copy(0, j).start()
    for j in range(1, 4):
        remote(r.bup.at[t], r.bup.at[t], S.bup_s + j, S.bup_r + t, (dp, zpeer(j))).start()

    is_long = r.lc[0]
    slot = (1 - is_long) * t
    step = jnp.int32(0)
    for n in range(4):
        step = step + jnp.where(slot == n, r.ts[n], 0)
    lane = lax.broadcasted_iota(jnp.int32, (1, TE), 1)
    half_lane = lax.rem(lane, TE // 2).astype(F32)
    angle = (step.astype(F32) / STEPS * TIME_SCALE) * jnp.exp(half_lane * (-LOG_BASE / (TE // 2)))
    feat = jnp.where(lane < TE // 2, jnp.cos(angle), jnp.sin(angle))
    r.feat[...] = feat
    wide_feat = jnp.broadcast_to(feat, (8, TE))
    loads[3].wait()
    loads[4].wait()
    modulation = jnp.dot(wide_feat, r.w_time[...], precision=HIGHEST, preferred_element_type=F32)
    r.modrow[...] = modulation[0:1] + row(r.b_time)
    gate = r.modrow[:, 2 * D :]
    r.gb[q] = (gate * r.cot[...].astype(F32)).astype(BF)
    for j in range(1, 4):
        remote(r.gb.at[q], r.gb.at[q], S.gb_s + j, S.gb_r + q, column(j)).start()

    lane = lax.broadcasted_iota(jnp.int32, (1, 128), 1)
    freqs = jnp.exp(lax.rem(lane, 32).astype(F32) * (-LOG_BASE / 32))
    sign = jnp.where(lax.rem(lane, 64) < 32, -1.0, 1.0)
    angles = lax.broadcasted_iota(jnp.int32, (256, 128), 0).astype(F32) * freqs
    r.turn[0] = jnp.cos(angles)
    r.turn[1] = jnp.sin(angles) * sign

    def rope_tables(b):
        offset = (b * 256 * is_long).astype(F32) * freqs
        cosine = jnp.cos(offset)
        sine = jnp.sin(offset) * sign
        return (
            r.turn[0] * cosine - r.turn[1] * sine,
            r.turn[1] * cosine + r.turn[0] * sine,
        )

    loads[1].wait()
    loads[2].wait()
    loads[5].wait()
    for n in range(4):

        @pl.when(q == n)
        def _():
            part = r.act[0:3].reshape(D, D)[:, 192 * n : 192 * (n + 1)]
            r.w[0, t] = part.T.reshape(2, 96, D)

    lower = lax.broadcasted_iota(jnp.int32, (256, 128), 1) < HEAD

    def project(b):
        y = dot_nt(r.normed[b], r.w_qkv[...]) + r.bqkv[...]
        at = rows(b, 256)
        cosine, sine = rope_tables(b)
        doubled = []
        for n in range(3):
            tile = y[:, 128 * n : 128 * (n + 1)]
            swapped = pltpu.roll(tile, HEAD, 1)
            doubled += [jnp.where(lower, tile, swapped), jnp.where(lower, swapped, tile)]
        for h in range(3):
            for part, dest in ((doubled[h], r.q), (doubled[3 + h], r.k)):
                turned = part * cosine + pltpu.roll(part, 32, 1) * sine
                dest[h, at, :] = turned.astype(BF)
            r.kt[h, b] = turned.T.astype(BF)
        tile = y[:, 384:512]
        for h, value in enumerate((jnp.where(lower, tile, 0.0), jnp.where(lower, 0.0, tile))):
            r.v[h, at, :] = value.astype(BF)
            r.vt[h, b] = value.T.astype(BF)
        value = y[:, 512:576]
        r.v[2, at, :HEAD] = value.astype(BF)
        r.vt[2, b, :HEAD, :] = value.T.astype(BF)

    def ag_step(i, carry):
        k, side, b, nxt = hop(i)

        @pl.when(inside(b))
        def _():
            @pl.when(i > 0)
            def _():
                for chunk in range(2):
                    got(ag_chunk(b, chunk), S.ag_r + 2 * b + chunk)

                    @pl.when(inside(nxt))
                    def _():
                        ag_copy(b, chunk, side, k, nxt).start()

            project(b)

        return carry

    lax.fori_loop(0, 7, ag_step, 0)

    for chunk in range(2):

        @pl.when(t < 3)
        def _():
            sent(ag_chunk(t, 0), S.ag_s + chunk)

        @pl.when(t > 0)
        def _():
            sent(ag_chunk(t, 0), S.ag_s + 8 + chunk)

    def ag_sent(i, carry):
        k, side, b, nxt = hop(i)

        @pl.when(inside(b) & inside(nxt))
        def _():
            for chunk in range(2):
                sent(ag_chunk(b, 0), S.ag_s + (side * 4 + k) * 2 + chunk)

        return carry

    lax.fori_loop(1, 7, ag_sent, 0)

    def wx_copy(b, j):
        index = b * 3 + j - 1
        piece = wo_piece(b, q)
        return remote(piece, piece, S.wx_s + index, S.wx_r + index, column(j))

    def wc_copy(a, b):
        piece = r.wo.at[b, :, rows(c, HALF)] if a == 0 else r.w.at[:, b, c]
        return remote(piece, piece, S.wc_s + a * 4 + b, S.wc_r + a * 4 + b, sibling)

    for j in range(1, 4):
        b = zpeer(j)
        got(wz_piece(0, b), S.wz_r + b)
        for col in range(1, 4):
            wx_copy(b, col).start()

    neg = jnp.where(is_long > 0, 0.0, -1e30)

    def attend(i, carry):
        qb = lax.rem(t + 1 + i, 4)
        outs = []
        for h in range(3):
            queries = r.q[h, rows(qb, 256), :]
            parts = []
            for kb in range(4):
                s = dot_nt(r.k[h, kb * 256 : (kb + 1) * 256, :], queries) * (0.5 * SCALE)
                parts.append(s + jnp.where(qb == kb, 0.0, neg))
            top = parts[0].max(axis=0, keepdims=True)
            for kb in range(1, 4):
                top = jnp.maximum(top, parts[kb].max(axis=0, keepdims=True))
            parts = [jnp.exp(s - top) for s in parts]
            inverse = 1.0 / sum(total(s) for s in parts)
            out = None
            for kb in range(4):
                p = (parts[kb] * inverse).astype(BF)
                r.probs[h, qb, kb * 256 : (kb + 1) * 256, :] = p
                term = dot(r.vt[h, kb] if h < 2 else r.vt[h, kb, :HEAD, :], p)
                out = term if out is None else out + term
            outs.append(out)
        low, high = (outs[0] + outs[1]).T.astype(BF), outs[2].T.astype(BF)

        @pl.when(i < 3)
        def _():
            r.blocks[qb, :, :128] = low
            r.blocks[qb, :, 128:192] = high
            remote(r.blocks.at[qb], r.mixed.at[t], S.mix_s + i, S.mix_r + t, (dp, qb)).start()

        @pl.when(i == 3)
        def _():
            r.mixed[t, :, :128] = low
            r.mixed[t, :, 128:192] = high

        return carry

    lax.fori_loop(0, 4, attend, 0)
    for j in range(1, 4):
        wz_copy(1, j).start()

    for j in range(1, 4):
        got(r.bup.at[zpeer(j)], S.bup_r + zpeer(j))
    for s in range(4):
        options = [r.bup[s, :, 192 * n : 192 * (n + 1)] for n in range(4)]
        r.bupq[:, 192 * s : 192 * (s + 1)] = pick(q, options)

    for j in range(1, 4):
        b = zpeer(j)
        for col in range(1, 4):
            got(wo_piece(b, columns[col]), S.wx_r + b * 3 + col - 1)
        wc_copy(0, b).start()
    for j in range(1, 4):
        got(r.wo.at[zpeer(j), :, rows(other, HALF)], S.wc_r + zpeer(j))
    for j in range(1, 4):
        got(r.mixed.at[zpeer(j)], S.mix_r + zpeer(j))

    attended = jnp.broadcast_to(row(r.b_out), (256, D))
    for g in range(4):
        attended = attended + dot(r.mixed[g], r.wo[g])
    resid = r.tok[...].astype(F32) + attended
    r.resid[...] = resid
    unit2, rstd2 = norm_parts(resid)
    scale1 = 1.0 + r.modrow[:, :D]
    r.mod[q] = (unit2 * scale1 + r.modrow[:, D : 2 * D]).astype(BF)
    for j in range(1, 4):
        remote(r.mod.at[q], r.mod.at[q], S.md_s + j, S.md_r + q, column(j)).start()
    for j in range(1, 4):
        b = zpeer(j)
        got(wz_piece(1, b), S.wz_r + 4 + b)
        wc_copy(1, b).start()
    for j in range(1, 4):
        got(r.w.at[:, zpeer(j), other], S.wc_r + 4 + zpeer(j))

    def forward(j, carry):
        col = pick(j, columns)

        @pl.when(j > 0)
        def _():
            got(r.gb.at[col], S.gb_r + col)
            got(r.mod.at[col], S.md_r + col)

        w_up = r.w[0].reshape(D, D)
        hidden = dot_nt(r.mod[col], w_up) + r.bupq[...]
        inner = math.sqrt(2.0 / math.pi)
        square = hidden * hidden
        th = jnp.tanh(inner * hidden * (1.0 + 0.044715 * square))
        halfsum = 0.5 * (1.0 + th)
        r.act[col] = (hidden * halfsum).astype(BF)
        slope = halfsum + 0.5 * hidden * (1.0 - th * th) * (inner * (1.0 + 3 * 0.044715 * square))
        grad_active = dot_nt(r.gb[col], r.w[1].reshape(D, D))
        gh = (slope * grad_active).astype(BF)
        r.gh[col] = gh
        grad_mod = dot(gh, w_up)

        @pl.when(j == 0)
        def _():
            r.gres[...] = grad_mod

        @pl.when(j > 0)
        def _():
            r.gmp_out[j - 1] = grad_mod.astype(BF)
            device = (block + 2 * col + c, t)
            remote(r.gmp_out.at[j - 1], r.gmp_in.at[j - 1], S.gmp_s + j, S.gmp_r + j, device).start()

        return carry

    lax.fori_loop(0, 4, forward, 0)

    def r2_copy(a, j):
        col = columns[j]
        src = r.gwo.at[c, :, col] if a == 0 else r.gqkv.at[c, col]
        dst = (r.r2o, r.r2q)[a].at[j - 1]
        return remote(src, dst, S.r2_s + a * 3 + j - 1, S.r2_r + a * 3 + j - 1, column(j))

    def r3_piece(a, shard):
        return r.gwo.at[c, shard, q] if a == 0 else r.gw.at[a - 1, shard, c]

    def r3_copy(a, j):
        goal = zpeer(j)
        dst = r.r3o.at[t] if a == 0 else r.r3w.at[a - 1, t]
        return remote(
            r3_piece(a, goal), dst, S.r3_s + a * 4 + j, S.r3_r + a * 4 + t, (dp, goal)
        )

    def out_piece(a, col):
        if a == 0:
            return r.oo.at[rows(col, 48), rows(c, HALF)]
        if a < 3:
            return r.ow.at[a - 1, col, c]
        return r.oqkv.at[rows(col, 144), rows(c, HALF)]

    def r4_copy(a, j):
        piece = out_piece(a, q)
        index = a * 3 + j - 1
        return remote(piece, piece, S.r4_s + index, S.r4_r + index, column(j))

    def half_out(a, who):
        if a == 0:
            return r.oo.at[:, rows(who, HALF)]
        if a < 3:
            return r.ow.at[a - 1, :, who]
        return r.oqkv.at[:, rows(who, HALF)]

    def r5_copy(a):
        piece = half_out(a, c)
        return remote(piece, piece, S.r5_s + a, S.r5_r + a, sibling)

    def r1_copy_w(a):
        return remote(r.gw.at[a, :, other], r.r1w.at[a], S.r1_s + a, S.r1_r + a, sibling)

    def r1_sum_w(a):
        got(r.r1w.at[a], S.r1_r + a)
        r.gw[a, :, c] = (r.gw[a, :, c].astype(F32) + r.r1w[a].astype(F32)).astype(BF)

    def r3_start(a):
        for j in range(1, 4):
            r3_copy(a, j).start()

    def r1_sum_o():
        got(r.r1o, S.r1_r + 2)
        r.gwo[c] = (r.gwo[c].astype(F32) + r.r1o[...].astype(F32)).astype(BF)
        for j in range(1, 4):
            r2_copy(0, j).start()

    def r2_sum(a):
        for j in range(1, 4):
            copy = r2_copy(a, j)
            copy.wait_recv()
            copy.wait_send()
        mine_ref = r.gwo.at[c, :, q] if a == 0 else r.gqkv.at[c, q]
        theirs = (r.r2o, r.r2q)[a]
        acc = mine_ref[...].astype(F32)
        for j in range(3):
            acc = acc + theirs[j].astype(F32)
        if a == 0:
            mine_ref[...] = acc.astype(BF)
            r3_start(0)
        else:
            out_piece(3, q)[...] = acc.astype(BF)
            for j in range(1, 4):
                r4_copy(3, j).start()

    def r3_sum(a):
        buf = r.r3o if a == 0 else r.r3w.at[a - 1]
        acc = r3_piece(a, t)[...].astype(F32)
        for j in range(1, 4):
            got(buf.at[zpeer(j)], S.r3_r + a * 4 + zpeer(j))
            acc = acc + buf[zpeer(j)].astype(F32)
        out_piece(a, q)[...] = acc.astype(BF)
        for j in range(1, 4):
            r4_copy(a, j).start()

    def r4_wait(a):
        for j in range(1, 4):
            got(out_piece(a, columns[j]), S.r4_r + a * 3 + j - 1)
        r5_copy(a).start()

    def weight_grad(a):
        left = (r.gh, r.act)[a][...].reshape(1024, D)
        right = (r.mod, r.gb)[a][...].reshape(1024, D)
        for s in range(4):
            grad = dot_tn(left[:, 192 * s : 192 * (s + 1)], right)
            r.gw[a, s] = grad.astype(BF).reshape(2, 96, D)

    for a in (1, 0):
        weight_grad(a)
        r1_copy_w(a).start()
    r1_sum_w(1)
    r3_start(2)
    r1_sum_w(0)

    grad_mod = r.gres[...]
    for j in range(1, 4):
        got(r.gmp_in.at[j - 1], S.gmp_r + j)
        grad_mod = grad_mod + r.gmp_in[j - 1].astype(F32)
    unit2, rstd2 = norm_parts(r.resid[...])
    scale1 = 1.0 + r.modrow[:, :D]
    grad_resid = r.cot[...].astype(F32) + norm_back(unit2, rstd2, grad_mod * scale1)
    r.gres[...] = grad_resid
    grad_att = grad_resid.astype(BF)
    for i in range(3):
        sent(r.blocks.at[0], S.mix_s + i)
    for i in range(1, 4):
        g = lax.rem(t + i, 4)
        r.blocks[g] = dot_nt(grad_att, r.wo[g]).astype(BF)
        remote(r.blocks.at[g], r.gm.at[t], S.gm_s + i, S.gm_r + t, (dp, g)).start()
    r.gm[t] = dot_nt(grad_att, r.wo[t]).astype(BF)
    r.small[0:1, :] = total(grad_mod * unit2)
    r.small[1:2, :] = total(grad_mod)
    r.small[3:4, :] = jnp.zeros((1, D), F32)
    r.small[3:4, :TE] = r.feat[...]
    r.small[4:5, :] = total(grad_att.astype(F32))
    r.small[5:6, :] = total(r.gb[q].astype(F32))
    r.small[6:7, :] = total(r.gh[...].reshape(1024, D).astype(F32))
    r.small[7:8, :] = jnp.zeros((1, D), F32)
    for g in range(4):
        grad = dot_tn(r.mixed[g], grad_att).astype(BF)
        for half in range(2):
            r.gwo[half, g] = grad[:, HALF * half : HALF * (half + 1)].reshape(4, 48, HALF)
    remote(r.gwo.at[other], r.r1o, S.r1_s + 2, S.r1_r + 2, sibling).start()
    for j in range(1, 4):
        sent(r.gmp_out.at[j - 1], S.gmp_s + j)

    def down(n, carry):
        j = lax.rem(n + 1, 4)
        col = pick(j, columns)
        branch = dot(r.act[col], r.w[1].reshape(D, D))

        @pl.when(j == 0)
        def _():
            r.gtok[...] = branch

        @pl.when(j > 0)
        def _():
            r.gmp_out[j - 1] = branch.astype(BF)
            device = (block + 2 * col + c, t)
            remote(r.gmp_out.at[j - 1], r.br_in.at[j - 1], S.br_s + j, S.br_r + j, device).start()

        return carry

    lax.fori_loop(0, 4, down, 0)


    r1_sum_o()

    r.wide[...] = jnp.zeros((12, 512, 128), F32)

    def attend_back(i, carry):
        qb = lax.rem(t + i, 4)

        @pl.when(i > 0)
        def _():
            got(r.gm.at[qb], S.gm_r + qb)

        @pl.when(i == 3)
        def _():
            r3_start(1)

        at = rows(qb, 256)
        cosine, sine = rope_tables(qb)
        for h in range(3):
            width = 128 if h < 2 else HEAD
            grad_out = r.gm[qb, :, :128] if h < 2 else r.gm[qb, :, 128:192]
            queries = r.q[h, at, :]
            probs = []
            grads = []
            inner = None
            for kb in range(4):
                keys = slice(kb * 256, (kb + 1) * 256)
                p = r.probs[h, qb, keys, :]
                g = dot_nt(r.v[h, keys, :width], grad_out)
                term = total(g * p.astype(F32))
                inner = term if inner is None else inner + term
                probs.append(p)
                grads.append(g)
                place = slice(256 * (kb % 2), 256 * (kb % 2 + 1))
                r.wide[6 + 2 * h + kb // 2, place, :width] += dot(p, grad_out)
            grad_q = None
            for kb in range(4):
                ds = (probs[kb].astype(F32) * (grads[kb] - inner)).astype(BF)
                place = slice(256 * (kb % 2), 256 * (kb % 2 + 1))
                r.wide[2 * h + kb // 2, place, :] += dot(ds, queries)
                term = dot(r.kt[h, kb], ds)
                grad_q = term if grad_q is None else grad_q + term
            grad_q = grad_q.T * SCALE
            turned = grad_q * cosine - pltpu.roll(grad_q, 32, 1) * sine
            if h == 0:
                first_q = turned
            elif h == 1:
                r.gp[qb, :, :128] = jnp.where(lower, first_q, turned).astype(BF)
            else:
                r.gp[qb, :, 128:256] = turned.astype(BF)
        return carry

    lax.fori_loop(0, 4, attend_back, 0)

    def finish(b, carry):
        cosine, sine = rope_tables(b)
        keys = []
        half = rows(lax.rem(b, 2), 256)
        place = lax.div(b, 2)
        for h in range(3):
            grad = r.wide[2 * h + place, half, :] * SCALE
            keys.append(grad * cosine - pltpu.roll(grad, 32, 1) * sine)
        values = [r.wide[6 + 2 * h + place, half, :] for h in range(3)]
        last_q = r.gp[b, :, 128:256].astype(F32)
        r.gp[b, :, 128:256] = jnp.where(lower, last_q, keys[0]).astype(BF)
        r.gp[b, :, 256:384] = jnp.where(lower, keys[1], keys[2]).astype(BF)
        r.gp[b, :, 384:512] = jnp.where(lower, values[0], values[1]).astype(BF)
        r.gp[b, :, 512:576] = values[2][:, :HEAD].astype(BF)
        return carry

    lax.fori_loop(0, 4, finish, 0)

    def rs_step(k):
        for side in range(2):
            step = 1 - 2 * side
            goal = t + step * (4 - k)
            nxt = t + step
            prev = t - step
            slot = 3 - k if side else k - 1

            @pl.when(inside(goal))
            def _():
                for chunk in range(2):
                    at = slice(128 * chunk, 128 * (chunk + 1))
                    part = dot(r.gp[goal, at, :], r.w_qkv[...])
                    r.rs_out[slot, at, :] = part.astype(BF)
                    if k > 1:

                        @pl.when(inside(prev))
                        def _():
                            index = (side * 3 + k - 2) * 2 + chunk
                            got(r.rs_in.at[side, k - 2, at], S.rs_r + index)
                            summed = part + r.rs_in[side, k - 2, at, :].astype(F32)
                            r.rs_out[slot, at, :] = summed.astype(BF)

                    index = (side * 3 + k - 1) * 2 + chunk
                    remote(
                        r.rs_out.at[slot, at],
                        r.rs_in.at[side, k - 1, at],
                        S.rs_s + index,
                        S.rs_r + index,
                        (dp, nxt),
                    ).start()

    rs_step(1)
    r2_sum(0)

    branch = r.gtok[...] + row(r.b_down)
    for j in range(1, 4):
        got(r.br_in.at[j - 1], S.br_r + j)
        branch = branch + r.br_in[j - 1].astype(F32)
    r.result[...] = (r.resid[...] + r.modrow[:, 2 * D :] * branch).astype(BF)
    store("result")
    r.small[2:3, :] = total(r.cot[...].astype(F32) * branch)
    r.zs[t] = r.small[...]
    for j in range(1, 4):
        remote(r.small, r.zs.at[t], S.ez_s + j, S.ez_r + t, (dp, zpeer(j))).start()

    grad_w = dot_tn(r.gp[...].reshape(1024, 576), r.normed[...].reshape(1024, D)).astype(BF)
    for half in range(2):
        lanes = slice(HALF * half, HALF * (half + 1))
        r.gqkv[half] = grad_w[:, lanes].reshape(4, 144, HALF)
    r3_sum(2)
    remote(r.gqkv.at[other], r.r1q, S.r1_s + 3, S.r1_r + 3, sibling).start()
    r.late[...] = jnp.zeros((8, D), F32)
    r.late[2:3, :576] = total(r.gp[...].reshape(1024, 576).astype(F32))
    got(r.r1q, S.r1_r + 3)
    r.gqkv[c] = (r.gqkv[c].astype(F32) + r.r1q[...].astype(F32)).astype(BF)
    for j in range(1, 4):
        r2_copy(1, j).start()
    rs_step(2)

    for j in range(1, 4):
        got(r.zs.at[zpeer(j)], S.ez_r + zpeer(j))
    for z in range(4):
        for n in range(4):
            r.ds[mine, 4 * n + z : 4 * n + z + 1, :] = r.zs[z, n : n + 1, :]
    r.ds[mine, 16:20, :] = r.zs[0, 4:8, :] + r.zs[1, 4:8, :] + r.zs[2, 4:8, :] + r.zs[3, 4:8, :]
    r.ds[mine, 20:24, :] = jnp.zeros((4, D), F32)
    for j in range(1, 8):
        peer = lax.rem(mine + j, 8)
        remote(
            r.ds.at[mine], r.ds.at[mine], S.ed_s + j, S.ed_r + mine, (block + peer, t)
        ).start()
    rs_step(3)
    own = dot(r.gp[t], r.w_qkv[...])
    r2_sum(1)
    r3_sum(1)
    r3_sum(0)

    for side in range(2):
        prev = t - (1 - 2 * side)

        @pl.when(inside(prev))
        def _():
            for chunk in range(2):
                at = slice(128 * chunk, 128 * (chunk + 1))
                got(r.rs_in.at[side, 2, at], S.rs_r + (side * 3 + 2) * 2 + chunk)

        @pl.when((prev < 0) | (prev > 3))
        def _():
            r.rs_in[side, 2] = jnp.zeros((256, D), BF)

    grad_normed = own + r.rs_in[0, 2].astype(F32) + r.rs_in[1, 2].astype(F32)
    unit1, rstd1 = norm_parts(r.tok[...].astype(F32))
    r.late[0:1, :] = total(grad_normed * unit1)
    r.late[1:2, :] = total(grad_normed)
    r.zl[t] = r.late[...]
    for j in range(1, 4):
        remote(r.late, r.zl.at[t], S.lz_s + j, S.lz_r + t, (dp, zpeer(j))).start()
    r.gtok[...] = r.gres[...] + norm_back(unit1, rstd1, grad_normed * row(r.gain))
    store("gtok")

    for a in (2, 3, 1, 0):
        r4_wait(a)
    for j in range(1, 4):
        got(r.zl.at[zpeer(j)], S.lz_r + zpeer(j))
    r.dl[mine] = r.zl[0] + r.zl[1] + r.zl[2] + r.zl[3]
    r.dl[mine, 2:3, :] = r.late[2:3, :]
    for j in range(1, 8):
        peer = lax.rem(mine + j, 8)
        remote(
            r.dl.at[mine], r.dl.at[mine], S.ld_s + j, S.ld_r + mine, (block + peer, t)
        ).start()
    for j in range(1, 8):
        peer = lax.rem(mine + j, 8)
        got(r.ds.at[peer], S.ed_r + peer)
    for peer in range(8):
        for n in range(4):
            r.gmat[n, 4 * peer : 4 * peer + 4, :] = r.ds[peer, 4 * n : 4 * n + 4, :]
    for n in range(3):
        r.gwt[:, D * n : D * (n + 1)] = dot_tn(r.gmat[3][:, :TE], r.gmat[n], HIGHEST)
        r.vec[4 + n : 5 + n, :] = total(r.gmat[n])
    r.vec[2:4, :] = sum(r.ds[peer, 16:18, :] for peer in range(8))
    for n in range(4):
        units = r.ds[2 * n, 18:19, :] + r.ds[2 * n + 1, 18:19, :]
        options = [units[:, 192 * s : 192 * (s + 1)] for s in range(4)]
        r.vec[7:8, 192 * n : 192 * (n + 1)] = pick(t, options)
    store("gwt")
    for a in (2, 3, 1, 0):
        got(half_out(a, other), S.r5_r + a)
    store("oqkv")
    store("oo")
    r.od[...] = r.ow[1].reshape(D, D)
    store("od")
    r.ou[...] = r.ow[0].reshape(D, D).T
    store("ou")
    for j in range(1, 8):
        peer = lax.rem(mine + j, 8)
        got(r.dl.at[peer], S.ld_r + peer)
    last = sum(r.dl[peer, 0:3, :] for peer in range(8))
    r.vec[0:2, :] = last[0:2]
    r.vec[8:9, :] = last[2:3]
    store("vec")

    for j in range(1, 4):
        sent(r.bup.at[t], S.bup_s + j)
        sent(r.small, S.ez_s + j)
        sent(r.late, S.lz_s + j)
        sent(r.blocks.at[0], S.gm_s + j)
        for base in (S.gb_s, S.md_s, S.br_s):
            sent(r.gb.at[0], base + j)
        for a in range(3):
            sent(r3_piece(a, t), S.r3_s + a * 4 + j)
        for a in range(2):
            sent(wz_piece(a, t), S.wz_s + a * 4 + j)
        b = zpeer(j)
        sent(r.wo.at[b, :, rows(c, HALF)], S.wc_s + b)
        sent(wz_piece(1, b), S.wc_s + 4 + b)
        for col in range(1, 4):
            sent(wo_piece(b, q), S.wx_s + b * 3 + col - 1)
    for a in range(2):
        sent(r.r1w.at[a], S.r1_s + a)
    sent(r.r1o, S.r1_s + 2)
    sent(r.r1q, S.r1_s + 3)
    for j in range(1, 8):
        sent(r.ds.at[mine], S.ed_s + j)
        sent(r.dl.at[mine], S.ld_s + j)
    for a in range(4):
        sent(half_out(a, c), S.r5_s + a)
        for j in range(1, 4):
            sent(out_piece(a, q), S.r4_s + a * 3 + j - 1)

    for k in range(1, 4):
        for side in range(2):
            goal = t + (1 - 2 * side) * (4 - k)

            @pl.when(inside(goal))
            def _():
                for chunk in range(2):
                    sent(r.rs_out.at[0, 0:128], S.rs_s + (side * 3 + k - 1) * 2 + chunk)
    for copy in stores:
        copy.wait()


def fused(scalars, blocks, far, outs):
    vmem = pl.BlockSpec(memory_space=pltpu.VMEM)
    smem = pl.BlockSpec(memory_space=pltpu.SMEM)
    anywhere = pl.BlockSpec(memory_space=pl.ANY)
    operands = scalars | blocks | far
    return pl.pallas_call(
        partial(body, [*operands, *outs, *SCRATCH]),
        out_shape=[jax.ShapeDtypeStruct(shape, kind) for shape, kind in outs.values()],
        in_specs=[smem] * len(scalars) + [vmem] * len(blocks) + [anywhere] * len(far),
        out_specs=[anywhere] * len(outs),
        scratch_shapes=[pltpu.VMEM(shape, kind) for shape, kind in SCRATCH.values()]
        + [pltpu.SemaphoreType.DMA((COUNT,))],
        compiler_params=pltpu.CompilerParams(
            collective_id=0, has_side_effects=True, vmem_limit_bytes=63 << 20
        ),
        name="layer",
    )(*operands.values())


def widen_body(result, gtok, oqkv, oo, ou, od, gwt, vec, *outs):
    for src, dst in zip((result, gtok, oqkv, gwt, oo, ou, od), outs[:7], strict=True):
        dst[...] = src[...].astype(dst.dtype)
    ggain, gbias, gbqkv, gbo, gbt, gbu, gbd = outs[7:]
    for n, dst in ((0, ggain), (1, gbias), (2, gbo), (3, gbd), (7, gbu)):
        dst[...] = vec[n : n + 1, :].reshape(D)
    for n in range(3):
        gbt[D * n : D * (n + 1)] = vec[4 + n : 5 + n, :].reshape(D)
        gbqkv[n : n + 1, :] = vec[8:9, 192 * n : 192 * (n + 1)]


def widen(parts):
    vmem = pl.BlockSpec(memory_space=pltpu.VMEM)
    outs = (
        ((256, D), BF),
        ((256, D), F32),
        ((576, D), F32),
        ((TE, 3 * D), F32),
        ((192, D), F32),
        ((D, D), F32),
        ((D, D), F32),
        ((D,), F32),
        ((D,), F32),
        ((3, 192), F32),
        ((D,), F32),
        ((3 * D,), F32),
        ((D,), F32),
        ((D,), F32),
    )
    return pl.pallas_call(
        widen_body,
        out_shape=[jax.ShapeDtypeStruct(shape, kind) for shape, kind in outs],
        in_specs=[vmem] * 8,
        out_specs=[vmem] * 14,
        compiler_params=pltpu.CompilerParams(vmem_limit_bytes=62 << 20),
        name="widen",
    )(*parts)


def on_device(
    tokens,
    long_count,
    timesteps,
    norm_gain,
    norm_bias,
    w_qkv,
    b_qkv,
    w_out,
    b_out,
    w_time,
    b_time,
    w_up,
    b_up,
    w_down,
    b_down,
    cotangent,
):
    n_dp = lax.axis_size("dp")
    assert tokens.shape == (SHORT, D) and lax.axis_size("tensor") * SHORT == LONG and n_dp % 8 == 0
    scalars = dict(lc=long_count, ts=timesteps)
    blocks = dict(
        tok=tokens,
        gain=norm_gain,
        bias=norm_bias,
        b_out=b_out,
        b_down=b_down,
        b_time=b_time,
        bup_own=b_up,
        b_qkv=b_qkv,
    )
    far = dict(
        wo_own=w_out,
        wu_own=w_up.reshape(3, 256, D),
        wd_own=w_down.reshape(4, 2, 96, D),
        w_time_far=w_time,
        cot_far=cotangent,
        w_qkv_far=jnp.transpose(w_qkv, (0, 2, 1)).reshape(576, D),
    )
    outs = dict(
        out_result=((256, D), BF),
        out_gtok=((256, D), F32),
        out_oqkv=((576, D), BF),
        out_oo=((192, D), BF),
        out_ou=((D, D), BF),
        out_od=((D, D), BF),
        out_gwt=((TE, 3 * D), F32),
        out_vec=((16, D), F32),
    )
    result, grad_tokens, gqkv, gwt, *rest = widen(fused(scalars, blocks, far, outs))
    gwo, gwu, gwd, ggain, gbias, gbqkv, gbo, gbt, gbu, gbd = rest
    grads = (
        ggain,
        gbias,
        jnp.transpose(gqkv.reshape(3, 192, D), (0, 2, 1)),
        gbqkv,
        gwo,
        gbo,
        gwt,
        gbt,
        gwu,
        gbu,
        gwd,
        gbd,
    )
    if n_dp > 8:
        groups = [[inner + 8 * outer for outer in range(n_dp // 8)] for inner in range(8)]
        grads = lax.psum(grads, "dp", axis_index_groups=groups)
    return (result, grad_tokens) + tuple(grads)


def solution(mesh):
    rows = P(("dp", "tensor"), None)
    placed = (
        rows,
        P("dp"),
        P("dp"),
        P(),
        P(),
        P(None, None, "tensor"),
        P(None, "tensor"),
        P("tensor", None),
        P(),
        P(),
        P(),
        P(None, "tensor"),
        P("tensor"),
        P("tensor", None),
        P(),
        rows,
    )
    return jax.shard_map(
        on_device,
        mesh=mesh,
        in_specs=placed,
        out_specs=(rows, rows) + placed[3:15],
        check_vma=False,
    )
```

```python
import math
from functools import partial
from itertools import accumulate
from types import SimpleNamespace

import jax
import jax.numpy as jnp
from jax import lax
from jax.experimental import pallas as pl
from jax.experimental.pallas import tpu as pltpu
from jax.sharding import PartitionSpec as P

HEAD = 64
TE = 128
STEPS = 1000
LONG = 1024
SHORT = 256
D = 768
HALF = 384
EPS = 1e-05
TIME_SCALE = 64.0
SCALE = 1.0 / math.sqrt(HEAD)
LOG_BASE = math.log(10000.0)
BF = jnp.bfloat16
F32 = jnp.float32
MESH = pl.DeviceIdType.MESH
HIGHEST = lax.Precision.HIGHEST

SEMS = dict(
    load=7,
    store=9,
    ag_s=16,
    ag_r=8,
    bup_s=4,
    bup_r=4,
    gb_s=4,
    gb_r=4,
    md_s=4,
    md_r=4,
    wz_s=12,
    wz_r=8,
    wx_s=12,
    wx_r=12,
    wc_s=8,
    wc_r=8,
    mix_s=4,
    mix_r=4,
    gmp_s=4,
    gmp_r=4,
    br_s=4,
    br_r=4,
    gm_s=4,
    gm_r=4,
    r1_s=4,
    r1_r=4,
    r2_s=6,
    r2_r=6,
    r3_s=12,
    r3_r=12,
    r4_s=12,
    r4_r=12,
    r5_s=4,
    r5_r=4,
    rs_s=12,
    rs_r=12,
    ez_s=4,
    ez_r=4,
    ed_s=8,
    ed_r=8,
    lz_s=4,
    lz_r=4,
    ld_s=8,
    ld_r=8,
)
COUNT = sum(SEMS.values())
S = SimpleNamespace(**dict(zip(SEMS, accumulate(SEMS.values(), initial=0))))

SCRATCH = dict(
    cot=((256, D), BF),
    w_qkv=((576, D), BF),
    w_time=((TE, 3 * D), F32),
    result=((256, D), BF),
    gtok=((256, D), F32),
    oqkv=((576, D), BF),
    oo=((192, D), BF),
    ou=((D, D), BF),
    od=((D, D), BF),
    gwt=((TE, 3 * D), F32),
    vec=((16, D), F32),
    turn=((2, 256, 128), F32),
    feat=((1, TE), F32),
    modrow=((1, 3 * D), F32),
    toks=((4, 256, D), BF),
    q=((3, 1024, 128), BF),
    k=((3, 1024, 128), BF),
    v=((3, 1024, 128), BF),
    kt=((3, 4, 128, 256), BF),
    vt=((3, 4, 128, 256), BF),
    probs=((3, 4, 1024, 256), BF),
    blocks=((4, 256, 192), BF),
    mixed=((4, 256, 192), BF),
    wo=((4, 192, D), BF),
    w=((2, 4, 2, 96, D), BF),
    bup=((4, 1, D), F32),
    bqkv=((1, 576), F32),
    bupq=((1, D), F32),
    mod=((4, 256, D), BF),
    gb=((4, 256, D), BF),
    act=((4, 256, D), BF),
    gh=((4, 256, D), BF),
    wide=((12, 512, 128), F32),
    gmp_out=((3, 256, D), BF),
    gmp_in=((3, 256, D), BF),
    br_in=((3, 256, D), BF),
    gwo=((2, 4, 4, 48, HALF), BF),
    gw=((2, 4, 2, 96, D), BF),
    resid=((256, D), F32),
    gres=((256, D), F32),
    gm=((4, 256, 192), BF),
    gp=((4, 256, 576), BF),
    gqkv=((2, 4, 144, HALF), BF),
    r1o=((4, 4, 48, HALF), BF),
    r1w=((2, 4, 96, D), BF),
    r1q=((4, 144, HALF), BF),
    r2o=((3, 4, 48, HALF), BF),
    r2q=((3, 144, HALF), BF),
    r3w=((2, 4, 96, D), BF),
    r3o=((4, 48, HALF), BF),
    ow=((2, 4, 2, 96, D), BF),
    rs_out=((3, 256, D), BF),
    rs_in=((2, 3, 256, D), BF),
    small=((8, D), F32),
    zs=((4, 8, D), F32),
    ds=((8, 24, D), F32),
    late=((8, D), F32),
    zl=((4, 8, D), F32),
    dl=((8, 8, D), F32),
    gmat=((4, 32, D), F32),
)


def dot(a, b):
    return jnp.dot(a, b, preferred_element_type=F32)


def dot_nt(a, b):
    return lax.dot_general(a, b, (((1,), (1,)), ((), ())), preferred_element_type=F32)


def dot_tn(a, b, precision=None):
    dims = (((0,), (0,)), ((), ()))
    return lax.dot_general(a, b, dims, precision=precision, preferred_element_type=F32)


def norm_parts(values):
    center = values - jnp.mean(values, axis=-1, keepdims=True)
    rstd = lax.rsqrt(jnp.mean(center * center, axis=-1, keepdims=True) + EPS)
    return center * rstd, rstd


def norm_back(unit, rstd, grad):
    mean_g = jnp.mean(grad, axis=-1, keepdims=True)
    mean_gn = jnp.mean(grad * unit, axis=-1, keepdims=True)
    return (grad - mean_g - unit * mean_gn) * rstd


def total(values):
    return jnp.sum(values, axis=0, keepdims=True)


def row(ref):
    return ref[...].reshape(1, -1)


def pick(index, options):
    chosen = options[-1]
    for n in range(len(options) - 2, -1, -1):
        chosen = jnp.where(index == n, options[n], chosen)
    return chosen


def body(names, *refs):
    sem = refs[-1]
    r = SimpleNamespace(**dict(zip(names, refs[:-1], strict=True)))
    dp = lax.axis_index("dp")
    t = lax.axis_index("tensor")
    mine = lax.rem(dp, 8)
    block = dp - mine
    c = lax.rem(dp, 2)
    q = lax.div(mine, 2)
    other = 1 - c
    sibling = (dp + 1 - 2 * c, t)
    columns = [q, q + 1 - 2 * lax.rem(q, 2), q + 2 - 4 * lax.div(q, 2), 3 - q]

    def column(j):
        return (block + 2 * columns[j] + c, t)

    def zpeer(j):
        return lax.rem(t + j, 4)

    def remote(src, dst, send, recv, device):
        return pltpu.make_async_remote_copy(
            src_ref=src,
            dst_ref=dst,
            send_sem=sem.at[send],
            recv_sem=sem.at[recv],
            device_id=device,
            device_id_type=MESH,
        )

    def got(ref, recv):
        remote(ref, ref, recv, recv, sibling).wait_recv()

    def sent(ref, send):
        remote(ref, ref, send, send, sibling).wait_send()

    def rows(index, size):
        return pl.ds(pl.multiple_of(index * size, size), size)

    def hop(i):
        k = lax.div(i + 1, 2)
        side = 1 - lax.rem(i, 2)
        step = 2 * side - 1
        return k, side, t + step * k, t - step

    def inside(b):
        return (b >= 0) & (b <= 3)

    barrier = pltpu.get_barrier_semaphore()
    for j in range(1, 4):
        pl.semaphore_signal(barrier, inc=1, device_id=(dp, zpeer(j)), device_id_type=MESH)
    for j in range(1, 8):
        peer = block + lax.rem(mine + j, 8)
        pl.semaphore_signal(barrier, inc=1, device_id=(peer, t), device_id_type=MESH)

    loads = [
        pltpu.make_async_copy(r.wo_own, r.wo.at[t], sem.at[S.load]),
        pltpu.make_async_copy(r.wu_own, r.act.at[0:3], sem.at[S.load + 1]),
        pltpu.make_async_copy(r.wd_own.at[q], r.w.at[1, t], sem.at[S.load + 2]),
        pltpu.make_async_copy(r.w_time_far, r.w_time, sem.at[S.load + 3]),
        pltpu.make_async_copy(r.cot_far, r.cot, sem.at[S.load + 4]),
        pltpu.make_async_copy(r.w_qkv_far, r.w_qkv, sem.at[S.load + 5]),
        pltpu.make_async_copy(r.tok_far, r.toks.at[t], sem.at[S.load + 6]),
    ]
    for load in reversed(loads):
        load.start()
    names_out = [name for name in names if name.startswith("out_")]

    def store(name):
        n = names_out.index("out_" + name)
        copy = pltpu.make_async_copy(getattr(r, name), getattr(r, "out_" + name), sem.at[S.store + n])
        copy.start()
        stores.append(copy)

    stores = []

    r.bup[t] = row(r.bup_own)
    for n in range(3):
        r.bqkv[:, 192 * n : 192 * (n + 1)] = r.b_qkv[n : n + 1, :]
    loads[6].wait()
    pl.semaphore_wait(barrier, 10)

    def ag_chunk(b, chunk):
        return r.toks.at[b, 128 * chunk : 128 * (chunk + 1)]

    def ag_copy(b, chunk, side, k, device):
        piece = ag_chunk(b, chunk)
        send = S.ag_s + (side * 4 + k) * 2 + chunk
        return remote(piece, piece, send, S.ag_r + 2 * b + chunk, (dp, device))

    for chunk in range(2):

        @pl.when(t < 3)
        def _():
            ag_copy(t, chunk, 0, 0, t + 1).start()

        @pl.when(t > 0)
        def _():
            ag_copy(t, chunk, 1, 0, t - 1).start()

    def wo_piece(shard, col):
        return r.wo.at[shard, rows(col, 48), rows(c, HALF)]

    def wz_piece(a, shard):
        return wo_piece(shard, q) if a == 0 else r.w.at[:, shard, c]

    def wz_copy(a, j):
        piece = wz_piece(a, t)
        return remote(piece, piece, S.wz_s + a * 4 + j, S.wz_r + a * 4 + t, (dp, zpeer(j)))

    def wr_copy(b, side, k, device):
        piece = wz_piece(1, b)
        send = S.wz_s + 4 + side * 4 + k
        return remote(piece, piece, send, S.wz_r + 4 + b, (dp, device))

    loads[0].wait()
    for j in range(1, 4):
        wz_copy(0, j).start()
    for j in range(1, 4):
        remote(r.bup.at[t], r.bup.at[t], S.bup_s + j, S.bup_r + t, (dp, zpeer(j))).start()

    is_long = r.lc[0]
    slot = (1 - is_long) * t
    step = jnp.int32(0)
    for n in range(4):
        step = step + jnp.where(slot == n, r.ts[n], 0)
    lane = lax.broadcasted_iota(jnp.int32, (1, TE), 1)
    half_lane = lax.rem(lane, TE // 2).astype(F32)
    angle = (step.astype(F32) / STEPS * TIME_SCALE) * jnp.exp(half_lane * (-LOG_BASE / (TE // 2)))
    feat = jnp.where(lane < TE // 2, jnp.cos(angle), jnp.sin(angle))
    r.feat[...] = feat
    wide_feat = jnp.broadcast_to(feat, (8, TE))
    loads[3].wait()
    loads[4].wait()
    modulation = jnp.dot(wide_feat, r.w_time[...], precision=HIGHEST, preferred_element_type=F32)
    r.modrow[...] = modulation[0:1] + row(r.b_time)
    gate = r.modrow[:, 2 * D :]
    r.gb[q] = (gate * r.cot[...].astype(F32)).astype(BF)
    for j in range(1, 4):
        remote(r.gb.at[q], r.gb.at[q], S.gb_s + j, S.gb_r + q, column(j)).start()

    lane = lax.broadcasted_iota(jnp.int32, (1, 128), 1)
    freqs = jnp.exp(lax.rem(lane, 32).astype(F32) * (-LOG_BASE / 32))
    sign = jnp.where(lax.rem(lane, 64) < 32, -1.0, 1.0)
    angles = lax.broadcasted_iota(jnp.int32, (256, 128), 0).astype(F32) * freqs
    r.turn[0] = jnp.cos(angles)
    r.turn[1] = jnp.sin(angles) * sign

    def rope_tables(b):
        offset = (b * 256 * is_long).astype(F32) * freqs
        cosine = jnp.cos(offset)
        sine = jnp.sin(offset) * sign
        return (
            r.turn[0] * cosine - r.turn[1] * sine,
            r.turn[1] * cosine + r.turn[0] * sine,
        )

    loads[1].wait()
    loads[2].wait()
    loads[5].wait()
    for n in range(4):

        @pl.when(q == n)
        def _():
            part = r.act[0:3].reshape(D, D)[:, 192 * n : 192 * (n + 1)]
            r.w[0, t] = part.T.reshape(2, 96, D)

    lower = lax.broadcasted_iota(jnp.int32, (256, 128), 1) < HEAD

    def normed_rows(b):
        unit, _ = norm_parts(r.toks[b].astype(F32))
        return unit, (unit * row(r.gain) + row(r.bias)).astype(BF)

    def project(b):
        y = dot_nt(normed_rows(b)[1], r.w_qkv[...]) + r.bqkv[...]
        at = rows(b, 256)
        cosine, sine = rope_tables(b)
        doubled = []
        for n in range(3):
            tile = y[:, 128 * n : 128 * (n + 1)]
            swapped = pltpu.roll(tile, HEAD, 1)
            doubled += [jnp.where(lower, tile, swapped), jnp.where(lower, swapped, tile)]
        for h in range(3):
            for part, dest in ((doubled[h], r.q), (doubled[3 + h], r.k)):
                turned = part * cosine + pltpu.roll(part, 32, 1) * sine
                dest[h, at, :] = turned.astype(BF)
            r.kt[h, b] = turned.T.astype(BF)
        tile = y[:, 384:512]
        for h, value in enumerate((jnp.where(lower, tile, 0.0), jnp.where(lower, 0.0, tile))):
            r.v[h, at, :] = value.astype(BF)
            r.vt[h, b] = value.T.astype(BF)
        value = y[:, 512:576]
        r.v[2, at, :HEAD] = value.astype(BF)
        r.vt[2, b, :HEAD, :] = value.T.astype(BF)

    def ag_step(i, carry):
        k, side, b, nxt = hop(i)

        @pl.when(inside(b))
        def _():
            @pl.when(i > 0)
            def _():
                for chunk in range(2):
                    got(ag_chunk(b, chunk), S.ag_r + 2 * b + chunk)

                    @pl.when(inside(nxt))
                    def _():
                        ag_copy(b, chunk, side, k, nxt).start()

            @pl.when((side == 1) & (k == t + 1))
            def _():
                wr_copy(t, 0, 0, t + 1).start()

            @pl.when((side == 0) & (k == 4 - t))
            def _():
                wr_copy(t, 1, 0, t - 1).start()

            project(b)

        return carry

    lax.fori_loop(0, 7, ag_step, 0)

    @pl.when(t == 2)
    def _():
        wr_copy(t, 0, 0, t + 1).start()

    @pl.when(t == 1)
    def _():
        wr_copy(t, 1, 0, t - 1).start()


    for chunk in range(2):

        @pl.when(t < 3)
        def _():
            sent(ag_chunk(t, 0), S.ag_s + chunk)

        @pl.when(t > 0)
        def _():
            sent(ag_chunk(t, 0), S.ag_s + 8 + chunk)

    def ag_sent(i, carry):
        k, side, b, nxt = hop(i)

        @pl.when(inside(b) & inside(nxt))
        def _():
            for chunk in range(2):
                sent(ag_chunk(b, 0), S.ag_s + (side * 4 + k) * 2 + chunk)

        return carry

    lax.fori_loop(1, 7, ag_sent, 0)

    def wx_copy(b, j):
        index = b * 3 + j - 1
        piece = wo_piece(b, q)
        return remote(piece, piece, S.wx_s + index, S.wx_r + index, column(j))

    def wc_copy(a, b):
        piece = r.wo.at[b, :, rows(c, HALF)] if a == 0 else r.w.at[:, b, c]
        return remote(piece, piece, S.wc_s + a * 4 + b, S.wc_r + a * 4 + b, sibling)

    for j in range(1, 4):
        b = zpeer(j)
        got(wz_piece(0, b), S.wz_r + b)
        for col in range(1, 4):
            wx_copy(b, col).start()

    neg = jnp.where(is_long > 0, 0.0, -1e30)

    def attend(i, carry):
        qb = lax.rem(t + 1 + i, 4)
        outs = []
        for h in range(3):
            queries = r.q[h, rows(qb, 256), :]
            parts = []
            for kb in range(4):
                s = dot_nt(r.k[h, kb * 256 : (kb + 1) * 256, :], queries) * (0.5 * SCALE)
                parts.append(s + jnp.where(qb == kb, 0.0, neg))
            top = parts[0].max(axis=0, keepdims=True)
            for kb in range(1, 4):
                top = jnp.maximum(top, parts[kb].max(axis=0, keepdims=True))
            parts = [jnp.exp(s - top) for s in parts]
            inverse = 1.0 / sum(total(s) for s in parts)
            out = None
            for kb in range(4):
                p = (parts[kb] * inverse).astype(BF)
                r.probs[h, qb, kb * 256 : (kb + 1) * 256, :] = p
                term = dot(r.vt[h, kb] if h < 2 else r.vt[h, kb, :HEAD, :], p)
                out = term if out is None else out + term
            outs.append(out)
        low, high = (outs[0] + outs[1]).T.astype(BF), outs[2].T.astype(BF)

        @pl.when(i < 3)
        def _():
            r.blocks[qb, :, :128] = low
            r.blocks[qb, :, 128:192] = high
            remote(r.blocks.at[qb], r.mixed.at[t], S.mix_s + i, S.mix_r + t, (dp, qb)).start()

        @pl.when(i == 3)
        def _():
            r.mixed[t, :, :128] = low
            r.mixed[t, :, 128:192] = high

        return carry

    lax.fori_loop(0, 4, attend, 0)
    for j in range(1, 4):
        got(r.bup.at[zpeer(j)], S.bup_r + zpeer(j))
    for s in range(4):
        options = [r.bup[s, :, 192 * n : 192 * (n + 1)] for n in range(4)]
        r.bupq[:, 192 * s : 192 * (s + 1)] = pick(q, options)

    for j in range(1, 4):
        b = zpeer(j)
        for col in range(1, 4):
            got(wo_piece(b, columns[col]), S.wx_r + b * 3 + col - 1)
        wc_copy(0, b).start()
    for j in range(1, 4):
        got(r.wo.at[zpeer(j), :, rows(other, HALF)], S.wc_r + zpeer(j))
    for j in range(1, 4):
        got(r.mixed.at[zpeer(j)], S.mix_r + zpeer(j))

    def wr_step(i, carry):
        k, side, b, nxt = hop(i)

        @pl.when(inside(b))
        def _():
            got(wz_piece(1, b), S.wz_r + 4 + b)

            @pl.when(inside(nxt))
            def _():
                wr_copy(b, side, k, nxt).start()

            wc_copy(1, b).start()

        return carry

    lax.fori_loop(1, 3, wr_step, 0)
    attended = jnp.broadcast_to(row(r.b_out), (256, D))
    for g in range(4):
        attended = attended + dot(r.mixed[g], r.wo[g])
    resid = r.toks[t].astype(F32) + attended
    r.resid[...] = resid
    unit2, rstd2 = norm_parts(resid)
    scale1 = 1.0 + r.modrow[:, :D]
    r.mod[q] = (unit2 * scale1 + r.modrow[:, D : 2 * D]).astype(BF)
    for j in range(1, 4):
        remote(r.mod.at[q], r.mod.at[q], S.md_s + j, S.md_r + q, column(j)).start()
    lax.fori_loop(3, 7, wr_step, 0)
    for j in range(1, 4):
        got(r.w.at[:, zpeer(j), other], S.wc_r + 4 + zpeer(j))

    def forward(n, carry):
        j = lax.rem(n + 1, 4)
        col = pick(j, columns)

        @pl.when(j > 0)
        def _():
            got(r.gb.at[col], S.gb_r + col)
            got(r.mod.at[col], S.md_r + col)

        w_up = r.w[0].reshape(D, D)
        hidden = dot_nt(r.mod[col], w_up) + r.bupq[...]
        inner = math.sqrt(2.0 / math.pi)
        square = hidden * hidden
        th = jnp.tanh(inner * hidden * (1.0 + 0.044715 * square))
        halfsum = 0.5 * (1.0 + th)
        r.act[col] = (hidden * halfsum).astype(BF)
        slope = halfsum + 0.5 * hidden * (1.0 - th * th) * (inner * (1.0 + 3 * 0.044715 * square))
        grad_active = dot_nt(r.gb[col], r.w[1].reshape(D, D))
        gh = (slope * grad_active).astype(BF)
        r.gh[col] = gh
        grad_mod = dot(gh, w_up)

        @pl.when(j == 0)
        def _():
            r.gres[...] = grad_mod

        @pl.when(j > 0)
        def _():
            r.gmp_out[j - 1] = grad_mod.astype(BF)
            device = (block + 2 * col + c, t)
            remote(r.gmp_out.at[j - 1], r.gmp_in.at[j - 1], S.gmp_s + j, S.gmp_r + j, device).start()

        return carry

    lax.fori_loop(0, 4, forward, 0)

    def r2_copy(a, j):
        col = columns[j]
        src = r.gwo.at[c, :, col] if a == 0 else r.gqkv.at[c, col]
        dst = (r.r2o, r.r2q)[a].at[j - 1]
        return remote(src, dst, S.r2_s + a * 3 + j - 1, S.r2_r + a * 3 + j - 1, column(j))

    def r3_piece(a, shard):
        return r.gwo.at[c, shard, q] if a == 0 else r.gw.at[a - 1, shard, c]

    def r3_copy(a, j):
        goal = zpeer(j)
        dst = r.r3o.at[t] if a == 0 else r.r3w.at[a - 1, t]
        return remote(
            r3_piece(a, goal), dst, S.r3_s + a * 4 + j, S.r3_r + a * 4 + t, (dp, goal)
        )

    def out_piece(a, col):
        if a == 0:
            return r.oo.at[rows(col, 48), rows(c, HALF)]
        if a < 3:
            return r.ow.at[a - 1, col, c]
        return r.oqkv.at[rows(col, 144), rows(c, HALF)]

    def r4_copy(a, j):
        piece = out_piece(a, q)
        index = a * 3 + j - 1
        return remote(piece, piece, S.r4_s + index, S.r4_r + index, column(j))

    def half_out(a, who):
        if a == 0:
            return r.oo.at[:, rows(who, HALF)]
        if a < 3:
            return r.ow.at[a - 1, :, who]
        return r.oqkv.at[:, rows(who, HALF)]

    def r5_copy(a):
        piece = half_out(a, c)
        return remote(piece, piece, S.r5_s + a, S.r5_r + a, sibling)

    def r1_copy_w(a):
        return remote(r.gw.at[a, :, other], r.r1w.at[a], S.r1_s + a, S.r1_r + a, sibling)

    def r1_sum_w(a):
        got(r.r1w.at[a], S.r1_r + a)
        r.gw[a, :, c] = (r.gw[a, :, c].astype(F32) + r.r1w[a].astype(F32)).astype(BF)

    def r3_start(a):
        for j in range(1, 4):
            r3_copy(a, j).start()

    def r1_sum_o():
        got(r.r1o, S.r1_r + 2)
        r.gwo[c] = (r.gwo[c].astype(F32) + r.r1o[...].astype(F32)).astype(BF)
        for j in range(1, 4):
            r2_copy(0, j).start()

    def r2_sum(a):
        for j in range(1, 4):
            copy = r2_copy(a, j)
            copy.wait_recv()
            copy.wait_send()
        mine_ref = r.gwo.at[c, :, q] if a == 0 else r.gqkv.at[c, q]
        theirs = (r.r2o, r.r2q)[a]
        acc = mine_ref[...].astype(F32)
        for j in range(3):
            acc = acc + theirs[j].astype(F32)
        if a == 0:
            mine_ref[...] = acc.astype(BF)
            r3_start(0)
        else:
            out_piece(3, q)[...] = acc.astype(BF)
            for j in range(1, 4):
                r4_copy(3, j).start()

    def r3_sum(a):
        buf = r.r3o if a == 0 else r.r3w.at[a - 1]
        acc = r3_piece(a, t)[...].astype(F32)
        for j in range(1, 4):
            got(buf.at[zpeer(j)], S.r3_r + a * 4 + zpeer(j))
            acc = acc + buf[zpeer(j)].astype(F32)
        out_piece(a, q)[...] = acc.astype(BF)
        for j in range(1, 4):
            r4_copy(a, j).start()

    def r4_wait(a):
        for j in range(1, 4):
            got(out_piece(a, columns[j]), S.r4_r + a * 3 + j - 1)
        r5_copy(a).start()

    def weight_grad(a):
        left = (r.gh, r.act)[a][...].reshape(1024, D)
        right = (r.mod, r.gb)[a][...].reshape(1024, D)
        for s in range(4):
            grad = dot_tn(left[:, 192 * s : 192 * (s + 1)], right)
            r.gw[a, s] = grad.astype(BF).reshape(2, 96, D)

    for a in (1, 0):
        weight_grad(a)
        r1_copy_w(a).start()
    r1_sum_w(1)
    r3_start(2)
    r1_sum_w(0)

    grad_mod = r.gres[...]
    for j in range(1, 4):
        got(r.gmp_in.at[j - 1], S.gmp_r + j)
        grad_mod = grad_mod + r.gmp_in[j - 1].astype(F32)
    unit2, rstd2 = norm_parts(r.resid[...])
    scale1 = 1.0 + r.modrow[:, :D]
    grad_resid = r.cot[...].astype(F32) + norm_back(unit2, rstd2, grad_mod * scale1)
    r.gres[...] = grad_resid
    grad_att = grad_resid.astype(BF)
    for i in range(3):
        sent(r.blocks.at[0], S.mix_s + i)
    for i in range(1, 4):
        g = lax.rem(t + i, 4)
        r.blocks[g] = dot_nt(grad_att, r.wo[g]).astype(BF)
        remote(r.blocks.at[g], r.gm.at[t], S.gm_s + i, S.gm_r + t, (dp, g)).start()
    r.gm[t] = dot_nt(grad_att, r.wo[t]).astype(BF)
    r.small[0:1, :] = total(grad_mod * unit2)
    r.small[1:2, :] = total(grad_mod)
    r.small[3:4, :] = jnp.zeros((1, D), F32)
    r.small[3:4, :TE] = r.feat[...]
    r.small[4:5, :] = total(grad_att.astype(F32))
    r.small[5:6, :] = total(r.gb[q].astype(F32))
    r.small[6:7, :] = total(r.gh[...].reshape(1024, D).astype(F32))
    r.small[7:8, :] = jnp.zeros((1, D), F32)
    for g in range(4):
        grad = dot_tn(r.mixed[g], grad_att).astype(BF)
        for half in range(2):
            r.gwo[half, g] = grad[:, HALF * half : HALF * (half + 1)].reshape(4, 48, HALF)
    remote(r.gwo.at[other], r.r1o, S.r1_s + 2, S.r1_r + 2, sibling).start()
    for j in range(1, 4):
        sent(r.gmp_out.at[j - 1], S.gmp_s + j)

    def down(n, carry):
        j = lax.rem(n + 1, 4)
        col = pick(j, columns)
        branch = dot(r.act[col], r.w[1].reshape(D, D))

        @pl.when(j == 0)
        def _():
            r.gtok[...] = branch

        @pl.when(j > 0)
        def _():
            r.gmp_out[j - 1] = branch.astype(BF)
            device = (block + 2 * col + c, t)
            remote(r.gmp_out.at[j - 1], r.br_in.at[j - 1], S.br_s + j, S.br_r + j, device).start()

        return carry

    lax.fori_loop(0, 4, down, 0)


    r1_sum_o()

    r.wide[...] = jnp.zeros((12, 512, 128), F32)

    def attend_back(i, carry):
        qb = lax.rem(t + i, 4)

        @pl.when(i > 0)
        def _():
            got(r.gm.at[qb], S.gm_r + qb)

        @pl.when(i == 3)
        def _():
            r3_start(1)

        at = rows(qb, 256)
        cosine, sine = rope_tables(qb)
        for h in range(3):
            width = 128 if h < 2 else HEAD
            grad_out = r.gm[qb, :, :128] if h < 2 else r.gm[qb, :, 128:192]
            queries = r.q[h, at, :]
            probs = []
            grads = []
            inner = None
            for kb in range(4):
                keys = slice(kb * 256, (kb + 1) * 256)
                p = r.probs[h, qb, keys, :]
                g = dot_nt(r.v[h, keys, :width], grad_out)
                term = total(g * p.astype(F32))
                inner = term if inner is None else inner + term
                probs.append(p)
                grads.append(g)
                place = slice(256 * (kb % 2), 256 * (kb % 2 + 1))
                r.wide[6 + 2 * h + kb // 2, place, :width] += dot(p, grad_out)
            grad_q = None
            for kb in range(4):
                ds = (probs[kb].astype(F32) * (grads[kb] - inner)).astype(BF)
                place = slice(256 * (kb % 2), 256 * (kb % 2 + 1))
                r.wide[2 * h + kb // 2, place, :] += dot(ds, queries)
                term = dot(r.kt[h, kb], ds)
                grad_q = term if grad_q is None else grad_q + term
            grad_q = grad_q.T * SCALE
            turned = grad_q * cosine - pltpu.roll(grad_q, 32, 1) * sine
            if h == 0:
                first_q = turned
            elif h == 1:
                r.gp[qb, :, :128] = jnp.where(lower, first_q, turned).astype(BF)
            else:
                r.gp[qb, :, 128:256] = turned.astype(BF)
        return carry

    lax.fori_loop(0, 4, attend_back, 0)

    def finish(b, carry):
        cosine, sine = rope_tables(b)
        keys = []
        half = rows(lax.rem(b, 2), 256)
        place = lax.div(b, 2)
        for h in range(3):
            grad = r.wide[2 * h + place, half, :] * SCALE
            keys.append(grad * cosine - pltpu.roll(grad, 32, 1) * sine)
        values = [r.wide[6 + 2 * h + place, half, :] for h in range(3)]
        last_q = r.gp[b, :, 128:256].astype(F32)
        r.gp[b, :, 128:256] = jnp.where(lower, last_q, keys[0]).astype(BF)
        r.gp[b, :, 256:384] = jnp.where(lower, keys[1], keys[2]).astype(BF)
        r.gp[b, :, 384:512] = jnp.where(lower, values[0], values[1]).astype(BF)
        r.gp[b, :, 512:576] = values[2][:, :HEAD].astype(BF)
        return carry

    lax.fori_loop(0, 4, finish, 0)

    def rs_step(k):
        for side in range(2):
            step = 1 - 2 * side
            goal = t + step * (4 - k)
            nxt = t + step
            prev = t - step
            slot = 3 - k if side else k - 1

            @pl.when(inside(goal))
            def _():
                for chunk in range(2):
                    at = slice(128 * chunk, 128 * (chunk + 1))
                    part = dot(r.gp[goal, at, :], r.w_qkv[...])
                    r.rs_out[slot, at, :] = part.astype(BF)
                    if k > 1:

                        @pl.when(inside(prev))
                        def _():
                            index = (side * 3 + k - 2) * 2 + chunk
                            got(r.rs_in.at[side, k - 2, at], S.rs_r + index)
                            summed = part + r.rs_in[side, k - 2, at, :].astype(F32)
                            r.rs_out[slot, at, :] = summed.astype(BF)

                    index = (side * 3 + k - 1) * 2 + chunk
                    remote(
                        r.rs_out.at[slot, at],
                        r.rs_in.at[side, k - 1, at],
                        S.rs_s + index,
                        S.rs_r + index,
                        (dp, nxt),
                    ).start()

    rs_step(1)
    r2_sum(0)

    branch = r.gtok[...] + row(r.b_down)
    for j in range(1, 4):
        got(r.br_in.at[j - 1], S.br_r + j)
        branch = branch + r.br_in[j - 1].astype(F32)
    r.result[...] = (r.resid[...] + r.modrow[:, 2 * D :] * branch).astype(BF)
    store("result")
    r.small[2:3, :] = total(r.cot[...].astype(F32) * branch)
    r.zs[t] = r.small[...]
    for j in range(1, 4):
        remote(r.small, r.zs.at[t], S.ez_s + j, S.ez_r + t, (dp, zpeer(j))).start()

    def norm_sums(b, carry):
        unit, r.act[b] = normed_rows(b)
        part = dot(r.gp[b], r.w_qkv[...])
        gain, bias = carry
        return gain + total(part * unit), bias + total(part)

    zero = jnp.zeros((1, D), F32)
    gain, bias = lax.fori_loop(0, 4, norm_sums, (zero, zero))
    r.late[...] = jnp.zeros((8, D), F32)
    r.late[0:1, :] = gain
    r.late[1:2, :] = bias
    r.late[2:3, :576] = total(r.gp[...].reshape(1024, 576).astype(F32))
    r.zl[t] = r.late[...]
    for j in range(1, 4):
        remote(r.late, r.zl.at[t], S.lz_s + j, S.lz_r + t, (dp, zpeer(j))).start()
    grad_w = dot_tn(r.gp[...].reshape(1024, 576), r.act[...].reshape(1024, D)).astype(BF)
    for half in range(2):
        lanes = slice(HALF * half, HALF * (half + 1))
        r.gqkv[half] = grad_w[:, lanes].reshape(4, 144, HALF)
    r3_sum(2)
    remote(r.gqkv.at[other], r.r1q, S.r1_s + 3, S.r1_r + 3, sibling).start()
    got(r.r1q, S.r1_r + 3)
    r.gqkv[c] = (r.gqkv[c].astype(F32) + r.r1q[...].astype(F32)).astype(BF)
    for j in range(1, 4):
        r2_copy(1, j).start()
    rs_step(2)

    for j in range(1, 4):
        got(r.zs.at[zpeer(j)], S.ez_r + zpeer(j))
    for z in range(4):
        for n in range(4):
            r.ds[mine, 4 * n + z : 4 * n + z + 1, :] = r.zs[z, n : n + 1, :]
    r.ds[mine, 16:20, :] = r.zs[0, 4:8, :] + r.zs[1, 4:8, :] + r.zs[2, 4:8, :] + r.zs[3, 4:8, :]
    r.ds[mine, 20:24, :] = jnp.zeros((4, D), F32)
    for j in range(1, 8):
        peer = lax.rem(mine + j, 8)
        remote(
            r.ds.at[mine], r.ds.at[mine], S.ed_s + j, S.ed_r + mine, (block + peer, t)
        ).start()
    for j in range(1, 4):
        got(r.zl.at[zpeer(j)], S.lz_r + zpeer(j))
    r.dl[mine] = r.zl[0] + r.zl[1] + r.zl[2] + r.zl[3]
    r.dl[mine, 2:3, :] = r.late[2:3, :]
    for j in range(1, 8):
        peer = lax.rem(mine + j, 8)
        remote(
            r.dl.at[mine], r.dl.at[mine], S.ld_s + j, S.ld_r + mine, (block + peer, t)
        ).start()
    rs_step(3)
    own = dot(r.gp[t], r.w_qkv[...])
    r2_sum(1)
    r3_sum(1)
    r3_sum(0)

    for j in range(1, 8):
        peer = lax.rem(mine + j, 8)
        got(r.ds.at[peer], S.ed_r + peer)
    for peer in range(8):
        for n in range(4):
            r.gmat[n, 4 * peer : 4 * peer + 4, :] = r.ds[peer, 4 * n : 4 * n + 4, :]
    for n in range(3):
        r.gwt[:, D * n : D * (n + 1)] = dot_tn(r.gmat[3][:, :TE], r.gmat[n], HIGHEST)
        r.vec[4 + n : 5 + n, :] = total(r.gmat[n])
    r.vec[2:4, :] = sum(r.ds[peer, 16:18, :] for peer in range(8))
    for n in range(4):
        units = r.ds[2 * n, 18:19, :] + r.ds[2 * n + 1, 18:19, :]
        options = [units[:, 192 * s : 192 * (s + 1)] for s in range(4)]
        r.vec[7:8, 192 * n : 192 * (n + 1)] = pick(t, options)
    store("gwt")
    for j in range(1, 8):
        peer = lax.rem(mine + j, 8)
        got(r.dl.at[peer], S.ld_r + peer)
    last = sum(r.dl[peer, 0:3, :] for peer in range(8))
    r.vec[0:2, :] = last[0:2]
    r.vec[8:9, :] = last[2:3]
    store("vec")

    for side in range(2):
        prev = t - (1 - 2 * side)

        @pl.when(inside(prev))
        def _():
            for chunk in range(2):
                at = slice(128 * chunk, 128 * (chunk + 1))
                got(r.rs_in.at[side, 2, at], S.rs_r + (side * 3 + 2) * 2 + chunk)

        @pl.when((prev < 0) | (prev > 3))
        def _():
            r.rs_in[side, 2] = jnp.zeros((256, D), BF)

    grad_normed = own + r.rs_in[0, 2].astype(F32) + r.rs_in[1, 2].astype(F32)
    unit1, rstd1 = norm_parts(r.toks[t].astype(F32))
    r.gtok[...] = r.gres[...] + norm_back(unit1, rstd1, grad_normed * row(r.gain))
    store("gtok")

    for a in (2, 3, 1, 0):
        r4_wait(a)
    for a in (2, 3, 1, 0):
        got(half_out(a, other), S.r5_r + a)
    store("oqkv")
    store("oo")
    r.od[...] = r.ow[1].reshape(D, D)
    store("od")
    r.ou[...] = r.ow[0].reshape(D, D).T
    store("ou")

    for j in range(1, 4):
        sent(r.bup.at[t], S.bup_s + j)
        sent(r.small, S.ez_s + j)
        sent(r.late, S.lz_s + j)
        sent(r.blocks.at[0], S.gm_s + j)
        for base in (S.gb_s, S.md_s, S.br_s):
            sent(r.gb.at[0], base + j)
        for a in range(3):
            sent(r3_piece(a, t), S.r3_s + a * 4 + j)
        sent(wz_piece(0, t), S.wz_s + j)
        b = zpeer(j)
        sent(r.wo.at[b, :, rows(c, HALF)], S.wc_s + b)
        sent(wz_piece(1, b), S.wc_s + 4 + b)
        for col in range(1, 4):
            sent(wo_piece(b, q), S.wx_s + b * 3 + col - 1)
    for side in range(2):

        @pl.when(inside(t + 1 - 2 * side))
        def _():
            sent(wz_piece(1, t), S.wz_s + 4 + side * 4)

    def wr_sent(i, carry):
        k, side, b, nxt = hop(i)

        @pl.when(inside(b) & inside(nxt))
        def _():
            sent(wz_piece(1, b), S.wz_s + 4 + side * 4 + k)

        return carry

    lax.fori_loop(1, 7, wr_sent, 0)
    for a in range(2):
        sent(r.r1w.at[a], S.r1_s + a)
    sent(r.r1o, S.r1_s + 2)
    sent(r.r1q, S.r1_s + 3)
    for j in range(1, 8):
        sent(r.ds.at[mine], S.ed_s + j)
        sent(r.dl.at[mine], S.ld_s + j)
    for a in range(4):
        sent(half_out(a, c), S.r5_s + a)
        for j in range(1, 4):
            sent(out_piece(a, q), S.r4_s + a * 3 + j - 1)

    for k in range(1, 4):
        for side in range(2):
            goal = t + (1 - 2 * side) * (4 - k)

            @pl.when(inside(goal))
            def _():
                for chunk in range(2):
                    sent(r.rs_out.at[0, 0:128], S.rs_s + (side * 3 + k - 1) * 2 + chunk)
    for copy in stores:
        copy.wait()


def fused(scalars, blocks, far, outs):
    vmem = pl.BlockSpec(memory_space=pltpu.VMEM)
    smem = pl.BlockSpec(memory_space=pltpu.SMEM)
    anywhere = pl.BlockSpec(memory_space=pl.ANY)
    operands = scalars | blocks | far
    return pl.pallas_call(
        partial(body, [*operands, *outs, *SCRATCH]),
        out_shape=[jax.ShapeDtypeStruct(shape, kind) for shape, kind in outs.values()],
        in_specs=[smem] * len(scalars) + [vmem] * len(blocks) + [anywhere] * len(far),
        out_specs=[anywhere] * len(outs),
        scratch_shapes=[pltpu.VMEM(shape, kind) for shape, kind in SCRATCH.values()]
        + [pltpu.SemaphoreType.DMA((COUNT,))],
        compiler_params=pltpu.CompilerParams(
            collective_id=0, has_side_effects=True, vmem_limit_bytes=63 << 20
        ),
        name="layer",
    )(*operands.values())


def widen_body(result, gtok, oqkv, oo, ou, od, gwt, vec, *outs):
    for src, dst in zip((result, gtok, oqkv, gwt, oo, ou, od), outs[:7], strict=True):
        dst[...] = src[...].astype(dst.dtype)
    ggain, gbias, gbqkv, gbo, gbt, gbu, gbd = outs[7:]
    for n, dst in ((0, ggain), (1, gbias), (2, gbo), (3, gbd), (7, gbu)):
        dst[...] = vec[n : n + 1, :].reshape(D)
    for n in range(3):
        gbt[D * n : D * (n + 1)] = vec[4 + n : 5 + n, :].reshape(D)
        gbqkv[n : n + 1, :] = vec[8:9, 192 * n : 192 * (n + 1)]


def widen(parts):
    vmem = pl.BlockSpec(memory_space=pltpu.VMEM)
    outs = (
        ((256, D), BF),
        ((256, D), F32),
        ((576, D), F32),
        ((TE, 3 * D), F32),
        ((192, D), F32),
        ((D, D), F32),
        ((D, D), F32),
        ((D,), F32),
        ((D,), F32),
        ((3, 192), F32),
        ((D,), F32),
        ((3 * D,), F32),
        ((D,), F32),
        ((D,), F32),
    )
    return pl.pallas_call(
        widen_body,
        out_shape=[jax.ShapeDtypeStruct(shape, kind) for shape, kind in outs],
        in_specs=[vmem] * 8,
        out_specs=[vmem] * 14,
        compiler_params=pltpu.CompilerParams(vmem_limit_bytes=62 << 20),
        name="widen",
    )(*parts)


def on_device(
    tokens,
    long_count,
    timesteps,
    norm_gain,
    norm_bias,
    w_qkv,
    b_qkv,
    w_out,
    b_out,
    w_time,
    b_time,
    w_up,
    b_up,
    w_down,
    b_down,
    cotangent,
):
    n_dp = lax.axis_size("dp")
    assert tokens.shape == (SHORT, D) and lax.axis_size("tensor") * SHORT == LONG and n_dp % 8 == 0
    scalars = dict(lc=long_count, ts=timesteps)
    blocks = dict(
        gain=norm_gain,
        bias=norm_bias,
        b_out=b_out,
        b_down=b_down,
        b_time=b_time,
        bup_own=b_up,
        b_qkv=b_qkv,
    )
    far = dict(
        wo_own=w_out,
        wu_own=w_up.reshape(3, 256, D),
        wd_own=w_down.reshape(4, 2, 96, D),
        w_time_far=w_time,
        cot_far=cotangent,
        tok_far=tokens,
        w_qkv_far=jnp.transpose(w_qkv, (0, 2, 1)).reshape(576, D),
    )
    outs = dict(
        out_result=((256, D), BF),
        out_gtok=((256, D), F32),
        out_oqkv=((576, D), BF),
        out_oo=((192, D), BF),
        out_ou=((D, D), BF),
        out_od=((D, D), BF),
        out_gwt=((TE, 3 * D), F32),
        out_vec=((16, D), F32),
    )
    result, grad_tokens, gqkv, gwt, *rest = widen(fused(scalars, blocks, far, outs))
    gwo, gwu, gwd, ggain, gbias, gbqkv, gbo, gbt, gbu, gbd = rest
    grads = (
        ggain,
        gbias,
        jnp.transpose(gqkv.reshape(3, 192, D), (0, 2, 1)),
        gbqkv,
        gwo,
        gbo,
        gwt,
        gbt,
        gwu,
        gbu,
        gwd,
        gbd,
    )
    if n_dp > 8:
        groups = [[inner + 8 * outer for outer in range(n_dp // 8)] for inner in range(8)]
        grads = lax.psum(grads, "dp", axis_index_groups=groups)
    return (result, grad_tokens) + tuple(grads)


def solution(mesh):
    rows = P(("dp", "tensor"), None)
    placed = (
        rows,
        P("dp"),
        P("dp"),
        P(),
        P(),
        P(None, None, "tensor"),
        P(None, "tensor"),
        P("tensor", None),
        P(),
        P(),
        P(),
        P(None, "tensor"),
        P("tensor"),
        P("tensor", None),
        P(),
        rows,
    )
    return jax.shard_map(
        on_device,
        mesh=mesh,
        in_specs=placed,
        out_specs=(rows, rows) + placed[3:15],
        check_vma=False,
    )
```

```python
import math
from functools import partial
from itertools import accumulate
from types import SimpleNamespace

import jax
import jax.numpy as jnp
from jax import lax
from jax.experimental import pallas as pl
from jax.experimental.pallas import tpu as pltpu
from jax.sharding import PartitionSpec as P

HEAD = 64
TE = 128
STEPS = 1000
LONG = 1024
SHORT = 256
D = 768
HALF = 384
EPS = 1e-05
TIME_SCALE = 64.0
SCALE = 1.0 / math.sqrt(HEAD)
LOG_BASE = math.log(10000.0)
BF = jnp.bfloat16
F32 = jnp.float32
MESH = pl.DeviceIdType.MESH
HIGHEST = lax.Precision.HIGHEST

SEMS = dict(
    load=7,
    store=9,
    ag_s=16,
    ag_r=8,
    bup_s=4,
    bup_r=4,
    gb_s=4,
    gb_r=4,
    md_s=4,
    md_r=4,
    wz_s=12,
    wz_r=8,
    wx_s=12,
    wx_r=12,
    wc_s=8,
    wc_r=8,
    mix_s=4,
    mix_r=4,
    gmp_s=4,
    gmp_r=4,
    br_s=4,
    br_r=4,
    gm_s=4,
    gm_r=4,
    r1_s=4,
    r1_r=4,
    r2_s=6,
    r2_r=6,
    r3_s=12,
    r3_r=12,
    r4_s=12,
    r4_r=12,
    r5_s=4,
    r5_r=4,
    rs_s=12,
    rs_r=12,
    ez_s=4,
    ez_r=4,
    ed_s=8,
    ed_r=8,
    lz_s=4,
    lz_r=4,
    ld_s=8,
    ld_r=8,
)
COUNT = sum(SEMS.values())
S = SimpleNamespace(**dict(zip(SEMS, accumulate(SEMS.values(), initial=0))))

SCRATCH = dict(
    cot=((256, D), BF),
    w_qkv=((576, D), BF),
    w_time=((TE, 3 * D), F32),
    result=((256, D), BF),
    gtok=((256, D), F32),
    oqkv=((576, D), BF),
    oo=((192, D), BF),
    ou=((D, D), BF),
    od=((D, D), BF),
    gwt=((TE, 3 * D), F32),
    vec=((16, D), F32),
    turn=((2, 256, 128), F32),
    feat=((1, TE), F32),
    modrow=((1, 3 * D), F32),
    toks=((4, 256, D), BF),
    normed=((4, 256, D), BF),
    q=((3, 1024, 128), BF),
    k=((3, 1024, 128), BF),
    v=((3, 1024, 128), BF),
    kt=((3, 4, 128, 256), BF),
    vt=((3, 4, 128, 256), BF),
    probs=((3, 4, 1024, 256), BF),
    blocks=((4, 256, 192), BF),
    mixed=((4, 256, 192), BF),
    wo=((4, 192, D), BF),
    w=((2, 4, 2, 96, D), BF),
    bup=((4, 1, D), F32),
    bqkv=((1, 576), F32),
    bupq=((1, D), F32),
    mod=((4, 256, D), BF),
    gb=((4, 256, D), BF),
    act=((4, 256, D), BF),
    gh=((4, 256, D), BF),
    wide=((12, 512, 128), F32),
    gmp_out=((3, 256, D), BF),
    gmp_in=((3, 256, D), BF),
    br_in=((3, 256, D), BF),
    gwo=((2, 4, 4, 48, HALF), BF),
    gw=((2, 4, 2, 96, D), BF),
    resid=((256, D), F32),
    gres=((256, D), F32),
    gm=((4, 256, 192), BF),
    gp=((4, 256, 576), BF),
    gqkv=((2, 4, 144, HALF), BF),
    r1o=((4, 4, 48, HALF), BF),
    r1w=((2, 4, 96, D), BF),
    r1q=((4, 144, HALF), BF),
    r2o=((3, 4, 48, HALF), BF),
    r2q=((3, 144, HALF), BF),
    r3w=((2, 4, 96, D), BF),
    r3o=((4, 48, HALF), BF),
    ow=((2, 4, 2, 96, D), BF),
    rs_in=((2, 3, 256, D), BF),
    small=((8, D), F32),
    zs=((4, 8, D), F32),
    ds=((8, 24, D), F32),
    late=((8, D), F32),
    zl=((4, 8, D), F32),
    dl=((8, 8, D), F32),
    gmat=((4, 32, D), F32),
)


def dot(a, b):
    return jnp.dot(a, b, preferred_element_type=F32)


def dot_nt(a, b):
    return lax.dot_general(a, b, (((1,), (1,)), ((), ())), preferred_element_type=F32)


def dot_tn(a, b, precision=None):
    dims = (((0,), (0,)), ((), ()))
    return lax.dot_general(a, b, dims, precision=precision, preferred_element_type=F32)


def norm_parts(values):
    center = values - jnp.mean(values, axis=-1, keepdims=True)
    rstd = lax.rsqrt(jnp.mean(center * center, axis=-1, keepdims=True) + EPS)
    return center * rstd, rstd


def norm_back(unit, rstd, grad):
    mean_g = jnp.mean(grad, axis=-1, keepdims=True)
    mean_gn = jnp.mean(grad * unit, axis=-1, keepdims=True)
    return (grad - mean_g - unit * mean_gn) * rstd


def total(values):
    return jnp.sum(values, axis=0, keepdims=True)


def row(ref):
    return ref[...].reshape(1, -1)


def pick(index, options):
    chosen = options[-1]
    for n in range(len(options) - 2, -1, -1):
        chosen = jnp.where(index == n, options[n], chosen)
    return chosen


def body(names, *refs):
    sem = refs[-1]
    r = SimpleNamespace(**dict(zip(names, refs[:-1], strict=True)))
    dp = lax.axis_index("dp")
    t = lax.axis_index("tensor")
    mine = lax.rem(dp, 8)
    block = dp - mine
    c = lax.rem(dp, 2)
    q = lax.div(mine, 2)
    other = 1 - c
    sibling = (dp + 1 - 2 * c, t)
    columns = [q, q + 1 - 2 * lax.rem(q, 2), q + 2 - 4 * lax.div(q, 2), 3 - q]

    def column(j):
        return (block + 2 * columns[j] + c, t)

    def zpeer(j):
        return lax.rem(t + j, 4)

    def remote(src, dst, send, recv, device):
        return pltpu.make_async_remote_copy(
            src_ref=src,
            dst_ref=dst,
            send_sem=sem.at[send],
            recv_sem=sem.at[recv],
            device_id=device,
            device_id_type=MESH,
        )

    def got(ref, recv):
        remote(ref, ref, recv, recv, sibling).wait_recv()

    def sent(ref, send):
        remote(ref, ref, send, send, sibling).wait_send()

    def rows(index, size):
        return pl.ds(pl.multiple_of(index * size, size), size)

    def hop(i):
        k = lax.div(i + 1, 2)
        side = 1 - lax.rem(i, 2)
        step = 2 * side - 1
        return k, side, t + step * k, t - step

    def inside(b):
        return (b >= 0) & (b <= 3)

    barrier = pltpu.get_barrier_semaphore()
    for j in range(1, 4):
        pl.semaphore_signal(barrier, inc=1, device_id=(dp, zpeer(j)), device_id_type=MESH)
    for j in range(1, 8):
        peer = block + lax.rem(mine + j, 8)
        pl.semaphore_signal(barrier, inc=1, device_id=(peer, t), device_id_type=MESH)

    loads = [
        pltpu.make_async_copy(r.wo_own, r.wo.at[t], sem.at[S.load]),
        pltpu.make_async_copy(r.wu_own, r.act.at[0:3], sem.at[S.load + 1]),
        pltpu.make_async_copy(r.wd_own.at[q], r.w.at[1, t], sem.at[S.load + 2]),
        pltpu.make_async_copy(r.w_time_far, r.w_time, sem.at[S.load + 3]),
        pltpu.make_async_copy(r.cot_far, r.cot, sem.at[S.load + 4]),
        pltpu.make_async_copy(r.w_qkv_far, r.w_qkv, sem.at[S.load + 5]),
        pltpu.make_async_copy(r.tok_far, r.toks.at[t], sem.at[S.load + 6]),
    ]
    for load in reversed(loads):
        load.start()
    names_out = [name for name in names if name.startswith("out_")]

    def store(name):
        n = names_out.index("out_" + name)
        copy = pltpu.make_async_copy(getattr(r, name), getattr(r, "out_" + name), sem.at[S.store + n])
        copy.start()
        stores.append(copy)

    stores = []

    r.bup[t] = row(r.bup_own)
    for n in range(3):
        r.bqkv[:, 192 * n : 192 * (n + 1)] = r.b_qkv[n : n + 1, :]
    loads[6].wait()
    pl.semaphore_wait(barrier, 10)

    def ag_chunk(b, chunk):
        return r.toks.at[b, 128 * chunk : 128 * (chunk + 1)]

    def ag_copy(b, chunk, side, k, device):
        piece = ag_chunk(b, chunk)
        send = S.ag_s + (side * 4 + k) * 2 + chunk
        return remote(piece, piece, send, S.ag_r + 2 * b + chunk, (dp, device))

    def ag_own(chunk):
        @pl.when(t < 3)
        def _():
            ag_copy(t, chunk, 0, 0, t + 1).start()

        @pl.when(t > 0)
        def _():
            ag_copy(t, chunk, 1, 0, t - 1).start()

    def ag_own_sent(chunk):
        @pl.when(t < 3)
        def _():
            sent(ag_chunk(t, 0), S.ag_s + chunk)

        @pl.when(t > 0)
        def _():
            sent(ag_chunk(t, 0), S.ag_s + 8 + chunk)

    ag_own(0)
    def wo_piece(shard, col):
        return r.wo.at[shard, rows(col, 48), rows(c, HALF)]

    def wz_piece(a, shard):
        return wo_piece(shard, q) if a == 0 else r.w.at[:, shard, c]

    def wz_copy(a, j):
        piece = wz_piece(a, t)
        return remote(piece, piece, S.wz_s + a * 4 + j, S.wz_r + a * 4 + t, (dp, zpeer(j)))

    def wr_copy(b, side, k, device):
        piece = wz_piece(1, b)
        send = S.wz_s + 4 + side * 4 + k
        return remote(piece, piece, send, S.wz_r + 4 + b, (dp, device))

    loads[0].wait()
    for j in range(1, 4):
        wz_copy(0, j).start()
    for j in range(1, 4):
        remote(r.bup.at[t], r.bup.at[t], S.bup_s + j, S.bup_r + t, (dp, zpeer(j))).start()

    is_long = r.lc[0]
    slot = (1 - is_long) * t
    step = jnp.int32(0)
    for n in range(4):
        step = step + jnp.where(slot == n, r.ts[n], 0)
    lane = lax.broadcasted_iota(jnp.int32, (1, TE), 1)
    half_lane = lax.rem(lane, TE // 2).astype(F32)
    angle = (step.astype(F32) / STEPS * TIME_SCALE) * jnp.exp(half_lane * (-LOG_BASE / (TE // 2)))
    feat = jnp.where(lane < TE // 2, jnp.cos(angle), jnp.sin(angle))
    r.feat[...] = feat
    wide_feat = jnp.broadcast_to(feat, (8, TE))
    loads[3].wait()
    loads[4].wait()
    modulation = jnp.dot(wide_feat, r.w_time[...], precision=HIGHEST, preferred_element_type=F32)
    r.modrow[...] = modulation[0:1] + row(r.b_time)
    gate = r.modrow[:, 2 * D :]
    r.gb[q] = (gate * r.cot[...].astype(F32)).astype(BF)
    for j in range(1, 4):
        remote(r.gb.at[q], r.gb.at[q], S.gb_s + j, S.gb_r + q, column(j)).start()

    ag_own_sent(0)
    ag_own(1)

    lane = lax.broadcasted_iota(jnp.int32, (1, 128), 1)
    freqs = jnp.exp(lax.rem(lane, 32).astype(F32) * (-LOG_BASE / 32))
    sign = jnp.where(lax.rem(lane, 64) < 32, -1.0, 1.0)
    angles = lax.broadcasted_iota(jnp.int32, (256, 128), 0).astype(F32) * freqs
    r.turn[0] = jnp.cos(angles)
    r.turn[1] = jnp.sin(angles) * sign

    def rope_tables(b):
        offset = (b * 256 * is_long).astype(F32) * freqs
        cosine = jnp.cos(offset)
        sine = jnp.sin(offset) * sign
        return (
            r.turn[0] * cosine - r.turn[1] * sine,
            r.turn[1] * cosine + r.turn[0] * sine,
        )

    loads[1].wait()
    loads[2].wait()
    loads[5].wait()
    for n in range(4):

        @pl.when(q == n)
        def _():
            part = r.act[0:3].reshape(D, D)[:, 192 * n : 192 * (n + 1)]
            r.w[0, t] = part.T.reshape(2, 96, D)

    lower = lax.broadcasted_iota(jnp.int32, (256, 128), 1) < HEAD

    def project(b):
        unit, _ = norm_parts(r.toks[b].astype(F32))
        r.normed[b] = (unit * row(r.gain) + row(r.bias)).astype(BF)
        y = dot_nt(r.normed[b], r.w_qkv[...]) + r.bqkv[...]
        at = rows(b, 256)
        cosine, sine = rope_tables(b)
        doubled = []
        for n in range(3):
            tile = y[:, 128 * n : 128 * (n + 1)]
            swapped = pltpu.roll(tile, HEAD, 1)
            doubled += [jnp.where(lower, tile, swapped), jnp.where(lower, swapped, tile)]
        for h in range(3):
            for part, dest in ((doubled[h], r.q), (doubled[3 + h], r.k)):
                turned = part * cosine + pltpu.roll(part, 32, 1) * sine
                dest[h, at, :] = turned.astype(BF)
            r.kt[h, b] = turned.T.astype(BF)
        tile = y[:, 384:512]
        for h, value in enumerate((jnp.where(lower, tile, 0.0), jnp.where(lower, 0.0, tile))):
            r.v[h, at, :] = value.astype(BF)
            r.vt[h, b] = value.T.astype(BF)
        value = y[:, 512:576]
        r.v[2, at, :HEAD] = value.astype(BF)
        r.vt[2, b, :HEAD, :] = value.T.astype(BF)

    project(t)

    def ag_step(k, carry):
        for chunk in range(2):
            for side in range(2):
                step = 2 * side - 1
                b = t + step * k
                nxt = t - step

                @pl.when(inside(b))
                def _():
                    got(ag_chunk(b, chunk), S.ag_r + 2 * b + chunk)

                    @pl.when(inside(nxt))
                    def _():
                        ag_copy(b, chunk, side, k, nxt).start()

        @pl.when((k == t + 1) & (t < 2))
        def _():
            wr_copy(t, 0, 0, t + 1).start()

        @pl.when((k == 4 - t) & (t > 1))
        def _():
            wr_copy(t, 1, 0, t - 1).start()

        for side in range(2):
            b = t + (2 * side - 1) * k

            @pl.when(inside(b))
            def _():
                project(b)

        return carry

    lax.fori_loop(1, 4, ag_step, 0)

    @pl.when(t == 2)
    def _():
        wr_copy(t, 0, 0, t + 1).start()

    @pl.when(t == 1)
    def _():
        wr_copy(t, 1, 0, t - 1).start()


    ag_own_sent(1)

    def ag_sent(i, carry):
        k, side, b, nxt = hop(i)

        @pl.when(inside(b) & inside(nxt))
        def _():
            for chunk in range(2):
                sent(ag_chunk(b, 0), S.ag_s + (side * 4 + k) * 2 + chunk)

        return carry

    lax.fori_loop(1, 7, ag_sent, 0)

    def wx_copy(b, j):
        index = b * 3 + j - 1
        piece = wo_piece(b, q)
        return remote(piece, piece, S.wx_s + index, S.wx_r + index, column(j))

    def wc_copy(a, b):
        piece = r.wo.at[b, :, rows(c, HALF)] if a == 0 else r.w.at[:, b, c]
        return remote(piece, piece, S.wc_s + a * 4 + b, S.wc_r + a * 4 + b, sibling)

    for j in range(1, 4):
        b = zpeer(j)
        got(wz_piece(0, b), S.wz_r + b)
        for col in range(1, 4):
            wx_copy(b, col).start()

    neg = jnp.where(is_long > 0, 0.0, -1e30)

    def attend(i, carry):
        qb = lax.rem(t + 1 + i, 4)
        outs = []
        for h in range(3):
            queries = r.q[h, rows(qb, 256), :]
            parts = []
            for kb in range(4):
                s = dot_nt(r.k[h, kb * 256 : (kb + 1) * 256, :], queries) * (0.5 * SCALE)
                parts.append(s + jnp.where(qb == kb, 0.0, neg))
            top = parts[0].max(axis=0, keepdims=True)
            for kb in range(1, 4):
                top = jnp.maximum(top, parts[kb].max(axis=0, keepdims=True))
            parts = [jnp.exp(s - top) for s in parts]
            inverse = 1.0 / sum(total(s) for s in parts)
            out = None
            for kb in range(4):
                p = (parts[kb] * inverse).astype(BF)
                r.probs[h, qb, kb * 256 : (kb + 1) * 256, :] = p
                term = dot(r.vt[h, kb] if h < 2 else r.vt[h, kb, :HEAD, :], p)
                out = term if out is None else out + term
            outs.append(out)
        low, high = (outs[0] + outs[1]).T.astype(BF), outs[2].T.astype(BF)

        @pl.when(i < 3)
        def _():
            r.blocks[qb, :, :128] = low
            r.blocks[qb, :, 128:192] = high
            remote(r.blocks.at[qb], r.mixed.at[t], S.mix_s + i, S.mix_r + t, (dp, qb)).start()

        @pl.when(i == 3)
        def _():
            r.mixed[t, :, :128] = low
            r.mixed[t, :, 128:192] = high

        return carry

    lax.fori_loop(0, 4, attend, 0)
    for j in range(1, 4):
        got(r.bup.at[zpeer(j)], S.bup_r + zpeer(j))
    for s in range(4):
        options = [r.bup[s, :, 192 * n : 192 * (n + 1)] for n in range(4)]
        r.bupq[:, 192 * s : 192 * (s + 1)] = pick(q, options)

    for j in range(1, 4):
        b = zpeer(j)
        for col in range(1, 4):
            got(wo_piece(b, columns[col]), S.wx_r + b * 3 + col - 1)
        wc_copy(0, b).start()
    for j in range(1, 4):
        got(r.wo.at[zpeer(j), :, rows(other, HALF)], S.wc_r + zpeer(j))
    for j in range(1, 4):
        got(r.mixed.at[zpeer(j)], S.mix_r + zpeer(j))

    def wr_step(i, carry):
        k, side, b, nxt = hop(i)

        @pl.when(inside(b))
        def _():
            got(wz_piece(1, b), S.wz_r + 4 + b)

            @pl.when(inside(nxt))
            def _():
                wr_copy(b, side, k, nxt).start()

            wc_copy(1, b).start()

        return carry

    lax.fori_loop(1, 3, wr_step, 0)
    attended = jnp.broadcast_to(row(r.b_out), (256, D))
    for g in range(4):
        attended = attended + dot(r.mixed[g], r.wo[g])
    resid = r.toks[t].astype(F32) + attended
    r.resid[...] = resid
    unit2, rstd2 = norm_parts(resid)
    scale1 = 1.0 + r.modrow[:, :D]
    r.mod[q] = (unit2 * scale1 + r.modrow[:, D : 2 * D]).astype(BF)
    for j in range(1, 4):
        remote(r.mod.at[q], r.mod.at[q], S.md_s + j, S.md_r + q, column(j)).start()
    lax.fori_loop(3, 7, wr_step, 0)
    for j in range(1, 4):
        got(r.w.at[:, zpeer(j), other], S.wc_r + 4 + zpeer(j))

    def forward(n, carry):
        j = lax.rem(n + 1, 4)
        col = pick(j, columns)

        @pl.when(j > 0)
        def _():
            got(r.gb.at[col], S.gb_r + col)
            got(r.mod.at[col], S.md_r + col)

        w_up = r.w[0].reshape(D, D)
        hidden = dot_nt(r.mod[col], w_up) + r.bupq[...]
        inner = math.sqrt(2.0 / math.pi)
        square = hidden * hidden
        th = jnp.tanh(inner * hidden * (1.0 + 0.044715 * square))
        halfsum = 0.5 * (1.0 + th)
        r.act[col] = (hidden * halfsum).astype(BF)
        slope = halfsum + 0.5 * hidden * (1.0 - th * th) * (inner * (1.0 + 3 * 0.044715 * square))
        grad_active = dot_nt(r.gb[col], r.w[1].reshape(D, D))
        gh = (slope * grad_active).astype(BF)
        r.gh[col] = gh
        grad_mod = dot(gh, w_up)

        @pl.when(j == 0)
        def _():
            r.gres[...] = grad_mod

        @pl.when(j > 0)
        def _():
            r.gmp_out[j - 1] = grad_mod.astype(BF)
            device = (block + 2 * col + c, t)
            remote(r.gmp_out.at[j - 1], r.gmp_in.at[j - 1], S.gmp_s + j, S.gmp_r + j, device).start()

        return carry

    lax.fori_loop(0, 4, forward, 0)

    def r2_copy(a, j):
        col = columns[j]
        src = r.gwo.at[c, :, col] if a == 0 else r.gqkv.at[c, col]
        dst = (r.r2o, r.r2q)[a].at[j - 1]
        return remote(src, dst, S.r2_s + a * 3 + j - 1, S.r2_r + a * 3 + j - 1, column(j))

    def r3_piece(a, shard):
        return r.gwo.at[c, shard, q] if a == 0 else r.gw.at[a - 1, shard, c]

    def r3_copy(a, j):
        goal = zpeer(j)
        dst = r.r3o.at[t] if a == 0 else r.r3w.at[a - 1, t]
        return remote(
            r3_piece(a, goal), dst, S.r3_s + a * 4 + j, S.r3_r + a * 4 + t, (dp, goal)
        )

    def out_piece(a, col):
        if a == 0:
            return r.oo.at[rows(col, 48), rows(c, HALF)]
        if a < 3:
            return r.ow.at[a - 1, col, c]
        return r.oqkv.at[rows(col, 144), rows(c, HALF)]

    def r4_copy(a, j):
        piece = out_piece(a, q)
        index = a * 3 + j - 1
        return remote(piece, piece, S.r4_s + index, S.r4_r + index, column(j))

    def half_out(a, who):
        if a == 0:
            return r.oo.at[:, rows(who, HALF)]
        if a < 3:
            return r.ow.at[a - 1, :, who]
        return r.oqkv.at[:, rows(who, HALF)]

    def r5_copy(a):
        piece = half_out(a, c)
        return remote(piece, piece, S.r5_s + a, S.r5_r + a, sibling)

    def r1_copy_w(a):
        return remote(r.gw.at[a, :, other], r.r1w.at[a], S.r1_s + a, S.r1_r + a, sibling)

    def r1_sum_w(a):
        got(r.r1w.at[a], S.r1_r + a)
        r.gw[a, :, c] = (r.gw[a, :, c].astype(F32) + r.r1w[a].astype(F32)).astype(BF)

    def r3_start(a):
        for j in range(1, 4):
            r3_copy(a, j).start()

    def r1_sum_o():
        got(r.r1o, S.r1_r + 2)
        r.gwo[c] = (r.gwo[c].astype(F32) + r.r1o[...].astype(F32)).astype(BF)
        for j in range(1, 4):
            r2_copy(0, j).start()

    def r2_sum(a):
        for j in range(1, 4):
            copy = r2_copy(a, j)
            copy.wait_recv()
            copy.wait_send()
        mine_ref = r.gwo.at[c, :, q] if a == 0 else r.gqkv.at[c, q]
        theirs = (r.r2o, r.r2q)[a]
        acc = mine_ref[...].astype(F32)
        for j in range(3):
            acc = acc + theirs[j].astype(F32)
        if a == 0:
            mine_ref[...] = acc.astype(BF)
            r3_start(0)
        else:
            out_piece(3, q)[...] = acc.astype(BF)
            for j in range(1, 4):
                r4_copy(3, j).start()

    def r3_sum(a):
        buf = r.r3o if a == 0 else r.r3w.at[a - 1]
        acc = r3_piece(a, t)[...].astype(F32)
        for j in range(1, 4):
            got(buf.at[zpeer(j)], S.r3_r + a * 4 + zpeer(j))
            acc = acc + buf[zpeer(j)].astype(F32)
        out_piece(a, q)[...] = acc.astype(BF)
        for j in range(1, 4):
            r4_copy(a, j).start()

    def r4_wait(a):
        for j in range(1, 4):
            got(out_piece(a, columns[j]), S.r4_r + a * 3 + j - 1)
        r5_copy(a).start()

    def weight_grad(a):
        left = (r.gh, r.act)[a][...].reshape(1024, D)
        right = (r.mod, r.gb)[a][...].reshape(1024, D)
        for s in range(4):
            grad = dot_tn(left[:, 192 * s : 192 * (s + 1)], right)
            r.gw[a, s] = grad.astype(BF).reshape(2, 96, D)

    for a in (1, 0):
        weight_grad(a)
        r1_copy_w(a).start()
    r1_sum_w(1)
    r3_start(2)
    r1_sum_w(0)

    grad_mod = r.gres[...]
    for j in range(1, 4):
        got(r.gmp_in.at[j - 1], S.gmp_r + j)
        grad_mod = grad_mod + r.gmp_in[j - 1].astype(F32)
    unit2, rstd2 = norm_parts(r.resid[...])
    scale1 = 1.0 + r.modrow[:, :D]
    grad_resid = r.cot[...].astype(F32) + norm_back(unit2, rstd2, grad_mod * scale1)
    r.gres[...] = grad_resid
    grad_att = grad_resid.astype(BF)
    for i in range(3):
        sent(r.blocks.at[0], S.mix_s + i)
    for i in range(1, 4):
        g = lax.rem(t + i, 4)
        r.blocks[g] = dot_nt(grad_att, r.wo[g]).astype(BF)
        remote(r.blocks.at[g], r.gm.at[t], S.gm_s + i, S.gm_r + t, (dp, g)).start()
    r.gm[t] = dot_nt(grad_att, r.wo[t]).astype(BF)
    r.small[0:1, :] = total(grad_mod * unit2)
    r.small[1:2, :] = total(grad_mod)
    r.small[3:4, :] = jnp.zeros((1, D), F32)
    r.small[3:4, :TE] = r.feat[...]
    r.small[4:5, :] = total(grad_att.astype(F32))
    r.small[5:6, :] = total(r.gb[q].astype(F32))
    r.small[6:7, :] = total(r.gh[...].reshape(1024, D).astype(F32))
    r.small[7:8, :] = jnp.zeros((1, D), F32)
    for g in range(4):
        grad = dot_tn(r.mixed[g], grad_att).astype(BF)
        for half in range(2):
            r.gwo[half, g] = grad[:, HALF * half : HALF * (half + 1)].reshape(4, 48, HALF)
    remote(r.gwo.at[other], r.r1o, S.r1_s + 2, S.r1_r + 2, sibling).start()
    for j in range(1, 4):
        sent(r.gmp_out.at[j - 1], S.gmp_s + j)

    def down(n, carry):
        j = lax.rem(n + 1, 4)
        col = pick(j, columns)
        branch = dot(r.act[col], r.w[1].reshape(D, D))

        @pl.when(j == 0)
        def _():
            r.gtok[...] = branch

        @pl.when(j > 0)
        def _():
            r.gmp_out[j - 1] = branch.astype(BF)
            device = (block + 2 * col + c, t)
            remote(r.gmp_out.at[j - 1], r.br_in.at[j - 1], S.br_s + j, S.br_r + j, device).start()

        return carry

    lax.fori_loop(0, 4, down, 0)


    r1_sum_o()

    r.wide[...] = jnp.zeros((12, 512, 128), F32)

    def attend_back(i, carry):
        qb = lax.rem(t + i, 4)

        @pl.when(i > 0)
        def _():
            got(r.gm.at[qb], S.gm_r + qb)

        @pl.when(i == 2)
        def _():
            r3_start(1)

        at = rows(qb, 256)
        cosine, sine = rope_tables(qb)
        for h in range(3):
            width = 128 if h < 2 else HEAD
            grad_out = r.gm[qb, :, :128] if h < 2 else r.gm[qb, :, 128:192]
            queries = r.q[h, at, :]
            probs = []
            grads = []
            inner = None
            for kb in range(4):
                keys = slice(kb * 256, (kb + 1) * 256)
                p = r.probs[h, qb, keys, :]
                g = dot_nt(r.v[h, keys, :width], grad_out)
                term = total(g * p.astype(F32))
                inner = term if inner is None else inner + term
                probs.append(p)
                grads.append(g)
                place = slice(256 * (kb % 2), 256 * (kb % 2 + 1))
                r.wide[6 + 2 * h + kb // 2, place, :width] += dot(p, grad_out)
            grad_q = None
            for kb in range(4):
                ds = (probs[kb].astype(F32) * (grads[kb] - inner)).astype(BF)
                place = slice(256 * (kb % 2), 256 * (kb % 2 + 1))
                r.wide[2 * h + kb // 2, place, :] += dot(ds, queries)
                term = dot(r.kt[h, kb], ds)
                grad_q = term if grad_q is None else grad_q + term
            grad_q = grad_q.T * SCALE
            turned = grad_q * cosine - pltpu.roll(grad_q, 32, 1) * sine
            if h == 0:
                first_q = turned
            elif h == 1:
                r.gp[qb, :, :128] = jnp.where(lower, first_q, turned).astype(BF)
            else:
                r.gp[qb, :, 128:256] = turned.astype(BF)
        return carry

    lax.fori_loop(0, 4, attend_back, 0)
    r3_sum(2)

    def finish(n, carry):
        b = jnp.where(t < 2, 3 - n, n)
        cosine, sine = rope_tables(b)
        keys = []
        half = rows(lax.rem(b, 2), 256)
        place = lax.div(b, 2)
        for h in range(3):
            grad = r.wide[2 * h + place, half, :] * SCALE
            keys.append(grad * cosine - pltpu.roll(grad, 32, 1) * sine)
        values = [r.wide[6 + 2 * h + place, half, :] for h in range(3)]
        last_q = r.gp[b, :, 128:256].astype(F32)
        r.gp[b, :, 128:256] = jnp.where(lower, last_q, keys[0]).astype(BF)
        r.gp[b, :, 256:384] = jnp.where(lower, keys[1], keys[2]).astype(BF)
        r.gp[b, :, 384:512] = jnp.where(lower, values[0], values[1]).astype(BF)
        r.gp[b, :, 512:576] = values[2][:, :HEAD].astype(BF)
        return carry

    lax.fori_loop(0, 4, finish, 0)

    def rs_sent(k, side):
        for chunk in range(2):
            sent(r.act.at[0, 0:128], S.rs_s + (side * 3 + k - 1) * 2 + chunk)

    def rs_step(k):
        for side in range(2):
            step = 1 - 2 * side
            goal = t + step * (4 - k)
            nxt = t + step
            prev = t - step
            slot = 3 - k if side else k - 1

            @pl.when(inside(goal))
            def _():
                if k > 1:

                    @pl.when(jnp.logical_not(inside(prev)))
                    def _():
                        rs_sent(k - 1, side)

                for chunk in range(2):
                    at = slice(128 * chunk, 128 * (chunk + 1))
                    part = dot(r.gp[goal, at, :], r.w_qkv[...])
                    r.act[slot, at, :] = part.astype(BF)
                    if k > 1:

                        @pl.when(inside(prev))
                        def _():
                            index = (side * 3 + k - 2) * 2 + chunk
                            got(r.rs_in.at[side, k - 2, at], S.rs_r + index)
                            summed = part + r.rs_in[side, k - 2, at, :].astype(F32)
                            r.act[slot, at, :] = summed.astype(BF)

                    index = (side * 3 + k - 1) * 2 + chunk
                    remote(
                        r.act.at[slot, at],
                        r.rs_in.at[side, k - 1, at],
                        S.rs_s + index,
                        S.rs_r + index,
                        (dp, nxt),
                    ).start()

    rs_step(1)

    grad_w = dot_tn(r.gp[...].reshape(1024, 576), r.normed[...].reshape(1024, D)).astype(BF)
    for half in range(2):
        lanes = slice(HALF * half, HALF * (half + 1))
        r.gqkv[half] = grad_w[:, lanes].reshape(4, 144, HALF)
    remote(r.gqkv.at[other], r.r1q, S.r1_s + 3, S.r1_r + 3, sibling).start()
    r2_sum(0)

    branch = r.gtok[...] + row(r.b_down)
    for j in range(1, 4):
        got(r.br_in.at[j - 1], S.br_r + j)
        branch = branch + r.br_in[j - 1].astype(F32)
    r.result[...] = (r.resid[...] + r.modrow[:, 2 * D :] * branch).astype(BF)
    store("result")
    r.small[2:3, :] = total(r.cot[...].astype(F32) * branch)
    r.zs[t] = r.small[...]
    for j in range(1, 4):
        remote(r.small, r.zs.at[t], S.ez_s + j, S.ez_r + t, (dp, zpeer(j))).start()

    got(r.r1q, S.r1_r + 3)
    r.gqkv[c] = (r.gqkv[c].astype(F32) + r.r1q[...].astype(F32)).astype(BF)
    for j in range(1, 4):
        r2_copy(1, j).start()
    r3_sum(1)
    rs_step(2)

    def norm_sums(b, carry):
        unit, _ = norm_parts(r.toks[b].astype(F32))
        part = dot(r.gp[b], r.w_qkv[...])
        gain, bias = carry
        return gain + total(part * unit), bias + total(part)

    zero = jnp.zeros((1, D), F32)
    gain, bias = lax.fori_loop(0, 4, norm_sums, (zero, zero))
    r.late[...] = jnp.zeros((8, D), F32)
    r.late[0:1, :] = gain
    r.late[1:2, :] = bias
    r.late[2:3, :576] = total(r.gp[...].reshape(1024, 576).astype(F32))
    r.zl[t] = r.late[...]
    for j in range(1, 4):
        remote(r.late, r.zl.at[t], S.lz_s + j, S.lz_r + t, (dp, zpeer(j))).start()

    for j in range(1, 4):
        got(r.zs.at[zpeer(j)], S.ez_r + zpeer(j))
    for z in range(4):
        for n in range(4):
            r.ds[mine, 4 * n + z : 4 * n + z + 1, :] = r.zs[z, n : n + 1, :]
    r.ds[mine, 16:20, :] = r.zs[0, 4:8, :] + r.zs[1, 4:8, :] + r.zs[2, 4:8, :] + r.zs[3, 4:8, :]
    r.ds[mine, 20:24, :] = jnp.zeros((4, D), F32)
    for j in range(1, 8):
        peer = lax.rem(mine + j, 8)
        remote(
            r.ds.at[mine], r.ds.at[mine], S.ed_s + j, S.ed_r + mine, (block + peer, t)
        ).start()
    r4_wait(2)
    r2_sum(1)
    r3_sum(0)
    rs_step(3)
    for j in range(1, 4):
        got(r.zl.at[zpeer(j)], S.lz_r + zpeer(j))
    r.dl[mine] = r.zl[0] + r.zl[1] + r.zl[2] + r.zl[3]
    r.dl[mine, 2:3, :] = r.late[2:3, :]
    for j in range(1, 8):
        peer = lax.rem(mine + j, 8)
        remote(
            r.dl.at[mine], r.dl.at[mine], S.ld_s + j, S.ld_r + mine, (block + peer, t)
        ).start()
    own = dot(r.gp[t], r.w_qkv[...])
    for a in (1, 3, 0):
        r4_wait(a)

    for j in range(1, 8):
        peer = lax.rem(mine + j, 8)
        got(r.ds.at[peer], S.ed_r + peer)
    for peer in range(8):
        for n in range(4):
            r.gmat[n, 4 * peer : 4 * peer + 4, :] = r.ds[peer, 4 * n : 4 * n + 4, :]
    for n in range(3):
        r.gwt[:, D * n : D * (n + 1)] = dot_tn(r.gmat[3][:, :TE], r.gmat[n], HIGHEST)
        r.vec[4 + n : 5 + n, :] = total(r.gmat[n])
    r.vec[2:4, :] = sum(r.ds[peer, 16:18, :] for peer in range(8))
    for n in range(4):
        units = r.ds[2 * n, 18:19, :] + r.ds[2 * n + 1, 18:19, :]
        options = [units[:, 192 * s : 192 * (s + 1)] for s in range(4)]
        r.vec[7:8, 192 * n : 192 * (n + 1)] = pick(t, options)
    store("gwt")
    for j in range(1, 8):
        peer = lax.rem(mine + j, 8)
        got(r.dl.at[peer], S.ld_r + peer)
    last = sum(r.dl[peer, 0:3, :] for peer in range(8))
    r.vec[0:2, :] = last[0:2]
    r.vec[8:9, :] = last[2:3]
    store("vec")

    got(half_out(2, other), S.r5_r + 2)
    r.od[...] = r.ow[1].reshape(D, D)
    store("od")

    for side in range(2):
        prev = t - (1 - 2 * side)

        @pl.when(inside(prev))
        def _():
            for chunk in range(2):
                at = slice(128 * chunk, 128 * (chunk + 1))
                got(r.rs_in.at[side, 2, at], S.rs_r + (side * 3 + 2) * 2 + chunk)

        @pl.when((prev < 0) | (prev > 3))
        def _():
            r.rs_in[side, 2] = jnp.zeros((256, D), BF)

    grad_normed = own + r.rs_in[0, 2].astype(F32) + r.rs_in[1, 2].astype(F32)
    unit1, rstd1 = norm_parts(r.toks[t].astype(F32))
    r.gtok[...] = r.gres[...] + norm_back(unit1, rstd1, grad_normed * row(r.gain))
    store("gtok")

    for a in (3, 1, 0):
        got(half_out(a, other), S.r5_r + a)
    store("oqkv")
    store("oo")
    r.ou[...] = r.ow[0].reshape(D, D).T
    store("ou")

    for j in range(1, 4):
        sent(r.bup.at[t], S.bup_s + j)
        sent(r.small, S.ez_s + j)
        sent(r.late, S.lz_s + j)
        sent(r.blocks.at[0], S.gm_s + j)
        for base in (S.gb_s, S.md_s, S.br_s):
            sent(r.gb.at[0], base + j)
        for a in range(3):
            sent(r3_piece(a, t), S.r3_s + a * 4 + j)
        sent(wz_piece(0, t), S.wz_s + j)
        b = zpeer(j)
        sent(r.wo.at[b, :, rows(c, HALF)], S.wc_s + b)
        sent(wz_piece(1, b), S.wc_s + 4 + b)
        for col in range(1, 4):
            sent(wo_piece(b, q), S.wx_s + b * 3 + col - 1)
    for side in range(2):

        @pl.when(inside(t + 1 - 2 * side))
        def _():
            sent(wz_piece(1, t), S.wz_s + 4 + side * 4)

    def wr_sent(i, carry):
        k, side, b, nxt = hop(i)

        @pl.when(inside(b) & inside(nxt))
        def _():
            sent(wz_piece(1, b), S.wz_s + 4 + side * 4 + k)

        return carry

    lax.fori_loop(1, 7, wr_sent, 0)
    for a in range(2):
        sent(r.r1w.at[a], S.r1_s + a)
    sent(r.r1o, S.r1_s + 2)
    sent(r.r1q, S.r1_s + 3)
    for j in range(1, 8):
        sent(r.ds.at[mine], S.ed_s + j)
        sent(r.dl.at[mine], S.ld_s + j)
    for a in range(4):
        sent(half_out(a, c), S.r5_s + a)
        for j in range(1, 4):
            sent(out_piece(a, q), S.r4_s + a * 3 + j - 1)

    for k in range(1, 4):
        for side in range(2):
            step = 1 - 2 * side
            goal = t + step * (4 - k)

            @pl.when(inside(goal) & (inside(t - step) | (k == 3)))
            def _():
                rs_sent(k, side)

    for copy in stores:
        copy.wait()


def fused(scalars, blocks, far, outs):
    vmem = pl.BlockSpec(memory_space=pltpu.VMEM)
    smem = pl.BlockSpec(memory_space=pltpu.SMEM)
    anywhere = pl.BlockSpec(memory_space=pl.ANY)
    operands = scalars | blocks | far
    return pl.pallas_call(
        partial(body, [*operands, *outs, *SCRATCH]),
        out_shape=[jax.ShapeDtypeStruct(shape, kind) for shape, kind in outs.values()],
        in_specs=[smem] * len(scalars) + [vmem] * len(blocks) + [anywhere] * len(far),
        out_specs=[anywhere] * len(outs),
        scratch_shapes=[pltpu.VMEM(shape, kind) for shape, kind in SCRATCH.values()]
        + [pltpu.SemaphoreType.DMA((COUNT,))],
        compiler_params=pltpu.CompilerParams(
            collective_id=0, has_side_effects=True, vmem_limit_bytes=63 << 20
        ),
        name="layer",
    )(*operands.values())


def widen_body(result, gtok, oqkv, oo, ou, od, gwt, vec, *outs):
    for src, dst in zip((result, gtok, oqkv, gwt, oo, ou, od), outs[:7], strict=True):
        dst[...] = src[...].astype(dst.dtype)
    ggain, gbias, gbqkv, gbo, gbt, gbu, gbd = outs[7:]
    for n, dst in ((0, ggain), (1, gbias), (2, gbo), (3, gbd), (7, gbu)):
        dst[...] = vec[n : n + 1, :].reshape(D)
    for n in range(3):
        gbt[D * n : D * (n + 1)] = vec[4 + n : 5 + n, :].reshape(D)
        gbqkv[n : n + 1, :] = vec[8:9, 192 * n : 192 * (n + 1)]


def widen(parts):
    vmem = pl.BlockSpec(memory_space=pltpu.VMEM)
    outs = (
        ((256, D), BF),
        ((256, D), F32),
        ((576, D), F32),
        ((TE, 3 * D), F32),
        ((192, D), F32),
        ((D, D), F32),
        ((D, D), F32),
        ((D,), F32),
        ((D,), F32),
        ((3, 192), F32),
        ((D,), F32),
        ((3 * D,), F32),
        ((D,), F32),
        ((D,), F32),
    )
    return pl.pallas_call(
        widen_body,
        out_shape=[jax.ShapeDtypeStruct(shape, kind) for shape, kind in outs],
        in_specs=[vmem] * 8,
        out_specs=[vmem] * 14,
        compiler_params=pltpu.CompilerParams(vmem_limit_bytes=62 << 20),
        name="widen",
    )(*parts)


def on_device(
    tokens,
    long_count,
    timesteps,
    norm_gain,
    norm_bias,
    w_qkv,
    b_qkv,
    w_out,
    b_out,
    w_time,
    b_time,
    w_up,
    b_up,
    w_down,
    b_down,
    cotangent,
):
    n_dp = lax.axis_size("dp")
    assert tokens.shape == (SHORT, D) and lax.axis_size("tensor") * SHORT == LONG and n_dp % 8 == 0
    scalars = dict(lc=long_count, ts=timesteps)
    blocks = dict(
        gain=norm_gain,
        bias=norm_bias,
        b_out=b_out,
        b_down=b_down,
        b_time=b_time,
        bup_own=b_up,
        b_qkv=b_qkv,
    )
    far = dict(
        wo_own=w_out,
        wu_own=w_up.reshape(3, 256, D),
        wd_own=w_down.reshape(4, 2, 96, D),
        w_time_far=w_time,
        cot_far=cotangent,
        tok_far=tokens,
        w_qkv_far=jnp.transpose(w_qkv, (0, 2, 1)).reshape(576, D),
    )
    outs = dict(
        out_result=((256, D), BF),
        out_gtok=((256, D), F32),
        out_oqkv=((576, D), BF),
        out_oo=((192, D), BF),
        out_ou=((D, D), BF),
        out_od=((D, D), BF),
        out_gwt=((TE, 3 * D), F32),
        out_vec=((16, D), F32),
    )
    result, grad_tokens, gqkv, gwt, *rest = widen(fused(scalars, blocks, far, outs))
    gwo, gwu, gwd, ggain, gbias, gbqkv, gbo, gbt, gbu, gbd = rest
    grads = (
        ggain,
        gbias,
        jnp.transpose(gqkv.reshape(3, 192, D), (0, 2, 1)),
        gbqkv,
        gwo,
        gbo,
        gwt,
        gbt,
        gwu,
        gbu,
        gwd,
        gbd,
    )
    if n_dp > 8:
        groups = [[inner + 8 * outer for outer in range(n_dp // 8)] for inner in range(8)]
        grads = lax.psum(grads, "dp", axis_index_groups=groups)
    return (result, grad_tokens) + tuple(grads)


def solution(mesh):
    rows = P(("dp", "tensor"), None)
    placed = (
        rows,
        P("dp"),
        P("dp"),
        P(),
        P(),
        P(None, None, "tensor"),
        P(None, "tensor"),
        P("tensor", None),
        P(),
        P(),
        P(),
        P(None, "tensor"),
        P("tensor"),
        P("tensor", None),
        P(),
        rows,
    )
    return jax.shard_map(
        on_device,
        mesh=mesh,
        in_specs=placed,
        out_specs=(rows, rows) + placed[3:15],
        check_vma=False,
    )
```

```python
import math
from functools import partial
from itertools import accumulate
from types import SimpleNamespace

import jax
import jax.numpy as jnp
from jax import lax
from jax.experimental import pallas as pl
from jax.experimental.pallas import tpu as pltpu
from jax.sharding import PartitionSpec as P

HEAD = 64
TE = 128
STEPS = 1000
LONG = 1024
SHORT = 256
D = 768
HALF = 384
EPS = 1e-05
TIME_SCALE = 64.0
SCALE = 1.0 / math.sqrt(HEAD)
LOG_BASE = math.log(10000.0)
BF = jnp.bfloat16
F32 = jnp.float32
MESH = pl.DeviceIdType.MESH
HIGHEST = lax.Precision.HIGHEST

SEMS = dict(
    load=7,
    store=9,
    ag_s=16,
    ag_r=8,
    bup_s=4,
    bup_r=4,
    gb_s=4,
    gb_r=4,
    md_s=4,
    md_r=4,
    wz_s=12,
    wz_r=8,
    wx_s=12,
    wx_r=12,
    wc_s=8,
    wc_r=8,
    mix_s=4,
    mix_r=4,
    gmp_s=4,
    gmp_r=4,
    br_s=4,
    br_r=4,
    gm_s=4,
    gm_r=4,
    r1_s=4,
    r1_r=4,
    r2_s=6,
    r2_r=6,
    r3_s=12,
    r3_r=12,
    r4_s=12,
    r4_r=12,
    r5_s=4,
    r5_r=4,
    rs_s=12,
    rs_r=12,
    ez_s=4,
    ez_r=4,
    ed_s=8,
    ed_r=8,
    lz_s=4,
    lz_r=4,
    ld_s=8,
    ld_r=8,
)
COUNT = sum(SEMS.values())
S = SimpleNamespace(**dict(zip(SEMS, accumulate(SEMS.values(), initial=0))))

SCRATCH = dict(
    cot=((256, D), BF),
    w_qkv=((576, D), BF),
    w_time=((TE, 3 * D), F32),
    result=((256, D), BF),
    gtok=((256, D), F32),
    oqkv=((576, D), BF),
    oo=((192, D), BF),
    ou=((D, D), BF),
    od=((D, D), BF),
    gwt=((TE, 3 * D), F32),
    vec=((16, D), F32),
    turn=((2, 256, 128), F32),
    feat=((1, TE), F32),
    modrow=((1, 3 * D), F32),
    toks=((4, 256, D), BF),
    normed=((4, 256, D), BF),
    q=((3, 1024, 128), BF),
    k=((3, 1024, 128), BF),
    v=((3, 1024, 128), BF),
    kt=((3, 4, 128, 256), BF),
    vt=((3, 4, 128, 256), BF),
    probs=((3, 4, 1024, 256), BF),
    blocks=((4, 256, 192), BF),
    mixed=((4, 256, 192), BF),
    wo=((4, 192, D), BF),
    w=((2, 4, 2, 96, D), BF),
    bup=((4, 1, D), F32),
    bqkv=((1, 576), F32),
    bupq=((1, D), F32),
    mod=((4, 256, D), BF),
    gb=((4, 256, D), BF),
    act=((4, 256, D), BF),
    gh=((4, 256, D), BF),
    wide=((12, 512, 128), F32),
    gmp_out=((3, 256, D), BF),
    gmp_in=((3, 256, D), BF),
    br_in=((3, 256, D), BF),
    gwo=((2, 4, 4, 48, HALF), BF),
    gw=((2, 4, 2, 96, D), BF),
    resid=((256, D), F32),
    gres=((256, D), F32),
    gm=((4, 256, 192), BF),
    gp=((4, 256, 576), BF),
    gqkv=((2, 4, 144, HALF), BF),
    r1o=((4, 4, 48, HALF), BF),
    r1w=((2, 4, 96, D), BF),
    r1q=((4, 144, HALF), BF),
    r2o=((3, 4, 48, HALF), BF),
    r2q=((3, 144, HALF), BF),
    r3w=((2, 4, 96, D), BF),
    r3o=((4, 48, HALF), BF),
    ow=((2, 4, 2, 96, D), BF),
    rs_in=((2, 3, 256, D), BF),
    small=((8, D), F32),
    zs=((4, 8, D), F32),
    ds=((8, 24, D), F32),
    late=((8, D), F32),
    zl=((4, 8, D), F32),
    dl=((8, 8, D), F32),
    gmat=((4, 32, D), F32),
)


def dot(a, b):
    return jnp.dot(a, b, preferred_element_type=F32)


def dot_nt(a, b):
    return lax.dot_general(a, b, (((1,), (1,)), ((), ())), preferred_element_type=F32)


def dot_tn(a, b, precision=None):
    dims = (((0,), (0,)), ((), ()))
    return lax.dot_general(a, b, dims, precision=precision, preferred_element_type=F32)


def norm_parts(values):
    center = values - jnp.mean(values, axis=-1, keepdims=True)
    rstd = lax.rsqrt(jnp.mean(center * center, axis=-1, keepdims=True) + EPS)
    return center * rstd, rstd


def norm_back(unit, rstd, grad):
    mean_g = jnp.mean(grad, axis=-1, keepdims=True)
    mean_gn = jnp.mean(grad * unit, axis=-1, keepdims=True)
    return (grad - mean_g - unit * mean_gn) * rstd


def total(values):
    return jnp.sum(values, axis=0, keepdims=True)


def row(ref):
    return ref[...].reshape(1, -1)


def pick(index, options):
    chosen = options[-1]
    for n in range(len(options) - 2, -1, -1):
        chosen = jnp.where(index == n, options[n], chosen)
    return chosen


def body(names, *refs):
    sem = refs[-1]
    r = SimpleNamespace(**dict(zip(names, refs[:-1], strict=True)))
    dp = lax.axis_index("dp")
    t = lax.axis_index("tensor")
    mine = lax.rem(dp, 8)
    block = dp - mine
    c = lax.rem(dp, 2)
    q = lax.div(mine, 2)
    other = 1 - c
    sibling = (dp + 1 - 2 * c, t)
    columns = [q, q + 1 - 2 * lax.rem(q, 2), q + 2 - 4 * lax.div(q, 2), 3 - q]

    def column(j):
        return (block + 2 * columns[j] + c, t)

    def zpeer(j):
        return lax.rem(t + j, 4)

    def remote(src, dst, send, recv, device):
        return pltpu.make_async_remote_copy(
            src_ref=src,
            dst_ref=dst,
            send_sem=sem.at[send],
            recv_sem=sem.at[recv],
            device_id=device,
            device_id_type=MESH,
        )

    def got(ref, recv):
        remote(ref, ref, recv, recv, sibling).wait_recv()

    def sent(ref, send):
        remote(ref, ref, send, send, sibling).wait_send()

    def rows(index, size):
        return pl.ds(pl.multiple_of(index * size, size), size)

    def hop(i):
        k = lax.div(i + 1, 2)
        side = 1 - lax.rem(i, 2)
        step = 2 * side - 1
        return k, side, t + step * k, t - step

    def inside(b):
        return (b >= 0) & (b <= 3)

    barrier = pltpu.get_barrier_semaphore()
    for j in range(1, 4):
        pl.semaphore_signal(barrier, inc=1, device_id=(dp, zpeer(j)), device_id_type=MESH)
    for j in range(1, 8):
        peer = block + lax.rem(mine + j, 8)
        pl.semaphore_signal(barrier, inc=1, device_id=(peer, t), device_id_type=MESH)

    loads = [
        pltpu.make_async_copy(r.wo_own, r.wo.at[t], sem.at[S.load]),
        pltpu.make_async_copy(r.wu_own, r.act.at[0:3], sem.at[S.load + 1]),
        pltpu.make_async_copy(r.wd_own.at[q], r.w.at[1, t], sem.at[S.load + 2]),
        pltpu.make_async_copy(r.w_time_far, r.w_time, sem.at[S.load + 3]),
        pltpu.make_async_copy(r.cot_far, r.cot, sem.at[S.load + 4]),
        pltpu.make_async_copy(r.w_qkv_far, r.w_qkv, sem.at[S.load + 5]),
        pltpu.make_async_copy(r.tok_far, r.toks.at[t], sem.at[S.load + 6]),
    ]
    for load in reversed(loads):
        load.start()
    names_out = [name for name in names if name.startswith("out_")]

    def store(name):
        n = names_out.index("out_" + name)
        copy = pltpu.make_async_copy(getattr(r, name), getattr(r, "out_" + name), sem.at[S.store + n])
        copy.start()
        stores.append(copy)

    stores = []

    r.bup[t] = row(r.bup_own)
    for n in range(3):
        r.bqkv[:, 192 * n : 192 * (n + 1)] = r.b_qkv[n : n + 1, :]
    loads[6].wait()
    pl.semaphore_wait(barrier, 10)

    def ag_chunk(b, chunk):
        return r.toks.at[b, 128 * chunk : 128 * (chunk + 1)]

    def ag_copy(b, chunk, side, k, device):
        piece = ag_chunk(b, chunk)
        send = S.ag_s + (side * 4 + k) * 2 + chunk
        return remote(piece, piece, send, S.ag_r + 2 * b + chunk, (dp, device))

    def ag_own(chunk):
        @pl.when(t < 3)
        def _():
            ag_copy(t, chunk, 0, 0, t + 1).start()

        @pl.when(t > 0)
        def _():
            ag_copy(t, chunk, 1, 0, t - 1).start()

    def ag_own_sent(chunk):
        @pl.when(t < 3)
        def _():
            sent(ag_chunk(t, 0), S.ag_s + chunk)

        @pl.when(t > 0)
        def _():
            sent(ag_chunk(t, 0), S.ag_s + 8 + chunk)

    ag_own(0)
    def wo_piece(shard, col):
        return r.wo.at[shard, rows(col, 48), rows(c, HALF)]

    def wz_piece(a, shard):
        return wo_piece(shard, q) if a == 0 else r.w.at[:, shard, c]

    def wz_copy(a, j):
        piece = wz_piece(a, t)
        return remote(piece, piece, S.wz_s + a * 4 + j, S.wz_r + a * 4 + t, (dp, zpeer(j)))

    def wr_copy(b, side, k, device):
        piece = wz_piece(1, b)
        send = S.wz_s + 4 + side * 4 + k
        return remote(piece, piece, send, S.wz_r + 4 + b, (dp, device))

    loads[0].wait()
    for j in range(1, 4):
        wz_copy(0, j).start()
    for j in range(1, 4):
        remote(r.bup.at[t], r.bup.at[t], S.bup_s + j, S.bup_r + t, (dp, zpeer(j))).start()

    is_long = r.lc[0]
    slot = (1 - is_long) * t
    step = jnp.int32(0)
    for n in range(4):
        step = step + jnp.where(slot == n, r.ts[n], 0)
    lane = lax.broadcasted_iota(jnp.int32, (1, TE), 1)
    half_lane = lax.rem(lane, TE // 2).astype(F32)
    angle = (step.astype(F32) / STEPS * TIME_SCALE) * jnp.exp(half_lane * (-LOG_BASE / (TE // 2)))
    feat = jnp.where(lane < TE // 2, jnp.cos(angle), jnp.sin(angle))
    r.feat[...] = feat
    wide_feat = jnp.broadcast_to(feat, (8, TE))
    loads[3].wait()
    loads[4].wait()
    modulation = jnp.dot(wide_feat, r.w_time[...], precision=HIGHEST, preferred_element_type=F32)
    r.modrow[...] = modulation[0:1] + row(r.b_time)
    gate = r.modrow[:, 2 * D :]
    r.gb[q] = (gate * r.cot[...].astype(F32)).astype(BF)
    for j in range(1, 4):
        remote(r.gb.at[q], r.gb.at[q], S.gb_s + j, S.gb_r + q, column(j)).start()

    ag_own_sent(0)
    ag_own(1)

    lane = lax.broadcasted_iota(jnp.int32, (1, 128), 1)
    freqs = jnp.exp(lax.rem(lane, 32).astype(F32) * (-LOG_BASE / 32))
    sign = jnp.where(lax.rem(lane, 64) < 32, -1.0, 1.0)
    angles = lax.broadcasted_iota(jnp.int32, (256, 128), 0).astype(F32) * freqs
    r.turn[0] = jnp.cos(angles)
    r.turn[1] = jnp.sin(angles) * sign

    def rope_tables(b):
        offset = (b * 256 * is_long).astype(F32) * freqs
        cosine = jnp.cos(offset)
        sine = jnp.sin(offset) * sign
        return (
            r.turn[0] * cosine - r.turn[1] * sine,
            r.turn[1] * cosine + r.turn[0] * sine,
        )

    loads[1].wait()
    loads[2].wait()
    loads[5].wait()
    for n in range(4):

        @pl.when(q == n)
        def _():
            part = r.act[0:3].reshape(D, D)[:, 192 * n : 192 * (n + 1)]
            r.w[0, t] = part.T.reshape(2, 96, D)

    lower = lax.broadcasted_iota(jnp.int32, (256, 128), 1) < HEAD

    def project(b):
        unit, _ = norm_parts(r.toks[b].astype(F32))
        r.normed[b] = (unit * row(r.gain) + row(r.bias)).astype(BF)
        y = dot_nt(r.normed[b], r.w_qkv[...]) + r.bqkv[...]
        at = rows(b, 256)
        cosine, sine = rope_tables(b)
        doubled = []
        for n in range(3):
            tile = y[:, 128 * n : 128 * (n + 1)]
            swapped = pltpu.roll(tile, HEAD, 1)
            doubled += [jnp.where(lower, tile, swapped), jnp.where(lower, swapped, tile)]
        for h in range(3):
            for part, dest in ((doubled[h], r.q), (doubled[3 + h], r.k)):
                turned = part * cosine + pltpu.roll(part, 32, 1) * sine
                dest[h, at, :] = turned.astype(BF)
            r.kt[h, b] = turned.T.astype(BF)
        tile = y[:, 384:512]
        for h, value in enumerate((jnp.where(lower, tile, 0.0), jnp.where(lower, 0.0, tile))):
            r.v[h, at, :] = value.astype(BF)
            r.vt[h, b] = value.T.astype(BF)
        value = y[:, 512:576]
        r.v[2, at, :HEAD] = value.astype(BF)
        r.vt[2, b, :HEAD, :] = value.T.astype(BF)

    project(t)

    def ag_step(k, carry):
        for chunk in range(2):
            for side in range(2):
                step = 2 * side - 1
                b = t + step * k
                nxt = t - step

                @pl.when(inside(b))
                def _():
                    got(ag_chunk(b, chunk), S.ag_r + 2 * b + chunk)

                    @pl.when(inside(nxt))
                    def _():
                        ag_copy(b, chunk, side, k, nxt).start()

        @pl.when((k == t + 1) & (t < 2))
        def _():
            wr_copy(t, 0, 0, t + 1).start()

        @pl.when((k == 4 - t) & (t > 1))
        def _():
            wr_copy(t, 1, 0, t - 1).start()

        for side in range(2):
            b = t + (2 * side - 1) * k

            @pl.when(inside(b))
            def _():
                project(b)

        return carry

    lax.fori_loop(1, 4, ag_step, 0)

    @pl.when(t == 2)
    def _():
        wr_copy(t, 0, 0, t + 1).start()

    @pl.when(t == 1)
    def _():
        wr_copy(t, 1, 0, t - 1).start()


    def wx_copy(b, j):
        index = b * 3 + j - 1
        piece = wo_piece(b, q)
        return remote(piece, piece, S.wx_s + index, S.wx_r + index, column(j))

    def wc_copy(a, b):
        piece = r.wo.at[b, :, rows(c, HALF)] if a == 0 else r.w.at[:, b, c]
        return remote(piece, piece, S.wc_s + a * 4 + b, S.wc_r + a * 4 + b, sibling)

    for j in range(1, 4):
        b = zpeer(j)
        got(wz_piece(0, b), S.wz_r + b)
        for col in range(1, 4):
            wx_copy(b, col).start()

    neg = jnp.where(is_long > 0, 0.0, -1e30)

    def attend(i, carry):
        qb = lax.rem(t + 1 + i, 4)
        outs = []
        for h in range(3):
            queries = r.q[h, rows(qb, 256), :]
            parts = []
            for kb in range(4):
                s = dot_nt(r.k[h, kb * 256 : (kb + 1) * 256, :], queries) * (0.5 * SCALE)
                parts.append(s + jnp.where(qb == kb, 0.0, neg))
            top = parts[0].max(axis=0, keepdims=True)
            for kb in range(1, 4):
                top = jnp.maximum(top, parts[kb].max(axis=0, keepdims=True))
            parts = [jnp.exp(s - top) for s in parts]
            inverse = 1.0 / sum(total(s) for s in parts)
            out = None
            for kb in range(4):
                p = (parts[kb] * inverse).astype(BF)
                r.probs[h, qb, kb * 256 : (kb + 1) * 256, :] = p
                term = dot(r.vt[h, kb] if h < 2 else r.vt[h, kb, :HEAD, :], p)
                out = term if out is None else out + term
            outs.append(out)
        low, high = (outs[0] + outs[1]).T.astype(BF), outs[2].T.astype(BF)

        @pl.when(i < 3)
        def _():
            r.blocks[qb, :, :128] = low
            r.blocks[qb, :, 128:192] = high
            remote(r.blocks.at[qb], r.mixed.at[t], S.mix_s + i, S.mix_r + t, (dp, qb)).start()

        @pl.when(i == 3)
        def _():
            r.mixed[t, :, :128] = low
            r.mixed[t, :, 128:192] = high

        return carry

    lax.fori_loop(0, 4, attend, 0)
    for j in range(1, 4):
        got(r.bup.at[zpeer(j)], S.bup_r + zpeer(j))
    for s in range(4):
        options = [r.bup[s, :, 192 * n : 192 * (n + 1)] for n in range(4)]
        r.bupq[:, 192 * s : 192 * (s + 1)] = pick(q, options)

    for j in range(1, 4):
        b = zpeer(j)
        for col in range(1, 4):
            got(wo_piece(b, columns[col]), S.wx_r + b * 3 + col - 1)
        wc_copy(0, b).start()
    for j in range(1, 4):
        got(r.wo.at[zpeer(j), :, rows(other, HALF)], S.wc_r + zpeer(j))
    for j in range(1, 4):
        got(r.mixed.at[zpeer(j)], S.mix_r + zpeer(j))

    def wr_step(i, carry):
        k, side, b, nxt = hop(i)

        @pl.when(inside(b))
        def _():
            got(wz_piece(1, b), S.wz_r + 4 + b)

            @pl.when(inside(nxt))
            def _():
                wr_copy(b, side, k, nxt).start()

            wc_copy(1, b).start()

        return carry

    lax.fori_loop(1, 3, wr_step, 0)
    attended = jnp.broadcast_to(row(r.b_out), (256, D))
    for g in range(4):
        attended = attended + dot(r.mixed[g], r.wo[g])
    resid = r.toks[t].astype(F32) + attended
    r.resid[...] = resid
    unit2, rstd2 = norm_parts(resid)
    scale1 = 1.0 + r.modrow[:, :D]
    r.mod[q] = (unit2 * scale1 + r.modrow[:, D : 2 * D]).astype(BF)
    for j in range(1, 4):
        remote(r.mod.at[q], r.mod.at[q], S.md_s + j, S.md_r + q, column(j)).start()
    lax.fori_loop(3, 7, wr_step, 0)
    for j in range(1, 4):
        got(r.w.at[:, zpeer(j), other], S.wc_r + 4 + zpeer(j))

    def forward(n, carry):
        j = lax.rem(n + 1, 4)
        col = pick(j, columns)

        @pl.when(j > 0)
        def _():
            got(r.gb.at[col], S.gb_r + col)
            got(r.mod.at[col], S.md_r + col)

        w_up = r.w[0].reshape(D, D)
        hidden = dot_nt(r.mod[col], w_up) + r.bupq[...]
        inner = math.sqrt(2.0 / math.pi)
        square = hidden * hidden
        th = jnp.tanh(inner * hidden * (1.0 + 0.044715 * square))
        halfsum = 0.5 * (1.0 + th)
        r.act[col] = (hidden * halfsum).astype(BF)
        slope = halfsum + 0.5 * hidden * (1.0 - th * th) * (inner * (1.0 + 3 * 0.044715 * square))
        grad_active = dot_nt(r.gb[col], r.w[1].reshape(D, D))
        gh = (slope * grad_active).astype(BF)
        r.gh[col] = gh
        grad_mod = dot(gh, w_up)

        @pl.when(j == 0)
        def _():
            r.gres[...] = grad_mod

        @pl.when(j > 0)
        def _():
            r.gmp_out[j - 1] = grad_mod.astype(BF)
            device = (block + 2 * col + c, t)
            remote(r.gmp_out.at[j - 1], r.gmp_in.at[j - 1], S.gmp_s + j, S.gmp_r + j, device).start()

        return carry

    lax.fori_loop(0, 4, forward, 0)

    def r2_copy(a, j):
        col = columns[j]
        src = r.gwo.at[c, :, col] if a == 0 else r.gqkv.at[c, col]
        dst = (r.r2o, r.r2q)[a].at[j - 1]
        return remote(src, dst, S.r2_s + a * 3 + j - 1, S.r2_r + a * 3 + j - 1, column(j))

    def r3_piece(a, shard):
        return r.gwo.at[c, shard, q] if a == 0 else r.gw.at[a - 1, shard, c]

    def r3_copy(a, j):
        goal = zpeer(j)
        dst = r.r3o.at[t] if a == 0 else r.r3w.at[a - 1, t]
        return remote(
            r3_piece(a, goal), dst, S.r3_s + a * 4 + j, S.r3_r + a * 4 + t, (dp, goal)
        )

    def out_piece(a, col):
        if a == 0:
            return r.oo.at[rows(col, 48), rows(c, HALF)]
        if a < 3:
            return r.ow.at[a - 1, col, c]
        return r.oqkv.at[rows(col, 144), rows(c, HALF)]

    def r4_copy(a, j):
        piece = out_piece(a, q)
        index = a * 3 + j - 1
        return remote(piece, piece, S.r4_s + index, S.r4_r + index, column(j))

    def half_out(a, who):
        if a == 0:
            return r.oo.at[:, rows(who, HALF)]
        if a < 3:
            return r.ow.at[a - 1, :, who]
        return r.oqkv.at[:, rows(who, HALF)]

    def r5_copy(a):
        piece = half_out(a, c)
        return remote(piece, piece, S.r5_s + a, S.r5_r + a, sibling)

    def r1_copy_w(a):
        return remote(r.gw.at[a, :, other], r.r1w.at[a], S.r1_s + a, S.r1_r + a, sibling)

    def r1_sum_w(a):
        got(r.r1w.at[a], S.r1_r + a)
        r.gw[a, :, c] = (r.gw[a, :, c].astype(F32) + r.r1w[a].astype(F32)).astype(BF)

    def r3_start(a):
        for j in range(1, 4):
            r3_copy(a, j).start()

    def r1_sum_o():
        got(r.r1o, S.r1_r + 2)
        r.gwo[c] = (r.gwo[c].astype(F32) + r.r1o[...].astype(F32)).astype(BF)
        for j in range(1, 4):
            r2_copy(0, j).start()

    def r2_sum(a):
        for j in range(1, 4):
            copy = r2_copy(a, j)
            copy.wait_recv()
            copy.wait_send()
        mine_ref = r.gwo.at[c, :, q] if a == 0 else r.gqkv.at[c, q]
        theirs = (r.r2o, r.r2q)[a]
        acc = mine_ref[...].astype(F32)
        for j in range(3):
            acc = acc + theirs[j].astype(F32)
        if a == 0:
            mine_ref[...] = acc.astype(BF)
            r3_start(0)
        else:
            out_piece(3, q)[...] = acc.astype(BF)
            for j in range(1, 4):
                r4_copy(3, j).start()

    def r3_sum(a):
        buf = r.r3o if a == 0 else r.r3w.at[a - 1]
        acc = r3_piece(a, t)[...].astype(F32)
        for j in range(1, 4):
            got(buf.at[zpeer(j)], S.r3_r + a * 4 + zpeer(j))
            acc = acc + buf[zpeer(j)].astype(F32)
        out_piece(a, q)[...] = acc.astype(BF)
        for j in range(1, 4):
            r4_copy(a, j).start()

    def r4_wait(a):
        for j in range(1, 4):
            got(out_piece(a, columns[j]), S.r4_r + a * 3 + j - 1)
        r5_copy(a).start()

    def weight_grad(a):
        left = (r.gh, r.act)[a][...].reshape(1024, D)
        right = (r.mod, r.gb)[a][...].reshape(1024, D)
        for s in range(4):
            grad = dot_tn(left[:, 192 * s : 192 * (s + 1)], right)
            r.gw[a, s] = grad.astype(BF).reshape(2, 96, D)

    for a in (1, 0):
        weight_grad(a)
        r1_copy_w(a).start()
    r1_sum_w(1)
    r3_start(2)
    r1_sum_w(0)

    grad_mod = r.gres[...]
    for j in range(1, 4):
        got(r.gmp_in.at[j - 1], S.gmp_r + j)
        grad_mod = grad_mod + r.gmp_in[j - 1].astype(F32)
    unit2, rstd2 = norm_parts(r.resid[...])
    scale1 = 1.0 + r.modrow[:, :D]
    grad_resid = r.cot[...].astype(F32) + norm_back(unit2, rstd2, grad_mod * scale1)
    r.gres[...] = grad_resid
    grad_att = grad_resid.astype(BF)
    for i in range(3):
        sent(r.blocks.at[0], S.mix_s + i)
    for i in range(1, 4):
        g = lax.rem(t + i, 4)
        r.blocks[g] = dot_nt(grad_att, r.wo[g]).astype(BF)
        remote(r.blocks.at[g], r.gm.at[t], S.gm_s + i, S.gm_r + t, (dp, g)).start()
    r.gm[t] = dot_nt(grad_att, r.wo[t]).astype(BF)
    r.small[0:1, :] = total(grad_mod * unit2)
    r.small[1:2, :] = total(grad_mod)
    r.small[3:4, :] = jnp.zeros((1, D), F32)
    r.small[3:4, :TE] = r.feat[...]
    r.small[4:5, :] = total(grad_att.astype(F32))
    r.small[5:6, :] = total(r.gb[q].astype(F32))
    r.small[6:7, :] = total(r.gh[...].reshape(1024, D).astype(F32))
    r.small[7:8, :] = jnp.zeros((1, D), F32)
    for g in range(4):
        grad = dot_tn(r.mixed[g], grad_att).astype(BF)
        for half in range(2):
            r.gwo[half, g] = grad[:, HALF * half : HALF * (half + 1)].reshape(4, 48, HALF)
    remote(r.gwo.at[other], r.r1o, S.r1_s + 2, S.r1_r + 2, sibling).start()
    for j in range(1, 4):
        sent(r.gmp_out.at[j - 1], S.gmp_s + j)

    def down(n, carry):
        j = lax.rem(n + 1, 4)
        col = pick(j, columns)
        branch = dot(r.act[col], r.w[1].reshape(D, D))

        @pl.when(j == 0)
        def _():
            r.gtok[...] = branch

        @pl.when(j > 0)
        def _():
            r.gmp_out[j - 1] = branch.astype(BF)
            device = (block + 2 * col + c, t)
            remote(r.gmp_out.at[j - 1], r.br_in.at[j - 1], S.br_s + j, S.br_r + j, device).start()

        return carry

    lax.fori_loop(0, 4, down, 0)


    r1_sum_o()

    r.wide[...] = jnp.zeros((12, 512, 128), F32)

    def attend_back(i, carry):
        qb = lax.rem(t + i, 4)

        @pl.when(i > 0)
        def _():
            got(r.gm.at[qb], S.gm_r + qb)

        @pl.when(i == 2)
        def _():
            r3_start(1)

        at = rows(qb, 256)
        cosine, sine = rope_tables(qb)
        for h in range(3):
            width = 128 if h < 2 else HEAD
            grad_out = r.gm[qb, :, :128] if h < 2 else r.gm[qb, :, 128:192]
            queries = r.q[h, at, :]
            probs = []
            grads = []
            inner = None
            for kb in range(4):
                keys = slice(kb * 256, (kb + 1) * 256)
                p = r.probs[h, qb, keys, :]
                g = dot_nt(r.v[h, keys, :width], grad_out)
                term = total(g * p.astype(F32))
                inner = term if inner is None else inner + term
                probs.append(p)
                grads.append(g)
                place = slice(256 * (kb % 2), 256 * (kb % 2 + 1))
                r.wide[6 + 2 * h + kb // 2, place, :width] += dot(p, grad_out)
            grad_q = None
            for kb in range(4):
                ds = (probs[kb].astype(F32) * (grads[kb] - inner)).astype(BF)
                place = slice(256 * (kb % 2), 256 * (kb % 2 + 1))
                r.wide[2 * h + kb // 2, place, :] += dot(ds, queries)
                term = dot(r.kt[h, kb], ds)
                grad_q = term if grad_q is None else grad_q + term
            grad_q = grad_q.T * SCALE
            turned = grad_q * cosine - pltpu.roll(grad_q, 32, 1) * sine
            if h == 0:
                first_q = turned
            elif h == 1:
                r.gp[qb, :, :128] = jnp.where(lower, first_q, turned).astype(BF)
            else:
                r.gp[qb, :, 128:256] = turned.astype(BF)
        return carry

    lax.fori_loop(0, 4, attend_back, 0)
    r3_sum(2)

    def finish(n, carry):
        b = jnp.where(t < 2, 3 - n, n)
        cosine, sine = rope_tables(b)
        keys = []
        half = rows(lax.rem(b, 2), 256)
        place = lax.div(b, 2)
        for h in range(3):
            grad = r.wide[2 * h + place, half, :] * SCALE
            keys.append(grad * cosine - pltpu.roll(grad, 32, 1) * sine)
        values = [r.wide[6 + 2 * h + place, half, :] for h in range(3)]
        last_q = r.gp[b, :, 128:256].astype(F32)
        r.gp[b, :, 128:256] = jnp.where(lower, last_q, keys[0]).astype(BF)
        r.gp[b, :, 256:384] = jnp.where(lower, keys[1], keys[2]).astype(BF)
        r.gp[b, :, 384:512] = jnp.where(lower, values[0], values[1]).astype(BF)
        r.gp[b, :, 512:576] = values[2][:, :HEAD].astype(BF)
        return carry

    lax.fori_loop(0, 4, finish, 0)

    def rs_sent(k, side):
        for chunk in range(2):
            sent(r.act.at[0, 0:128], S.rs_s + (side * 3 + k - 1) * 2 + chunk)

    def rs_step(k):
        for side in range(2):
            step = 1 - 2 * side
            goal = t + step * (4 - k)
            nxt = t + step
            prev = t - step
            slot = 3 - k if side else k - 1

            @pl.when(inside(goal))
            def _():
                if k > 1:

                    @pl.when(jnp.logical_not(inside(prev)))
                    def _():
                        rs_sent(k - 1, side)

                for chunk in range(2):
                    at = slice(128 * chunk, 128 * (chunk + 1))
                    part = dot(r.gp[goal, at, :], r.w_qkv[...])
                    r.act[slot, at, :] = part.astype(BF)
                    if k > 1:

                        @pl.when(inside(prev))
                        def _():
                            index = (side * 3 + k - 2) * 2 + chunk
                            got(r.rs_in.at[side, k - 2, at], S.rs_r + index)
                            summed = part + r.rs_in[side, k - 2, at, :].astype(F32)
                            r.act[slot, at, :] = summed.astype(BF)

                    index = (side * 3 + k - 1) * 2 + chunk
                    remote(
                        r.act.at[slot, at],
                        r.rs_in.at[side, k - 1, at],
                        S.rs_s + index,
                        S.rs_r + index,
                        (dp, nxt),
                    ).start()

    rs_step(1)

    grad_w = dot_tn(r.gp[...].reshape(1024, 576), r.normed[...].reshape(1024, D)).astype(BF)
    for half in range(2):
        lanes = slice(HALF * half, HALF * (half + 1))
        r.gqkv[half] = grad_w[:, lanes].reshape(4, 144, HALF)
    remote(r.gqkv.at[other], r.r1q, S.r1_s + 3, S.r1_r + 3, sibling).start()
    r2_sum(0)

    branch = r.gtok[...] + row(r.b_down)
    for j in range(1, 4):
        got(r.br_in.at[j - 1], S.br_r + j)
        branch = branch + r.br_in[j - 1].astype(F32)
    r.result[...] = (r.resid[...] + r.modrow[:, 2 * D :] * branch).astype(BF)
    store("result")
    r.small[2:3, :] = total(r.cot[...].astype(F32) * branch)
    r.zs[t] = r.small[...]
    for j in range(1, 4):
        remote(r.small, r.zs.at[t], S.ez_s + j, S.ez_r + t, (dp, zpeer(j))).start()

    got(r.r1q, S.r1_r + 3)
    r.gqkv[c] = (r.gqkv[c].astype(F32) + r.r1q[...].astype(F32)).astype(BF)
    for j in range(1, 4):
        r2_copy(1, j).start()
    r3_sum(1)
    rs_step(2)

    def norm_sums(b, carry):
        unit, _ = norm_parts(r.toks[b].astype(F32))
        part = dot(r.gp[b], r.w_qkv[...])
        gain, bias = carry
        return gain + total(part * unit), bias + total(part)

    zero = jnp.zeros((1, D), F32)
    gain, bias = lax.fori_loop(0, 4, norm_sums, (zero, zero))
    r.late[...] = jnp.zeros((8, D), F32)
    r.late[0:1, :] = gain
    r.late[1:2, :] = bias
    r.late[2:3, :576] = total(r.gp[...].reshape(1024, 576).astype(F32))
    r.zl[t] = r.late[...]
    for j in range(1, 4):
        remote(r.late, r.zl.at[t], S.lz_s + j, S.lz_r + t, (dp, zpeer(j))).start()

    for j in range(1, 4):
        got(r.zs.at[zpeer(j)], S.ez_r + zpeer(j))
    for z in range(4):
        for n in range(4):
            r.ds[mine, 4 * n + z : 4 * n + z + 1, :] = r.zs[z, n : n + 1, :]
    r.ds[mine, 16:20, :] = r.zs[0, 4:8, :] + r.zs[1, 4:8, :] + r.zs[2, 4:8, :] + r.zs[3, 4:8, :]
    r.ds[mine, 20:24, :] = jnp.zeros((4, D), F32)
    for j in range(1, 8):
        peer = lax.rem(mine + j, 8)
        remote(
            r.ds.at[mine], r.ds.at[mine], S.ed_s + j, S.ed_r + mine, (block + peer, t)
        ).start()
    r4_wait(2)
    r2_sum(1)
    r3_sum(0)
    rs_step(3)
    for j in range(1, 4):
        got(r.zl.at[zpeer(j)], S.lz_r + zpeer(j))
    r.dl[mine] = r.zl[0] + r.zl[1] + r.zl[2] + r.zl[3]
    r.dl[mine, 2:3, :] = r.late[2:3, :]
    for j in range(1, 8):
        peer = lax.rem(mine + j, 8)
        remote(
            r.dl.at[mine], r.dl.at[mine], S.ld_s + j, S.ld_r + mine, (block + peer, t)
        ).start()
    own = dot(r.gp[t], r.w_qkv[...])
    for a in (1, 3, 0):
        r4_wait(a)

    for j in range(1, 8):
        peer = lax.rem(mine + j, 8)
        got(r.ds.at[peer], S.ed_r + peer)
    for peer in range(8):
        for n in range(4):
            r.gmat[n, 4 * peer : 4 * peer + 4, :] = r.ds[peer, 4 * n : 4 * n + 4, :]
    for n in range(3):
        r.gwt[:, D * n : D * (n + 1)] = dot_tn(r.gmat[3][:, :TE], r.gmat[n], HIGHEST)
        r.vec[4 + n : 5 + n, :] = total(r.gmat[n])
    r.vec[2:4, :] = sum(r.ds[peer, 16:18, :] for peer in range(8))
    for n in range(4):
        units = r.ds[2 * n, 18:19, :] + r.ds[2 * n + 1, 18:19, :]
        options = [units[:, 192 * s : 192 * (s + 1)] for s in range(4)]
        r.vec[7:8, 192 * n : 192 * (n + 1)] = pick(t, options)
    store("gwt")
    for j in range(1, 8):
        peer = lax.rem(mine + j, 8)
        got(r.dl.at[peer], S.ld_r + peer)
    last = sum(r.dl[peer, 0:3, :] for peer in range(8))
    r.vec[0:2, :] = last[0:2]
    r.vec[8:9, :] = last[2:3]
    store("vec")

    got(half_out(2, other), S.r5_r + 2)
    r.od[...] = r.ow[1].reshape(D, D)
    store("od")

    for side in range(2):
        prev = t - (1 - 2 * side)

        @pl.when(inside(prev))
        def _():
            for chunk in range(2):
                at = slice(128 * chunk, 128 * (chunk + 1))
                got(r.rs_in.at[side, 2, at], S.rs_r + (side * 3 + 2) * 2 + chunk)

        @pl.when((prev < 0) | (prev > 3))
        def _():
            r.rs_in[side, 2] = jnp.zeros((256, D), BF)

    grad_normed = own + r.rs_in[0, 2].astype(F32) + r.rs_in[1, 2].astype(F32)
    unit1, rstd1 = norm_parts(r.toks[t].astype(F32))
    r.gtok[...] = r.gres[...] + norm_back(unit1, rstd1, grad_normed * row(r.gain))
    store("gtok")

    for a in (3, 1, 0):
        got(half_out(a, other), S.r5_r + a)
    store("oqkv")
    store("oo")
    r.ou[...] = r.ow[0].reshape(D, D).T
    store("ou")

    for j in range(1, 4):
        sent(r.bup.at[t], S.bup_s + j)
        sent(r.small, S.ez_s + j)
        sent(r.late, S.lz_s + j)
        sent(r.blocks.at[0], S.gm_s + j)
        for base in (S.gb_s, S.md_s, S.br_s):
            sent(r.gb.at[0], base + j)
        for a in range(3):
            sent(r3_piece(a, t), S.r3_s + a * 4 + j)
        sent(wz_piece(0, t), S.wz_s + j)
        b = zpeer(j)
        sent(r.wo.at[b, :, rows(c, HALF)], S.wc_s + b)
        sent(wz_piece(1, b), S.wc_s + 4 + b)
        for col in range(1, 4):
            sent(wo_piece(b, q), S.wx_s + b * 3 + col - 1)
    for side in range(2):

        @pl.when(inside(t + 1 - 2 * side))
        def _():
            sent(wz_piece(1, t), S.wz_s + 4 + side * 4)

    def wr_sent(i, carry):
        k, side, b, nxt = hop(i)

        @pl.when(inside(b) & inside(nxt))
        def _():
            sent(wz_piece(1, b), S.wz_s + 4 + side * 4 + k)

        return carry

    lax.fori_loop(1, 7, wr_sent, 0)
    for a in range(2):
        sent(r.r1w.at[a], S.r1_s + a)
    sent(r.r1o, S.r1_s + 2)
    sent(r.r1q, S.r1_s + 3)
    for j in range(1, 8):
        sent(r.ds.at[mine], S.ed_s + j)
        sent(r.dl.at[mine], S.ld_s + j)
    for a in range(4):
        sent(half_out(a, c), S.r5_s + a)
        for j in range(1, 4):
            sent(out_piece(a, q), S.r4_s + a * 3 + j - 1)

    for k in range(1, 4):
        for side in range(2):
            step = 1 - 2 * side
            goal = t + step * (4 - k)

            @pl.when(inside(goal) & (inside(t - step) | (k == 3)))
            def _():
                rs_sent(k, side)

    ag_own_sent(1)

    def ag_sent(i, carry):
        k, side, b, nxt = hop(i)

        @pl.when(inside(b) & inside(nxt))
        def _():
            for chunk in range(2):
                sent(ag_chunk(b, 0), S.ag_s + (side * 4 + k) * 2 + chunk)

        return carry

    lax.fori_loop(1, 7, ag_sent, 0)
    for copy in stores:
        copy.wait()


def fused(scalars, blocks, far, outs):
    vmem = pl.BlockSpec(memory_space=pltpu.VMEM)
    smem = pl.BlockSpec(memory_space=pltpu.SMEM)
    anywhere = pl.BlockSpec(memory_space=pl.ANY)
    operands = scalars | blocks | far
    return pl.pallas_call(
        partial(body, [*operands, *outs, *SCRATCH]),
        out_shape=[jax.ShapeDtypeStruct(shape, kind) for shape, kind in outs.values()],
        in_specs=[smem] * len(scalars) + [vmem] * len(blocks) + [anywhere] * len(far),
        out_specs=[anywhere] * len(outs),
        scratch_shapes=[pltpu.VMEM(shape, kind) for shape, kind in SCRATCH.values()]
        + [pltpu.SemaphoreType.DMA((COUNT,))],
        compiler_params=pltpu.CompilerParams(
            collective_id=0, has_side_effects=True, vmem_limit_bytes=63 << 20
        ),
        name="layer",
    )(*operands.values())


def widen_body(result, gtok, oqkv, oo, ou, od, gwt, vec, *outs):
    for src, dst in zip((result, gtok, oqkv, gwt, oo, ou, od), outs[:7], strict=True):
        dst[...] = src[...].astype(dst.dtype)
    ggain, gbias, gbqkv, gbo, gbt, gbu, gbd = outs[7:]
    for n, dst in ((0, ggain), (1, gbias), (2, gbo), (3, gbd), (7, gbu)):
        dst[...] = vec[n : n + 1, :].reshape(D)
    for n in range(3):
        gbt[D * n : D * (n + 1)] = vec[4 + n : 5 + n, :].reshape(D)
        gbqkv[n : n + 1, :] = vec[8:9, 192 * n : 192 * (n + 1)]


def widen(parts):
    vmem = pl.BlockSpec(memory_space=pltpu.VMEM)
    outs = (
        ((256, D), BF),
        ((256, D), F32),
        ((576, D), F32),
        ((TE, 3 * D), F32),
        ((192, D), F32),
        ((D, D), F32),
        ((D, D), F32),
        ((D,), F32),
        ((D,), F32),
        ((3, 192), F32),
        ((D,), F32),
        ((3 * D,), F32),
        ((D,), F32),
        ((D,), F32),
    )
    return pl.pallas_call(
        widen_body,
        out_shape=[jax.ShapeDtypeStruct(shape, kind) for shape, kind in outs],
        in_specs=[vmem] * 8,
        out_specs=[vmem] * 14,
        compiler_params=pltpu.CompilerParams(vmem_limit_bytes=62 << 20),
        name="widen",
    )(*parts)


def on_device(
    tokens,
    long_count,
    timesteps,
    norm_gain,
    norm_bias,
    w_qkv,
    b_qkv,
    w_out,
    b_out,
    w_time,
    b_time,
    w_up,
    b_up,
    w_down,
    b_down,
    cotangent,
):
    n_dp = lax.axis_size("dp")
    assert tokens.shape == (SHORT, D) and lax.axis_size("tensor") * SHORT == LONG and n_dp % 8 == 0
    scalars = dict(lc=long_count, ts=timesteps)
    blocks = dict(
        gain=norm_gain,
        bias=norm_bias,
        b_out=b_out,
        b_down=b_down,
        b_time=b_time,
        bup_own=b_up,
        b_qkv=b_qkv,
    )
    far = dict(
        wo_own=w_out,
        wu_own=w_up.reshape(3, 256, D),
        wd_own=w_down.reshape(4, 2, 96, D),
        w_time_far=w_time,
        cot_far=cotangent,
        tok_far=tokens,
        w_qkv_far=jnp.transpose(w_qkv, (0, 2, 1)).reshape(576, D),
    )
    outs = dict(
        out_result=((256, D), BF),
        out_gtok=((256, D), F32),
        out_oqkv=((576, D), BF),
        out_oo=((192, D), BF),
        out_ou=((D, D), BF),
        out_od=((D, D), BF),
        out_gwt=((TE, 3 * D), F32),
        out_vec=((16, D), F32),
    )
    result, grad_tokens, gqkv, gwt, *rest = widen(fused(scalars, blocks, far, outs))
    gwo, gwu, gwd, ggain, gbias, gbqkv, gbo, gbt, gbu, gbd = rest
    grads = (
        ggain,
        gbias,
        jnp.transpose(gqkv.reshape(3, 192, D), (0, 2, 1)),
        gbqkv,
        gwo,
        gbo,
        gwt,
        gbt,
        gwu,
        gbu,
        gwd,
        gbd,
    )
    if n_dp > 8:
        groups = [[inner + 8 * outer for outer in range(n_dp // 8)] for inner in range(8)]
        grads = lax.psum(grads, "dp", axis_index_groups=groups)
    return (result, grad_tokens) + tuple(grads)


def solution(mesh):
    rows = P(("dp", "tensor"), None)
    placed = (
        rows,
        P("dp"),
        P("dp"),
        P(),
        P(),
        P(None, None, "tensor"),
        P(None, "tensor"),
        P("tensor", None),
        P(),
        P(),
        P(),
        P(None, "tensor"),
        P("tensor"),
        P("tensor", None),
        P(),
        rows,
    )
    return jax.shard_map(
        on_device,
        mesh=mesh,
        in_specs=placed,
        out_specs=(rows, rows) + placed[3:15],
        check_vma=False,
    )
```
